32 devices in a mesh: seq: 8 (over y, x, core), fsdp: 4 (over z).
Axes of the slice: x: 2, y: 2, z: 4, core: 2. Of those that a mesh axis runs over, the one named last changes fastest.
Arguments:
- block_in: bfloat16 [4096, 1536], P(('seq', 'fsdp')), may hold values from -6 to 6
- norm_gain: float32 [1536], replicated, may hold values from 0.5 to 1.5
- in_weight: bfloat16 [1536, 6448], P('fsdp'), may hold values from -0.15625 to 0.15625
- conv_inner_weight: float32 [4, 48, 64], P(None, 'seq', 'fsdp'), may hold values from -3 to 3
- conv_inner_bias: float32 [48, 64], P('seq', 'fsdp'), may hold values from -3 to 3
- conv_pair_weight: float32 [4, 256], replicated, may hold values from -3 to 3
- conv_pair_bias: float32 [256], replicated, may hold values from -3 to 3
- step_bias: float32 [48], P('seq'), may hold values from -6 to -1
- decay_log: float32 [48], P('seq'), may hold values from 0 to 2.77
- skip_gain: float32 [48], P('seq'), may hold values from 0.5 to 1.5
- gate_gain: float32 [48, 64], P('seq', 'fsdp'), may hold values from 0.5 to 1.5
- out_weight: bfloat16 [3072, 1536], P(None, 'fsdp'), may hold values from -0.109375 to 0.109375
- cotangent: bfloat16 [4096, 1536], P(('seq', 'fsdp')), may hold values from -6 to 6
Outputs:
- block_out: bfloat16 [4096, 1536], P(('seq', 'fsdp'))
- grad_input: bfloat16 [4096, 1536], P(('seq', 'fsdp'))
- grad_norm_gain: float32 [1536], replicated
- grad_in_weight: float32 [1536, 6448], P('fsdp')
- grad_conv_inner_weight: float32 [4, 48, 64], P(None, 'seq', 'fsdp')
- grad_conv_inner_bias: float32 [48, 64], P('seq', 'fsdp')
- grad_conv_pair_weight: float32 [4, 256], replicated
- grad_conv_pair_bias: float32 [256], replicated
- grad_step_bias: float32 [48], P('seq')
- grad_decay_log: float32 [48], P('seq')
- grad_skip_gain: float32 [48], P('seq')
- grad_gate_gain: float32 [48, 64], P('seq', 'fsdp')
- grad_out_weight: float32 [3072, 1536], P(None, 'fsdp')
The draws below stay inside these ranges and needn't reach their ends.
All inputs are finite; a program needn't handle non-finite values.
Results may differ from the reference program's by a relative error of at most 0.015.
The reference program's roundings to bfloat16 on the way count: a program that leaves them out, or rounds other values in their place, can miss the bound.
Values may be sent and summed in bfloat16 or wider, within the bound.
No kernel may reach another device: no remote copies, remote signals or barrier semaphores. Data moves between devices by JAX's collectives and lax.ppermute only.
A program may use at most 384 MiB of HBM per device.

```python
import jax
import jax.numpy as jnp
from jax import lax

D = 1536
H = 48
P_SIZE = 64
N = 128
KW = 4
Q = 256
DI = 3072
E = 6448
L = 4096


def shard_levels(key, shape, shards, least, high):
    factor_of = 1.0
    for dim, blocks in shards:
        heights = jax.random.uniform(jax.random.fold_in(jax.random.fold_in(key, 6), dim), (blocks,), jnp.float32, least / len(shards), high / len(shards))
        factor_of = factor_of * jnp.repeat(jnp.exp(heights), shape[dim] // blocks).reshape((-1,) + (1,) * (len(shape) - 1 - dim))
    return factor_of


def gaussian(own_key, shape, width, bound, shards=(), kind=jnp.bfloat16):
    entries = jax.random.normal(own_key, shape, jnp.float32) * width
    if len(shards) > 0:
        entries = shard_levels(own_key, shape, shards, -0.22, 0.18) * entries
    return jnp.clip(entries, min=-bound, max=bound).astype(kind)


def setup_inputs(seed: int = 0) -> dict:
    streams_of = jax.random.split(jax.random.key(seed), 14)
    block_in = gaussian(streams_of[0], (L, D), 1.0, 6.0, ((0, 32),))
    norm_gain = jnp.clip(1.0 + 0.1 * jax.random.normal(streams_of[1], (D,), jnp.float32), 0.5, 1.5)
    in_weight = gaussian(streams_of[2], (D, E), D ** -0.5, 0.15625, ((0, 4),))
    conv_inner_weight = gaussian(streams_of[3], (KW, H, P_SIZE), KW ** -0.5, 3.0, ((1, 8), (2, 4)), jnp.float32)
    conv_inner_bias = gaussian(streams_of[4], (H, P_SIZE), 0.5, 3.0, ((0, 8), (1, 4)), jnp.float32)
    conv_pair_weight = gaussian(streams_of[5], (KW, 2 * N), KW ** -0.5, 3.0, (), jnp.float32)
    conv_pair_bias = gaussian(streams_of[6], (2 * N,), 0.5, 3.0, (), jnp.float32)
    step_bias = jnp.clip(-6.0 + 5.0 * jax.random.uniform(streams_of[7], (H,), jnp.float32) ** shard_levels(streams_of[7], (H,), ((0, 8),), -0.2, 0.2), -6.0, -1.0)
    decay_log = jnp.clip(2.77 * jax.random.uniform(streams_of[8], (H,), jnp.float32) ** shard_levels(streams_of[8], (H,), ((0, 8),), -0.2, 0.2), 0.0, 2.77)
    skip_gain = jnp.clip(0.5 + 1.0 * jax.random.uniform(streams_of[9], (H,), jnp.float32) ** shard_levels(streams_of[9], (H,), ((0, 8),), -0.2, 0.2), 0.5, 1.5)
    gate_gain = jnp.clip(1.0 + 0.1 * jax.random.normal(streams_of[10], (H, P_SIZE), jnp.float32), 0.5, 1.5)
    out_weight = gaussian(streams_of[11], (DI, D), DI ** -0.5, 0.109375, ((1, 4),))
    cotangent = gaussian(streams_of[12], (L, D), 1.0, 6.0, ((0, 32),))
    return {"block_in": block_in, "norm_gain": norm_gain, "in_weight": in_weight, "conv_inner_weight": conv_inner_weight, "conv_inner_bias": conv_inner_bias, "conv_pair_weight": conv_pair_weight, "conv_pair_bias": conv_pair_bias, "step_bias": step_bias, "decay_log": decay_log, "skip_gain": skip_gain, "gate_gain": gate_gain, "out_weight": out_weight, "cotangent": cotangent}


norm_epsilon = 1e-05
far_below = -1e+30
highest = lax.Precision.HIGHEST

@jax.custom_vjp
def low(v):
    return lax.optimization_barrier(v.astype(jnp.bfloat16)).astype(jnp.float32)

@jax.custom_vjp
def low_back(v):
    return v

def low_keep(v):
    return (low(v), None)

def low_pass(kept, grad):
    return (grad,)

def back_keep(v):
    return (v, None)

def back_low(kept, grad):
    return (low(grad),)
low.defvjp(low_keep, low_pass)
low_back.defvjp(back_keep, back_low)

def causal_conv(values, weight, shift_bias):
    padded = jnp.pad(values, ((KW - 1, 0), (0, 0)))
    summed = shift_bias[None, :] + jnp.zeros_like(values)
    for offset in range(KW):
        summed = summed + weight[offset][None, :] * padded[offset:offset + values.shape[0]]
    return jax.nn.silu(summed)

def block_step(carry_state, inputs):
    inner_piece, b_piece, c_piece, rate_piece, step_piece = inputs
    cumulative = jnp.cumsum(rate_piece, axis=0)
    causal_mask = jnp.arange(Q)[:, None] >= jnp.arange(Q)[None, :]
    spread = cumulative[:, None, :] - cumulative[None, :, :]
    decay_mask = jnp.exp(jnp.where(causal_mask[:, :, None], spread, far_below))
    scores = jnp.dot(c_piece, b_piece.T, precision=highest)
    mixing = scores[:, :, None] * decay_mask * step_piece[None, :, :]
    output = jnp.einsum('ijh,jhp->ihp', mixing, inner_piece, precision=highest)
    carried = jnp.einsum('in,hnp->ihp', c_piece, carry_state, precision=highest)
    output = output + carried * jnp.exp(cumulative)[:, :, None]
    tail_weight = jnp.exp(cumulative[-1][None, :] - cumulative) * step_piece
    fresh_state = jnp.einsum('jn,jhp->hnp', b_piece, inner_piece * tail_weight[:, :, None], precision=highest)
    carry_state = jnp.exp(cumulative[-1])[:, None, None] * carry_state + fresh_state
    return (carry_state, output)

def state_scan(inner_heads, b_conv, c_conv, log_decay, step_size):
    blocks = L // Q
    inputs = (inner_heads.reshape(blocks, Q, H, P_SIZE), b_conv.reshape(blocks, Q, N), c_conv.reshape(blocks, Q, N), log_decay.reshape(blocks, Q, H), step_size.reshape(blocks, Q, H))
    initial = jnp.zeros((H, N, P_SIZE), jnp.float32)
    last_state, outputs = lax.scan(jax.checkpoint(block_step), initial, inputs)
    return outputs.reshape(L, H, P_SIZE)

def forward(block_in, norm_gain, in_weight, conv_inner_weight, conv_inner_bias, conv_pair_weight, conv_pair_bias, step_bias, decay_log, skip_gain, gate_gain, out_weight):
    inverse_scale = lax.rsqrt(lax.optimization_barrier(jnp.mean(block_in * block_in, axis=1, keepdims=True)) + norm_epsilon)
    normed = low(block_in * inverse_scale * norm_gain[None, :])
    projected = jnp.dot(normed, in_weight, precision=highest)
    gate_raw = low_back(low(projected[:, :DI]))
    inner_raw = low_back(low(projected[:, DI:2 * DI]))
    pair_raw = low_back(low(projected[:, 2 * DI:2 * DI + 2 * N]))
    step_raw = low_back(low(projected[:, 2 * DI + 2 * N:]))
    inner_conv = low(causal_conv(inner_raw, conv_inner_weight.reshape(KW, DI), conv_inner_bias.reshape(DI)))
    pair_conv = low(causal_conv(pair_raw, conv_pair_weight, conv_pair_bias))
    step_size = jax.nn.softplus(step_raw + step_bias[None, :])
    log_decay = step_size * (-jnp.exp(decay_log))[None, :]
    inner_heads = inner_conv.reshape(L, H, P_SIZE)
    mixer_out = state_scan(inner_heads, pair_conv[:, :N], pair_conv[:, N:], log_decay, step_size)
    mixer_out = mixer_out + skip_gain[None, :, None] * inner_heads
    gated_out = mixer_out.reshape(L, DI) * jax.nn.silu(gate_raw)
    gate_scale = lax.rsqrt(lax.optimization_barrier(jnp.mean(gated_out * gated_out, axis=1, keepdims=True)) + norm_epsilon)
    gated_normed = low_back(low(gated_out * gate_scale * gate_gain.reshape(DI)[None, :]))
    return block_in + jnp.dot(gated_normed, out_weight, precision=highest)

def reference(block_in, norm_gain, in_weight, conv_inner_weight, conv_inner_bias, conv_pair_weight, conv_pair_bias, step_bias, decay_log, skip_gain, gate_gain, out_weight, cotangent):
    primals = [value.astype(jnp.float32) for value in (block_in, norm_gain, in_weight, conv_inner_weight, conv_inner_bias, conv_pair_weight, conv_pair_bias, step_bias, decay_log, skip_gain, gate_gain, out_weight)]
    result, pullback = jax.vjp(forward, *primals)
    gradients = pullback(cotangent.astype(jnp.float32))
    return (result.astype(jnp.bfloat16), gradients[0].astype(jnp.bfloat16), gradients[1], gradients[2], gradients[3], gradients[4], gradients[5], gradients[6], gradients[7], gradients[8], gradients[9], gradients[10], gradients[11])
```

```python
import jax
import jax.numpy as jnp
from jax import lax
from jax.sharding import PartitionSpec as P

H = 48
P_SIZE = 64
N = 128
KW = 4
Q = 256

norm_epsilon = 1e-05
far_below = -1e30
highest = lax.Precision.HIGHEST
f32 = jnp.float32
bf16 = jnp.bfloat16
everyone = ("seq", "fsdp")


def spread(value, axis, count, groups=None):
    copies = jnp.broadcast_to(value[None], (count,) + value.shape)
    return lax.all_to_all(copies, axis, 0, 0, axis_index_groups=groups, tiled=True)


def dot_f32(left, right, dims, batch=((), ())):
    return lax.dot_general(left, right, (dims, batch), preferred_element_type=f32)


def body(
    block_in,
    norm_gain,
    in_weight,
    conv_inner_weight,
    conv_inner_bias,
    conv_pair_weight,
    conv_pair_bias,
    step_bias,
    decay_log,
    skip_gain,
    gate_gain,
    out_weight,
    cotangent,
):
    S = lax.axis_size("seq")
    F = lax.axis_size("fsdp")
    devices = S * F
    R = S // F
    s = lax.axis_index("seq")
    f = lax.axis_index("fsdp")
    q = s // R
    c = s % R
    member = c * F + f
    tokens, D = block_in.shape
    TL = tokens * S
    blocks = TL // Q
    HG = H // S
    GW = HG * P_SIZE
    QW = GW // F
    DI = H * P_SIZE
    Dl = in_weight.shape[0]
    PF = P_SIZE // F
    PQ = 2 * N // F
    parts = [[cc + R * qq for qq in range(F)] for cc in range(R)]
    twins = [(i, i ^ 1) for i in range(S)]
    forth = [(i, i + R) for i in range(S - R)]
    back = [(i + R, i) for i in range(S - R)]

    def twin(value):
        return lax.ppermute(value, "seq", twins)

    def pair_up(value):
        other = twin(value)
        return jnp.where(
            c == 0, jnp.stack([value, other]), jnp.stack([other, value])
        )

    def gather_group(value):
        line = spread(value, "fsdp", F)
        return pair_up(line).reshape((S * value.shape[0],) + value.shape[1:])

    def scatter_group(value):
        halves = value.reshape(R, F * tokens, value.shape[1])
        away = jnp.where(c == 0, halves[1], halves[0])
        mine = jnp.where(c == 0, halves[0], halves[1])
        total = mine.astype(f32) + twin(away.astype(bf16)).astype(f32)
        sent = total.astype(bf16).reshape(F, tokens, value.shape[1])
        got = lax.all_to_all(sent, "fsdp", 0, 0, tiled=True)
        return jnp.sum(got.astype(f32), axis=0)

    small = jnp.concatenate(
        [
            conv_inner_weight.reshape(KW, HG * PF),
            conv_inner_bias.reshape(1, HG * PF),
            gate_gain.reshape(1, HG * PF),
        ],
        axis=0,
    )
    small = jnp.pad(small, ((0, 0), (0, 128 - HG * PF)))
    heads_row = jnp.concatenate([step_bias, decay_log, skip_gain])
    heads_row = jnp.pad(heads_row, (0, 128 - 3 * HG))[None]
    small = jnp.concatenate([small, heads_row, jnp.zeros((1, 128), f32)], axis=0)
    small_all = spread(small, everyone, devices)
    small_here = lax.dynamic_slice(small_all, (member * F, 0, 0), (F, 8, 128))
    chan = small_here[:, : KW + 2, : HG * PF].reshape(F, KW + 2, HG, PF)
    chan = jnp.transpose(chan, (1, 2, 0, 3)).reshape(KW + 2, GW)
    heads_here = small_here[0, KW + 2]
    bias_h = heads_here[:HG]
    rate_h = jnp.exp(heads_here[HG : 2 * HG])
    skip_h = heads_here[2 * HG : 3 * HG]
    gain_row = chan[KW + 1]
    conv_w = jnp.concatenate([chan[:KW], conv_pair_weight], axis=1)
    conv_b = jnp.concatenate([chan[KW], conv_pair_bias])

    def head_rows(columns):
        half = lax.dynamic_slice(columns, (0, c * (DI // R)), (Dl, DI // R))
        rows = jnp.transpose(half).reshape(F, F, QW, Dl)
        return lax.dynamic_slice(rows, (0, q, 0, 0), (F, 1, QW, Dl)).reshape(F, QW, Dl)

    pair_rows = jnp.transpose(in_weight[:, 2 * DI : 2 * DI + 2 * N]).reshape(F, PQ, Dl)
    pair_rows = lax.dynamic_slice(pair_rows, (q, 0, 0), (1, PQ, Dl))
    pair_rows = jnp.broadcast_to(pair_rows, (F, PQ, Dl))
    step_rows = jnp.transpose(in_weight[:, 2 * DI + 2 * N :]).reshape(R, F, HG, Dl)
    step_rows = lax.dynamic_slice(step_rows, (c, 0, 0, 0), (1, F, HG, Dl)).reshape(F, HG, Dl)
    step_rows = jnp.pad(step_rows, ((0, 0), (0, 8 - HG), (0, 0)))
    sent = jnp.concatenate(
        [
            head_rows(in_weight[:, :DI]),
            head_rows(in_weight[:, DI : 2 * DI]),
            pair_rows,
            step_rows,
        ],
        axis=1,
    )
    got = lax.all_to_all(sent, "fsdp", 0, 0, tiled=True)
    rows = jnp.transpose(got, (1, 0, 2)).reshape(2 * QW + PQ + 8, D)
    rows = spread(rows, "seq", F, parts)
    in_rows = jnp.concatenate(
        [
            rows[:, :QW].reshape(GW, D),
            rows[:, QW : 2 * QW].reshape(GW, D),
            rows[0, 2 * QW + PQ :],
        ],
        axis=0,
    )
    pair_in = rows[:, 2 * QW : 2 * QW + PQ].reshape(2 * N, D)

    out_sent = lax.dynamic_slice(
        out_weight.reshape(R, F, F, QW, Dl), (c, 0, q, 0, 0), (1, F, 1, QW, Dl)
    ).reshape(F, QW, Dl)
    out_got = lax.all_to_all(out_sent, "fsdp", 0, 0, tiled=True)
    out_rows = jnp.transpose(out_got, (1, 0, 2)).reshape(QW, D)
    out_rows = spread(out_rows, "seq", F, parts).reshape(GW, D)

    hidden = block_in.astype(f32)
    inverse_scale = lax.rsqrt(jnp.mean(hidden * hidden, axis=1, keepdims=True) + norm_epsilon)
    normed = (hidden * inverse_scale * norm_gain[None, :]).astype(bf16)
    x_group = gather_group(normed)
    cot_group = gather_group(cotangent)

    proj = dot_f32(x_group, in_rows, ((1,), (1,))).astype(bf16)
    pair_raw = dot_f32(x_group, pair_in, ((1,), (1,))).astype(bf16)
    gate = proj[:, :GW].astype(f32)
    raw = jnp.concatenate([proj[:, GW : 2 * GW], pair_raw], axis=1)
    halo = lax.ppermute(raw[TL - (KW - 1) :], "seq", forth)
    step_raw = proj[:, 2 * GW : 2 * GW + HG].astype(f32)

    raw_ext = jnp.concatenate([halo, raw], axis=0).astype(f32)
    pre = conv_b[None] + sum(
        conv_w[k][None] * raw_ext[k : k + TL] for k in range(KW)
    )
    sig_pre = jax.nn.sigmoid(pre)
    act = lax.optimization_barrier((pre * sig_pre).astype(bf16))
    act_slope = sig_pre * (1.0 + pre * (1.0 - sig_pre))
    xs = act[:, :GW].reshape(blocks, Q, HG, P_SIZE)
    bs = act[:, GW : GW + N].reshape(blocks, Q, N)
    cs = act[:, GW + N :].reshape(blocks, Q, N)

    step_in = step_raw + bias_h[None]
    step = jax.nn.softplus(step_in)
    log_decay = step * (-rate_h)[None]
    causal = lax.broadcasted_iota(jnp.int32, (Q, Q), 0) >= lax.broadcasted_iota(
        jnp.int32, (Q, Q), 1
    )
    lower = causal.astype(f32)
    ld = log_decay.reshape(blocks, Q, HG)
    dt = step.reshape(blocks, Q, HG)
    cum = jnp.einsum("ij,bjh->bih", lower, ld, precision=highest)
    total = cum[:, -1]
    tail = jnp.exp(total[:, None] - cum)
    head = jnp.exp(cum)
    xf = xs.astype(f32)
    u32 = xf * dt[..., None]
    u = lax.optimization_barrier(u32.astype(bf16))
    uw = (u32 * tail[..., None]).astype(bf16)
    scores = jnp.einsum("bin,bjn->bij", cs, bs, preferred_element_type=f32)
    cum_t = jnp.transpose(cum, (0, 2, 1))
    decay = jnp.exp(
        jnp.where(causal[None, None], cum_t[:, :, :, None] - cum_t[:, :, None, :], far_below)
    )
    mix = lax.optimization_barrier((scores[:, None] * decay).astype(bf16))

    def wide(per_head):
        return jnp.repeat(per_head, P_SIZE, axis=-1)

    fresh = jnp.einsum(
        "bjn,bjw->bnw", bs, uw.reshape(blocks, Q, GW), preferred_element_type=f32
    )
    local = [jnp.zeros((N, GW), f32)]
    for b in range(blocks):
        local.append(local[b] * wide(jnp.exp(total[b]))[None] + fresh[b])
    whole_total = jnp.sum(total, axis=0)
    packed = jnp.concatenate(
        [local[blocks], jnp.broadcast_to(wide(whole_total)[None], (8, GW))], axis=0
    )
    packed = spread(packed, "seq", F, parts)
    totals = packed[:, N, :]
    part_no = jnp.arange(F)
    before = jnp.zeros((N, GW), f32)
    for p in range(F):
        between = jnp.sum(jnp.where(((part_no > p) & (part_no < q))[:, None], totals, 0.0), axis=0)
        before = before + jnp.where(p < q, jnp.exp(between)[None] * packed[p, :N], 0.0)
    prefix = jnp.cumsum(total, axis=0) - total
    states = jnp.stack(
        [local[b] + wide(jnp.exp(prefix[b]))[None] * before for b in range(blocks)]
    )
    states_low = states.astype(bf16)
    y_intra = jnp.einsum("bhij,bjhp->bihp", mix, u, preferred_element_type=f32)
    carried = jnp.einsum("bin,bnw->biw", cs, states_low, preferred_element_type=f32)
    y_inter = carried.reshape(blocks, Q, HG, P_SIZE) * head[..., None]
    mixer = y_intra + y_inter + skip_h[:, None] * xf
    mixer_flat = mixer.reshape(TL, GW)
    sig = jax.nn.sigmoid(gate)
    silu_gate = gate * sig
    gated = mixer_flat * silu_gate

    back_normed = dot_f32(cot_group, out_rows, ((1,), (1,))).astype(bf16).astype(f32)
    back_gain = back_normed * gain_row[None]
    sums = jnp.stack([jnp.sum(gated * gated, axis=1), jnp.sum(back_gain * gated, axis=1)])
    sums = sums + twin(sums)
    sums = jnp.sum(spread(sums, "fsdp", F), axis=0)
    scale = lax.rsqrt(sums[0] / DI + norm_epsilon)[:, None]
    cross = (sums[1][:, None] * scale * scale * scale) / DI
    gated_normed = (gated * scale * gain_row[None]).astype(bf16)
    branch = scatter_group(dot_f32(gated_normed, out_rows, ((1,), (0,))))
    block_out = (hidden + branch).astype(bf16)
    gate_gain_part = jnp.sum(back_normed * gated * scale, axis=0)
    back_gated = scale * back_gain - gated * cross
    back_mixer = back_gated * silu_gate
    back_gate = (back_gated * mixer_flat * sig * (1.0 + gate * (1.0 - sig))).astype(bf16)

    def finish_in(part):
        rows4 = part.astype(bf16).reshape(F, F, Dl // F, GW)
        got = lax.all_to_all(
            jnp.transpose(rows4, (1, 0, 2, 3)), "seq", 0, 0, axis_index_groups=parts, tiled=True
        )
        mine = jnp.sum(got.astype(f32), axis=0).astype(bf16)
        cols = lax.all_to_all(mine, "fsdp", 0, 0, tiled=True)
        everywhere = spread(cols, "seq", F, parts)
        full = pair_up(everywhere)
        return jnp.transpose(full, (1, 3, 0, 2, 4)).reshape(Dl, DI).astype(f32)

    def finish_out(part):
        got = lax.all_to_all(
            part.astype(bf16).reshape(F, QW, D),
            "seq",
            0,
            0,
            axis_index_groups=parts,
            tiled=True,
        )
        mine = jnp.sum(got.astype(f32), axis=0).astype(bf16).reshape(QW, F, Dl)
        cols = lax.all_to_all(jnp.transpose(mine, (1, 0, 2)), "fsdp", 0, 0, tiled=True)
        everywhere = spread(cols, "seq", F, parts)
        full = pair_up(everywhere)
        return jnp.transpose(full, (0, 2, 1, 3, 4)).reshape(DI, Dl).astype(f32)

    grad_out_weight = finish_out(dot_f32(gated_normed, cot_group, ((0,), (0,))))
    grad_gate_cols = finish_in(dot_f32(x_group, back_gate, ((0,), (0,))))

    dy = back_mixer.reshape(blocks, Q, HG, P_SIZE)
    dy_low = lax.optimization_barrier(dy.astype(bf16))
    dyh = (dy * head[..., None]).astype(bf16).reshape(blocks, Q, GW)
    fresh_back = jnp.einsum("bin,biw->bnw", cs, dyh, preferred_element_type=f32)
    local_back = [jnp.zeros((N, GW), f32)]
    for b in reversed(range(blocks)):
        local_back.append(local_back[-1] * wide(jnp.exp(total[b]))[None] + fresh_back[b])
    local_back = local_back[::-1]
    packed_back = spread(local_back[0], "seq", F, parts)
    after = jnp.zeros((N, GW), f32)
    for p in range(F):
        between = jnp.sum(jnp.where(((part_no < p) & (part_no > q))[:, None], totals, 0.0), axis=0)
        after = after + jnp.where(p > q, jnp.exp(between)[None] * packed_back[p], 0.0)
    suffix = whole_total[None] - prefix - total
    states_back = jnp.stack(
        [
            local_back[b + 1] + wide(jnp.exp(suffix[b]))[None] * after
            for b in range(blocks)
        ]
    )
    back_low = states_back.astype(bf16)
    back_mix = jnp.einsum("bihp,bjhp->bhij", dy_low, u, preferred_element_type=f32)
    back_scores = jnp.sum(back_mix * decay, axis=1).astype(bf16)
    back_c = jnp.einsum("bij,bjn->bin", back_scores, bs, preferred_element_type=f32)
    back_c = back_c + jnp.einsum("biw,bnw->bin", dyh, states_low, preferred_element_type=f32)
    back_b = jnp.einsum("bij,bin->bjn", back_scores, cs, preferred_element_type=f32)
    back_b = back_b + jnp.einsum(
        "bjw,bnw->bjn", uw.reshape(blocks, Q, GW), back_low, preferred_element_type=f32
    )
    du_intra = jnp.einsum("bhij,bihp->bjhp", mix, dy_low, preferred_element_type=f32)
    du_inter = (
        jnp.einsum("bjn,bnw->bjw", bs, back_low, preferred_element_type=f32).reshape(
            blocks, Q, HG, P_SIZE
        )
        * tail[..., None]
    )
    du = du_intra + du_inter
    back_x = du * dt[..., None] + skip_h[:, None] * dy
    back_dt = jnp.sum(xf * du, axis=-1)
    row_term = jnp.sum(dy_low.astype(f32) * y_intra + dy * y_inter, axis=-1)
    col_intra = jnp.sum(u.astype(f32) * du_intra, axis=-1)
    col_inter = jnp.sum(u32 * du_inter, axis=-1)
    across = jnp.sum(
        (states_back * states).reshape(blocks, N, HG, P_SIZE), axis=(1, 3)
    ) * jnp.exp(total)
    strict = lower - jnp.eye(Q, dtype=f32)
    back_ld = (
        jnp.einsum("it,bih->bth", lower, row_term - col_intra, precision=highest)
        + jnp.einsum("tj,bjh->bth", strict, col_inter, precision=highest)
        + across[:, None]
    ).reshape(TL, HG)
    back_dt = back_dt.reshape(TL, HG) - rate_h[None] * back_ld
    back_step = back_dt * jax.nn.sigmoid(step_in)
    step_bias_part = jnp.sum(back_step, axis=0)
    decay_part = jnp.sum(back_ld * log_decay, axis=0)
    skip_part = jnp.sum((dy * xf).reshape(TL, HG, P_SIZE), axis=(0, 2))

    back_act = jnp.concatenate(
        [back_x.reshape(TL, GW), back_b.reshape(TL, N), back_c.reshape(TL, N)], axis=1
    )
    back_pre = back_act * act_slope
    halo_back = lax.ppermute(back_pre[: KW - 1], "seq", back)
    back_ext = jnp.concatenate([back_pre, halo_back], axis=0)
    back_raw = sum(
        conv_w[k][None] * back_ext[KW - 1 - k : KW - 1 - k + TL] for k in range(KW)
    )
    conv_w_part = jnp.stack(
        [jnp.sum(back_pre * raw_ext[k : k + TL], axis=0) for k in range(KW)]
    )
    conv_b_part = jnp.sum(back_pre, axis=0)
    back_inner = back_raw[:, :GW].astype(bf16)
    back_pair_own = scatter_group(back_raw[:, GW:]).astype(bf16)
    back_step_low = back_step.astype(bf16)

    rows_low = jnp.concatenate(
        [back_gate, back_inner, jnp.pad(back_step_low, ((0, 0), (0, 8 - HG)))], axis=1
    )
    back_in = scatter_group(dot_f32(rows_low, in_rows, ((1,), (0,))))
    back_in = back_in + dot_f32(back_pair_own, pair_in, ((1,), (0,)))
    gain_part = jnp.sum(back_in * hidden * inverse_scale, axis=0)
    scaled_back = back_in * norm_gain[None, :]
    inverse_cubed = inverse_scale * inverse_scale * inverse_scale
    grad_input = (
        cotangent.astype(f32)
        + inverse_scale * scaled_back
        - hidden * inverse_cubed * jnp.mean(scaled_back * hidden, axis=1, keepdims=True)
    ).astype(bf16)

    grad_inner_cols = finish_in(dot_f32(x_group, back_inner, ((0,), (0,))))
    step_wide = jnp.pad(jnp.transpose(back_step_low), ((0, 8 - HG), (0, 0)))
    step_wide = step_wide.reshape(8 * TL // (2 * N), 2 * N)
    rest = pair_up(spread(jnp.concatenate([back_pair_own, step_wide], axis=0), "fsdp", F))
    rest = rest.reshape(S, tokens + step_wide.shape[0], 2 * N)
    pair_all = rest[:, :tokens].reshape(TL, 2 * N)
    step_all = rest[:, tokens:].reshape(S, 8, TL)[:, :HG].reshape(H, TL)
    x_rows = lax.dynamic_slice(x_group, (0, f * Dl), (TL, Dl))
    grad_pair = dot_f32(x_rows, pair_all, ((0,), (0,)))
    grad_step = dot_f32(step_all, x_rows, ((1,), (0,)))
    grad_rest = jnp.concatenate([jnp.transpose(grad_pair), grad_step], axis=0).astype(bf16)
    grad_rest = jnp.sum(spread(grad_rest, "seq", F, parts).astype(f32), axis=0)
    grad_in_weight = jnp.concatenate(
        [grad_gate_cols, grad_inner_cols, jnp.transpose(grad_rest)], axis=1
    )

    per_channel = jnp.concatenate(
        [conv_w_part[:, :GW], conv_b_part[None, :GW], gate_gain_part[None]], axis=0
    )
    per_channel = jnp.transpose(per_channel.reshape(KW + 2, HG, F, PF), (2, 0, 1, 3))
    per_channel = jnp.pad(
        per_channel.reshape(F, KW + 2, HG * PF), ((0, 0), (0, 0), (0, 128 - HG * PF))
    )
    per_head = jnp.concatenate([step_bias_part, decay_part, skip_part])
    per_head = jnp.broadcast_to(jnp.pad(per_head, (0, 128 - 3 * HG))[None, None], (F, 1, 128))
    slots = lax.dynamic_update_slice(
        jnp.zeros((devices, KW + 3, 128), f32),
        jnp.concatenate([per_channel, per_head], axis=1),
        (member * F, 0, 0),
    )
    pair_grads = jnp.concatenate([conv_w_part[:, GW:], conv_b_part[None, GW:]], axis=0)
    shared = jnp.concatenate(
        [
            pair_grads.reshape(devices, (KW + 1) * 2 * N // devices),
            gain_part.reshape(devices, D // devices),
        ],
        axis=1,
    )
    width = shared.shape[1]
    shared = jnp.pad(shared, ((0, 0), (0, 128 - width)))[:, None]
    slots = jnp.concatenate([slots, shared], axis=1)
    mine = jnp.sum(lax.all_to_all(slots, everyone, 0, 0, tiled=True), axis=0)
    shared_all = spread(mine[KW + 3 :], everyone, devices)[:, 0]
    cut = (KW + 1) * 2 * N // devices
    pair_grads = shared_all[:, :cut].reshape(KW + 1, 2 * N)
    gain_sum = shared_all[:, cut:width].reshape(D)
    channel_grads = mine[: KW + 2, : HG * PF].reshape(KW + 2, HG, PF)
    head_grads = mine[KW + 2]
    return (
        block_out,
        grad_input,
        gain_sum,
        grad_in_weight,
        channel_grads[:KW],
        channel_grads[KW],
        pair_grads[:KW],
        pair_grads[KW],
        head_grads[:HG],
        head_grads[HG : 2 * HG],
        head_grads[2 * HG : 3 * HG],
        channel_grads[KW + 1],
        grad_out_weight,
    )


def solution(mesh):
    in_specs = (
        P(("seq", "fsdp"), None),
        P(),
        P("fsdp", None),
        P(None, "seq", "fsdp"),
        P("seq", "fsdp"),
        P(),
        P(),
        P("seq"),
        P("seq"),
        P("seq"),
        P("seq", "fsdp"),
        P(None, "fsdp"),
        P(("seq", "fsdp"), None),
    )
    out_specs = (
        P(("seq", "fsdp"), None),
        P(("seq", "fsdp"), None),
        P(),
        P("fsdp", None),
        P(None, "seq", "fsdp"),
        P("seq", "fsdp"),
        P(),
        P(),
        P("seq"),
        P("seq"),
        P("seq"),
        P("seq", "fsdp"),
        P(None, "fsdp"),
    )
    return jax.shard_map(body, mesh=mesh, in_specs=in_specs, out_specs=out_specs, check_vma=False)
```

```python
import functools

import jax
import jax.numpy as jnp
from jax import lax
from jax.experimental import pallas as pl
from jax.experimental.pallas import tpu as pltpu
from jax.sharding import PartitionSpec as P


H = 48
P_SIZE = 64
N = 128
KW = 4
Q = 256

norm_epsilon = 1e-05
far_below = -1e30
highest = lax.Precision.HIGHEST
f32 = jnp.float32
bf16 = jnp.bfloat16
everyone = ("seq", "fsdp")


def spread(value, axis, count):
    copies = jnp.broadcast_to(value[None], (count,) + value.shape)
    return lax.all_to_all(copies, axis, 0, 0, tiled=True)


def dot_f32(left, right, dims, batch=((), ())):
    return lax.dot_general(left, right, (dims, batch), preferred_element_type=f32)


def mm(left, right, dims, precision=None):
    return lax.dot_general(
        left, right, (dims, ((), ())), preferred_element_type=f32, precision=precision
    )


def split3(value):
    first = value.astype(bf16)
    rest = value - first.astype(f32)
    second = rest.astype(bf16)
    return first, second, (rest - second.astype(f32)).astype(bf16)


def mm_ones(ones, value, dims, flip=False):
    ones = ones.astype(bf16)
    parts = [
        mm(part, ones, dims) if flip else mm(ones, part, dims) for part in reversed(split3(value))
    ]
    return sum(parts[1:], parts[0])


def lanes_of(width):
    return [(at, min(2 * P_SIZE, width - at)) for at in range(0, width, 2 * P_SIZE)]


def widen(per_head, width):
    rows = per_head.shape[0]
    out = []
    for at, wide in lanes_of(width):
        h = at // P_SIZE
        first = jnp.broadcast_to(per_head[:, h : h + 1], (rows, wide))
        if wide > P_SIZE:
            second = jnp.broadcast_to(per_head[:, h + 1 : h + 2], (rows, wide))
            lane = lax.broadcasted_iota(jnp.int32, (rows, wide), 1)
            first = jnp.where(lane < P_SIZE, first, second)
        out.append(first)
    return out[0] if len(out) == 1 else jnp.concatenate(out, axis=1)


def pick_heads(width):
    row = lax.broadcasted_iota(jnp.int32, (width, 8), 0)
    col = lax.broadcasted_iota(jnp.int32, (width, 8), 1)
    return ((row >= col * P_SIZE) & (row < (col + 1) * P_SIZE)).astype(f32)


def lower_ones(strict=False):
    row = lax.broadcasted_iota(jnp.int32, (Q, Q), 0)
    col = lax.broadcasted_iota(jnp.int32, (Q, Q), 1)
    return (row > col) if strict else (row >= col)


def upper_ones():
    row = lax.broadcasted_iota(jnp.int32, (Q, Q), 0)
    col = lax.broadcasted_iota(jnp.int32, (Q, Q), 1)
    return row <= col


def split_heads(value):
    if value.shape[1] == P_SIZE:
        return [value]
    lane = lax.broadcasted_iota(jnp.int32, value.shape, 1)
    zero = jnp.zeros_like(value)
    return [jnp.where(lane < P_SIZE, value, zero), jnp.where(lane < P_SIZE, zero, value)]


def soft_plus(value):
    small = jnp.exp(-jnp.abs(value))
    series = small * (1.0 - small * (0.5 - small * (1.0 / 3.0 - 0.25 * small)))
    return jnp.maximum(value, 0.0) + jnp.where(small < 0.01, series, jnp.log(1.0 + small))


def choose_half(spot_ref, mine_ref, other_ref, out_ref):
    half = pl.program_id(0) // (pl.num_programs(0) // 2)
    mine = half == spot_ref[1]

    @pl.when(mine)
    def _():
        out_ref[...] = mine_ref[...]

    @pl.when(jnp.logical_not(mine))
    def _():
        out_ref[...] = other_ref[...]


def to_halves(spot_ref, block, value, away_ref, mine_ref):
    mine = (block // (pl.num_programs(0) // 2)) == spot_ref[1]

    @pl.when(mine)
    def _():
        mine_ref[...] = value

    @pl.when(jnp.logical_not(mine))
    def _():
        away_ref[...] = value


def project_kernel(
    absolute, QW, spot_ref, mine_ref, other_ref, halo0_ref, halo1_ref, *refs
):
    count = (len(refs) - 23) // 2
    pieces = refs[: 2 * count]
    (
        cwx_ref, cwp_ref, heads_ref,
        x_ref, win_ref, wpair_ref, rawx_ref, rawp_ref, actx_ref, actp_ref, slopex_ref,
        slopep_ref, dt_ref, cum_ref, cumt_ref, stepin_ref, local_ref, total_ref, final_ref,
        state, whole, extx, extp,
    ) = refs[2 * count :]
    b = pl.program_id(0)
    GW = rawx_ref.shape[1]
    PH = N // count
    Dl = win_ref.shape[1] // count
    HA = pieces[0].shape[1] - PH

    @pl.when(b == 0)
    def _():
        def place(ref, at, rows, value):
            if absolute:
                ref[at : at + rows.stop - rows.start, cols] = value[far, rows]
            else:
                at = pl.multiple_of(at, 16)
                ref[pl.ds(at, rows.stop - rows.start), cols] = value[far, rows]

        for k in range(count):
            first, second = pieces[2 * k], pieces[2 * k + 1]
            here = k if absolute else spot_ref[0] ^ k
            for src in range(count):
                cols = slice(src * Dl, (src + 1) * Dl)
                far = lax.rem(spot_ref[2] - src + count, count)
                place(win_ref, here * QW, slice(0, HA), first)
                place(wpair_ref, here * 2 * PH, slice(HA, HA + PH), first)
                if HA < QW:
                    place(win_ref, here * QW + HA, slice(0, QW - HA), second)
                place(
                    wpair_ref, here * 2 * PH + PH, slice(QW - HA, QW - HA + PH), second
                )
                if k == 0:
                    win_ref[GW : GW + 8, cols] = second[far, QW - HA + PH : QW - HA + PH + 8]
        state[...] = jnp.zeros_like(state)
        whole[...] = jnp.zeros_like(whole)
        edge = halo0_ref[...] + halo1_ref[...]
        ex = mm(edge, win_ref[0:GW], ((1,), (1,))).astype(bf16).astype(f32)
        ep = mm(edge, wpair_ref[...], ((1,), (1,))).astype(bf16).astype(f32)
        extx[0:8] = ex[8:16]
        extp[0:8] = ep[8:16]

    @pl.when(b > 0)
    def _():
        extx[0:8] = extx[Q : Q + 8]
        extp[0:8] = extp[Q : Q + 8]

    choose_half(spot_ref, mine_ref, other_ref, x_ref)
    x = x_ref[...]
    rx = mm(x, win_ref[0:GW], ((1,), (1,))).astype(bf16)
    rp = mm(x, wpair_ref[...], ((1,), (1,))).astype(bf16)
    st = mm(x, win_ref[GW : GW + 8], ((1,), (1,))).astype(bf16).astype(f32)
    rawx_ref[...] = rx
    rawp_ref[...] = rp
    extx[8 : Q + 8] = rx.astype(f32)
    extp[8 : Q + 8] = rp.astype(f32)

    def conv(ext, cw, act_out, slope_out):
        pre = cw[KW : KW + 1, :]
        for k in range(KW):
            pre = pre + cw[k : k + 1, :] * ext[9 - KW + k : 9 - KW + k + Q]
        sig = jax.nn.sigmoid(pre)
        act_out[...] = (pre * sig).astype(bf16)
        slope_out[...] = (sig * (1.0 + pre * (1.0 - sig))).astype(bf16)

    conv(extx, cwx_ref, actx_ref, slopex_ref)
    conv(extp, cwp_ref, actp_ref, slopep_ref)
    step_in = st + heads_ref[0:1, 0:8]
    dt = soft_plus(step_in)
    ld = -dt * heads_ref[1:2, 0:8]
    cum = mm_ones(lower_ones().astype(f32), ld, ((1,), (0,)))
    dt_ref[...] = dt
    cum_ref[...] = cum
    stepin_ref[...] = step_in
    eye = (
        lax.broadcasted_iota(jnp.int32, (8, 8), 0) == lax.broadcasted_iota(jnp.int32, (8, 8), 1)
    ).astype(f32)
    cumt_ref[...] = mm(eye, cum, ((1,), (1,)), highest)
    total = cum[Q - 1 : Q]
    total_wide = widen(total, GW)
    total_ref[0] = jnp.broadcast_to(total_wide, (8, GW))
    u32 = actx_ref[...].astype(f32) * widen(dt, GW)
    uw = (u32 * widen(jnp.exp(total - cum), GW)).astype(bf16)
    local_ref[0] = state[...]
    state[...] = state[...] * jnp.exp(total_wide) + mm(actp_ref[:, 0:N], uw, ((0,), (0,)))
    whole[...] = whole[...] + total_wide

    @pl.when(b == pl.num_programs(0) - 1)
    def _():
        final_ref[0:N] = state[...]
        final_ref[N : N + 8] = whole[...]


def intra_kernel(spot_ref, actx_ref, actp_ref, dt_ref, cum_ref, cumt_ref, y_ref):
    GW = y_ref.shape[1]
    scores = mm(actp_ref[:, N : 2 * N], actp_ref[:, 0:N], ((1,), (1,)))
    causal = lower_ones()
    for at, wide in lanes_of(GW):
        u = (
            actx_ref[:, at : at + wide].astype(f32)
            * widen(dt_ref[...], GW)[:, at : at + wide]
        ).astype(bf16)
        mixes = []
        for h in range(at // P_SIZE, (at + wide) // P_SIZE):
            gap = cum_ref[:, h : h + 1] - cumt_ref[h : h + 1, :]
            mixes.append((scores * jnp.exp(jnp.where(causal, gap, far_below))).astype(bf16))
        y_ref[:, at : at + wide] = sum(
            mm(m, p, ((1,), (0,))) for m, p in zip(mixes, split_heads(u), strict=True)
        )


def merge_states(spot_ref, states, totals, forward):
    q = spot_ref[0]
    out = jnp.zeros(states[0].shape, f32)
    count = len(states) + 1
    for k in range(1, count):
        p = q ^ k
        between = jnp.zeros(totals[0].shape, f32)
        for j in range(1, count):
            if j != k:
                o = q ^ j
                inside = ((o > p) & (o < q)) if forward else ((o < p) & (o > q))
                between = between + totals[j - 1] * inside.astype(f32)
        reaches = (p < q) if forward else (p > q)
        out = out + states[k - 1] * (jnp.exp(between) * reaches.astype(f32))
    return out


def inter_kernel(
    spot_ref, actx_ref, actp_ref, cum_ref, total_ref, local_ref, y_ref, z_ref, bn_ref, rows_ref,
    *refs,
):
    finals = refs[:-5]
    yx_ref, states_ref, sums_ref, prefix, before_ref = refs[-5:]
    GW = y_ref.shape[1]

    @pl.when(pl.program_id(0) == 0)
    def _():
        prefix[...] = jnp.zeros_like(prefix)
        before_ref[...] = merge_states(
            spot_ref, [r[0:N] for r in finals], [r[N : N + 1] for r in finals], True
        )

    low = (local_ref[0] + jnp.exp(prefix[0:1]) * before_ref[...]).astype(bf16)
    prefix[...] = prefix[...] + total_ref[0]
    states_ref[0] = low
    yx = mm(actp_ref[:, N : 2 * N], low, ((1,), (0,))) * widen(jnp.exp(cum_ref[...]), GW)
    yx_ref[...] = yx
    mixer = y_ref[...] + yx + rows_ref[1:2] * actx_ref[...].astype(f32)
    z = z_ref[...].astype(f32)
    gated = mixer * (z * jax.nn.sigmoid(z))
    row = lax.broadcasted_iota(jnp.int32, (8, GW), 0)
    squares = mm_ones((row == 0).astype(f32), gated * gated, ((1,), (1,)))
    cross = mm_ones(
        (row == 1).astype(f32), bn_ref[...].astype(f32) * rows_ref[0:1] * gated, ((1,), (1,))
    )
    sums_ref[...] = squares + cross


def gate_kernel(
    spot_ref, actx_ref, actp_ref, cum_ref, total_ref, y_ref, yx_ref, z_ref, bn_ref, rows_ref, *refs
):
    sums = sum(r[...] for r in refs[:-10])
    out_rows_ref, gn_ref, bgate_ref, dy_ref, local_ref, first_ref, small_ref = refs[-10:-3]
    away_ref, mine_ref, state = refs[-3:]
    GW = y_ref.shape[1]
    b = pl.program_id(0)

    @pl.when(b == 0)
    def _():
        state[...] = jnp.zeros_like(state)
        small_ref[...] = jnp.zeros_like(small_ref)

    eye = (
        lax.broadcasted_iota(jnp.int32, (8, 8), 0) == lax.broadcasted_iota(jnp.int32, (8, 8), 1)
    ).astype(f32)
    cols = mm(sums, eye, ((0,), (0,)), highest)
    scale = lax.rsqrt(cols[:, 0:1] * rows_ref[2:3, 0:1] + norm_epsilon)
    cross = cols[:, 1:2] * scale * scale * scale * rows_ref[2:3, 0:1]
    x = actx_ref[...].astype(f32)
    mixer = y_ref[...] + yx_ref[...] + rows_ref[1:2] * x
    z = z_ref[...].astype(f32)
    sig = jax.nn.sigmoid(z)
    silu = z * sig
    gated = mixer * silu
    bn = bn_ref[...].astype(f32)
    gain = rows_ref[0:1]
    gn = (gated * scale * gain).astype(bf16)
    gn_ref[...] = gn
    to_halves(
        spot_ref,
        pl.num_programs(0) - 1 - b,
        mm(gn, out_rows_ref[...], ((1,), (0,))).astype(bf16),
        away_ref,
        mine_ref,
    )
    back_gated = scale * (bn * gain) - gated * cross
    dy = (back_gated * silu).astype(bf16)
    dy_ref[...] = dy
    bgate_ref[...] = (back_gated * mixer * sig * (1.0 + z * (1.0 - sig))).astype(bf16)
    dyf = dy.astype(f32)
    small_ref[0:1] += jnp.sum(bn * gated * scale, axis=0, keepdims=True)
    small_ref[1:2] += jnp.sum(dyf * x, axis=0, keepdims=True)
    dyh = (dyf * widen(jnp.exp(cum_ref[...]), GW)).astype(bf16)
    local_ref[0] = state[...]
    state[...] = state[...] * jnp.exp(total_ref[0, 0:1]) + mm(
        actp_ref[:, N : 2 * N], dyh, ((0,), (0,))
    )

    @pl.when(b == pl.num_programs(0) - 1)
    def _():
        first_ref[...] = state[...]


def back_intra_kernel(
    spot_ref, actx_ref, actp_ref, dt_ref, cum_ref, cumt_ref, dy_ref, states_ref,
    du_ref, dbc_ref,
):
    GW = dy_ref.shape[1]
    bs = actp_ref[:, 0:N]
    cs = actp_ref[:, N : 2 * N]
    scores = mm(cs, bs, ((1,), (1,)))
    causal = lower_ones()
    dscores = jnp.zeros((Q, Q), f32)
    dt_wide = widen(dt_ref[...], GW)
    for at, wide in lanes_of(GW):
        u = (actx_ref[:, at : at + wide].astype(f32) * dt_wide[:, at : at + wide]).astype(bf16)
        du = jnp.zeros((Q, wide), f32)
        for k, dyk in enumerate(split_heads(dy_ref[:, at : at + wide])):
            h = at // P_SIZE + k
            gap = cum_ref[:, h : h + 1] - cumt_ref[h : h + 1, :]
            decay = jnp.exp(jnp.where(causal, gap, far_below))
            mix = (scores * decay).astype(bf16)
            dscores = dscores + mm(dyk, u, ((1,), (1,))) * decay
            du = du + mm(mix, dyk, ((0,), (0,)))
        du_ref[:, at : at + wide] = du
    dlow = dscores.astype(bf16)
    dyh = (dy_ref[...].astype(f32) * widen(jnp.exp(cum_ref[...]), GW)).astype(bf16)
    dbc_ref[:, 0:N] = mm(dlow, cs, ((0,), (0,)))
    dbc_ref[:, N : 2 * N] = mm(dlow, bs, ((1,), (0,))) + mm(dyh, states_ref[0], ((1,), (1,)))


def back_inter_kernel(
    spot_ref, actx_ref, actp_ref, slopex_ref, slopep_ref, dt_ref, cum_ref, stepin_ref, total_ref, whole_ref,
    local_ref, states_ref, dy_ref, y_ref, yx_ref, du_ref, dbc_ref, heads_ref, rows_ref, *refs,
):
    others, refs = refs[:-7], refs[-7:]
    dprex_ref, dprep_ref, dstep_ref, hsum_ref, edge_ref, seen, after_ref = refs
    finals, firsts = others[: len(others) // 2], others[len(others) // 2 :]
    GW = dy_ref.shape[1]
    b = pl.program_id(0)

    @pl.when(b == 0)
    def _():
        seen[...] = jnp.zeros_like(seen)
        hsum_ref[...] = jnp.zeros_like(hsum_ref)
        after_ref[...] = merge_states(
            spot_ref, [r[...] for r in firsts], [r[N : N + 1] for r in finals], False
        )

    seen[...] = seen[...] + total_ref[0]
    left = jnp.exp(whole_ref[0:1] - seen[0:1])
    grown = local_ref[0] + left * after_ref[...]
    low = grown.astype(bf16)
    cum = cum_ref[...]
    total = cum[Q - 1 : Q]
    dt = dt_ref[...]
    dt_wide = widen(dt, GW)
    tail = widen(jnp.exp(total - cum), GW)
    x = actx_ref[...].astype(f32)
    u32 = x * dt_wide
    ub = u32.astype(bf16).astype(f32)
    uw = (u32 * tail).astype(bf16)
    bs = actp_ref[:, 0:N]
    du_inter = mm(bs, low, ((1,), (0,))) * tail
    dui = du_ref[...]
    du = dui + du_inter
    dy = dy_ref[...].astype(f32)
    dprex_ref[...] = (du * dt_wide + rows_ref[1:2] * dy) * slopex_ref[...].astype(f32)
    db = dbc_ref[:, 0:N] + mm(uw, low, ((1,), (1,)))
    dprep_ref[:, 0:N] = db * slopep_ref[:, 0:N].astype(f32)
    dprep_ref[:, N : 2 * N] = dbc_ref[:, N : 2 * N] * slopep_ref[:, N : 2 * N].astype(f32)

    @pl.when(b == 0)
    def _():
        edge_ref[:, 0:GW] = dprex_ref[0:8]
        edge_ref[:, GW:] = dprep_ref[0:8]

    sel = pick_heads(GW)
    ddt = mm_ones(sel, x * du, ((1,), (0,)), True)
    later = mm_ones(sel, dy * (y_ref[...] + yx_ref[...]) - ub * dui, ((1,), (0,)), True)
    earlier = mm_ones(sel, u32 * du_inter, ((1,), (0,)), True)
    over = jnp.sum(grown * states_ref[0].astype(f32), axis=0, keepdims=True)
    over = mm(jnp.broadcast_to(over, (8, GW)), sel, ((1,), (0,)), highest)[0:1] * jnp.exp(total)
    dld = (
        mm_ones(upper_ones().astype(f32), later, ((1,), (0,)))
        + mm_ones(lower_ones(True).astype(f32), earlier, ((1,), (0,)))
        + over
    )
    rate = heads_ref[1:2, 0:8]
    dstep = (ddt - rate * dld) * jax.nn.sigmoid(stepin_ref[...])
    dstep_ref[...] = dstep
    hsum_ref[0:1] += jnp.sum(dstep, axis=0, keepdims=True)
    hsum_ref[1:2] += jnp.sum(-dld * dt * rate, axis=0, keepdims=True)


def back_conv_kernel(
    spot_ref, dprex_ref, dprep_ref, nextx_ref, nextp_ref, halo_ref, rawx_ref, rawp_ref,
    cwx_ref, cwp_ref, bgate_ref, step_ref, x_ref, wgate_ref, win_ref,
    backx_ref, pair_away_ref, pair_mine_ref, gradx_ref, gradp_ref, away_ref, mine_ref, gain_ref,
    extx, extp,
):
    b = pl.program_id(0)
    last = b == pl.num_programs(0) - 1

    @pl.when(b == 0)
    def _():
        gradx_ref[...] = jnp.zeros_like(gradx_ref)
        gradp_ref[...] = jnp.zeros_like(gradp_ref)
        gain_ref[...] = jnp.zeros_like(gain_ref)

    def conv(dpre, following, halo, raw, cw, ext, grad):
        ext[0:Q] = dpre[...]
        ext[Q : Q + 8] = jnp.where(last, halo, following[...])
        value = raw[...].astype(f32)
        total = jnp.zeros(dpre.shape, f32)
        for k in range(KW):
            shifted = ext[KW - 1 - k : KW - 1 - k + Q]
            total = total + cw[k : k + 1, :] * shifted
            grad[k : k + 1] += jnp.sum(value * shifted, axis=0, keepdims=True)
        grad[KW : KW + 1] += jnp.sum(dpre[...], axis=0, keepdims=True)
        return total.astype(bf16)

    GW = dprex_ref.shape[1]
    inner = conv(dprex_ref, nextx_ref, halo_ref[:, 0:GW], rawx_ref, cwx_ref, extx, gradx_ref)
    backx_ref[...] = inner
    pair = conv(dprep_ref, nextp_ref, halo_ref[:, GW:], rawp_ref, cwp_ref, extp, gradp_ref)
    to_halves(spot_ref, b, pair, pair_away_ref, pair_mine_ref)
    value = mm(bgate_ref[...], wgate_ref[...], ((1,), (0,)))
    value = value + mm(step_ref[...].astype(bf16), win_ref[GW : GW + 8], ((1,), (0,)))
    value = value + mm(inner, win_ref[0:GW], ((1,), (0,)))
    gain_ref[0:1] += jnp.sum(value * x_ref[...].astype(f32), axis=0, keepdims=True)
    to_halves(spot_ref, b, value.astype(bf16), away_ref, mine_ref)


def cotangent_kernel(absolute, spot_ref, mine_ref, other_ref, x_ref, *refs):
    pieces = refs[:-5]
    cot_ref, gate_rows_ref, rows_ref, z_ref, bn_ref = refs[-5:]
    count = len(pieces)
    QW = rows_ref.shape[0] // count
    Dl = rows_ref.shape[1] // count

    @pl.when(pl.program_id(0) == 0)
    def _():
        for k, piece in enumerate(pieces):
            for src in range(count):
                cols = slice(src * Dl, (src + 1) * Dl)
                far = lax.rem(spot_ref[2] - src + count, count)
                if absolute:
                    gate_rows_ref[k * QW : (k + 1) * QW, cols] = piece[far, 0:QW]
                    rows_ref[k * QW : (k + 1) * QW, cols] = piece[far, QW : 2 * QW]
                else:
                    at = pl.multiple_of((spot_ref[0] ^ k) * QW, 16)
                    gate_rows_ref[pl.ds(at, QW), cols] = piece[far, 0:QW]
                    rows_ref[pl.ds(at, QW), cols] = piece[far, QW : 2 * QW]

    choose_half(spot_ref, mine_ref, other_ref, cot_ref)
    z_ref[...] = mm(x_ref[...], gate_rows_ref[...], ((1,), (1,))).astype(bf16)
    bn_ref[...] = mm(cot_ref[...], rows_ref[...], ((1,), (1,))).astype(bf16)


def partial_blocks_kernel(count, pairs, spot_ref, *refs):
    lefts, rights = refs[:pairs], refs[pairs : 2 * pairs]
    step_ref = refs[2 * pairs] if pairs == 1 else None
    outs, turned, total = refs[-count - 2 : -2], refs[-2], refs[-1]
    GW = total.shape[0]
    QW = GW // count

    @pl.when(pl.program_id(0) == 0)
    def _():
        for at in range(pairs):
            turned[at] = lefts[at][...].T

    for at in range(pairs):
        right = rights[at][...]
        total[...] = mm(turned[at], right, ((1,), (0,)))
        for k in range(count):
            start = pl.multiple_of((spot_ref[0] ^ k) * QW, 8)
            outs[k][0, at * QW : (at + 1) * QW] = total[pl.ds(start, QW)].astype(bf16)
    if step_ref is not None:
        value = mm(step_ref[...].astype(bf16), rights[0][...], ((0,), (0,)))
        for k in range(count):
            keep = ((spot_ref[0] ^ k) == 0).astype(f32)
            outs[k][0, QW : QW + 8] = (value * keep).astype(bf16)


def partial_kernel(count, pairs, spot_ref, *refs):
    lefts, rights = refs[:pairs], refs[pairs : 2 * pairs]
    step_ref = refs[2 * pairs] if pairs == 1 else None
    outs = refs[len(refs) - count - pairs - (pairs == 1) : len(refs) - pairs - (pairs == 1)]
    sums = refs[len(refs) - pairs - (pairs == 1) :]
    b = pl.program_id(0)
    lefts = [r[...] for r in lefts]
    rights = [r[...] for r in rights]
    if step_ref is not None:
        lefts.append(step_ref[...].astype(bf16))
        rights.append(rights[0])
    for left, right, total in zip(lefts, rights, sums, strict=True):
        value = mm(left, right, ((0,), (0,)))

        @pl.when(b == 0)
        def _(value=value, total=total):
            total[...] = value

        @pl.when(b > 0)
        def _(value=value, total=total):
            total[...] += value

    @pl.when(b == pl.num_programs(0) - 1)
    def _():
        GW, D = sums[0].shape
        QW, Dl = GW // count, D // count
        for k in range(count):
            part = spot_ref[0] ^ k
            start = pl.multiple_of(part * QW, 8)
            for j in range(count):
                cols = slice(j * Dl, (j + 1) * Dl)
                for at in range(pairs):
                    outs[k][j, at * QW : (at + 1) * QW] = sums[at][pl.ds(start, QW), cols].astype(
                        bf16
                    )
                if step_ref is not None:
                    keep = (part == 0).astype(f32)
                    outs[k][j, QW : QW + 8] = (sums[1][:, cols] * keep).astype(bf16)


def sum_kernel(outs_count, spot_ref, *refs):
    i = pl.program_id(0)
    outs = refs[len(refs) - outs_count :]
    total = sum(r[0].astype(f32) for r in refs[: len(refs) - outs_count]).astype(bf16)
    for k, out in enumerate(outs):

        @pl.when(i == k)
        def _(out=out):
            out[...] = total


def place_rows(count, spot_ref, step, own, other, rows, out_ref):
    q, c, f = spot_ref[0], spot_ref[1], spot_ref[2]
    far = lax.rem(f - lax.rem(step, count) + count, count)
    width = rows.stop - rows.start
    for side in range(2):
        owner = c if side == 0 else 1 - c

        @pl.when((step >= owner * count) & (step < (owner + 1) * count))
        def _(side=side):
            for k in range(count):
                value = own[k][far, rows] if side == 0 else other[k, far, rows]
                out_ref[pl.ds(pl.multiple_of((q ^ k) * width, 8), width)] = value.astype(f32)


def early_grads_kernel(count, spot_ref, *refs):
    own, other, in_ref, out_ref = refs[:count], refs[count], refs[-2], refs[-1]
    QW = own[0].shape[1] // 2
    step = pl.program_id(0)
    place_rows(count, spot_ref, step, own, other, slice(0, QW), out_ref)
    place_rows(count, spot_ref, step, own, other, slice(QW, 2 * QW), in_ref)


def pair_grads_kernel(spot_ref, pair_ref, array_ref, out_ref):
    out_ref[...] = pair_ref[...]


def late_grads_kernel(count, QW, heads, spot_ref, *refs):
    own, other, in_ref = refs[:count], refs[count], refs[-1]
    step = pl.program_id(0)
    place_rows(count, spot_ref, step, own, other, slice(0, QW), in_ref)
    q, c, f = spot_ref[0], spot_ref[1], spot_ref[2]
    GW = in_ref.shape[0]
    groups = 2 * count
    for block in range(-(-(2 * N + H) // GW)):

        @pl.when(step == groups + block)
        def _(block=block):
            first = block * GW
            for k in range(count):

                @pl.when((q ^ k) == 0)
                def _(k=k):
                    for g in range(groups):
                        at = 2 * N + g * heads - first
                        if at < 0 or at >= GW:
                            continue
                        far = lax.rem(f - g % count + count, count)
                        mine = own[k][far, QW : QW + 8].astype(f32)
                        theirs = other[k, far, QW : QW + 8].astype(f32)
                        value = jnp.where(c == g // count, mine, theirs)
                        in_ref[at : at + heads] = value[0:heads]


def body(
    block_in,
    norm_gain,
    in_weight,
    conv_inner_weight,
    conv_inner_bias,
    conv_pair_weight,
    conv_pair_bias,
    step_bias,
    decay_log,
    skip_gain,
    gate_gain,
    out_weight,
    cotangent,
):
    S = lax.axis_size("seq")
    F = lax.axis_size("fsdp")
    devices = S * F
    R = S // F
    s = lax.axis_index("seq")
    f = lax.axis_index("fsdp")
    q = s // R
    c = s % R
    member = c * F + f
    spot = jnp.stack([q, c, f]).astype(jnp.int32)
    tokens, D = block_in.shape
    TL = tokens * S
    blocks = TL // Q
    half = blocks // 2
    HG = H // S
    GW = HG * P_SIZE
    QW = GW // F
    DI = H * P_SIZE
    Dl = in_weight.shape[0]
    PF = P_SIZE // F
    NP = 2 * N
    PH = N // F
    absolute = QW % 16 != 0 or PH % 16 != 0
    twins = [(i, i ^ 1) for i in range(S)]
    back = [(i + R, i) for i in range(S - R)]
    bits = [1 << i for i in range(F.bit_length() - 1)]
    struct = jax.ShapeDtypeStruct

    def twin(value):
        return lax.ppermute(value, "seq", twins)

    def from_part(value, k):
        return lax.ppermute(value, "seq", [(i, i ^ (k * R)) for i in range(S)])

    def from_line(value, k):
        return lax.ppermute(value, "fsdp", [(i, (i + k) % F) for i in range(F)])

    def take(value, at, axis=0):
        return lax.dynamic_index_in_dim(value, at, axis, keepdims=False)

    def line_chain(value):
        up, down, ups, downs = value, value, [], []
        for k in range(1, F):
            up = lax.ppermute(up, "fsdp", [(i, i + 1) for i in range(k - 1, F - 1)])
            down = lax.ppermute(down, "fsdp", [(i, i - 1) for i in range(1, F - k + 1)])
            ups.append(up)
            downs.append(down)
        line = []
        for j in range(F):
            here = value
            for k in range(1, F):
                if j + k < F:
                    here = jnp.where(f == j + k, ups[k - 1], here)
                if j - k >= 0:
                    here = jnp.where(f == j - k, downs[k - 1], here)
            line.append(here)
        return jnp.concatenate(line, axis=0)

    def line_ordered(rel):
        line = []
        for j in range(F):
            here = rel[0]
            for k in range(1, F):
                here = jnp.where(lax.rem(f - k + F, F) == j, rel[k], here)
            line.append(here)
        return jnp.concatenate(line, axis=0)

    def gather_parts(value, order):
        pieces = {0: value}
        for bit in order:
            pieces.update({k ^ bit: from_part(v, bit) for k, v in list(pieces.items())})
        return [pieces[k] for k in range(F)]

    def in_order(pieces):
        if not absolute:
            return pieces
        out = []
        for j in range(F):
            here = pieces[0]
            for k in range(1, F):
                here = jnp.where(q == (j ^ k), pieces[k], here)
            out.append(here)
        return out

    def rows_of(width, shift=0):
        return pl.BlockSpec((Q, width), lambda i, p: (i + shift, 0))

    def rows_back(width):
        return pl.BlockSpec((Q, width), lambda i, p: (blocks - 1 - i, 0))

    def rows_half(width):
        return pl.BlockSpec((Q, width), lambda i, p: (lax.rem(i, half), 0))

    def fixed(*shape):
        return pl.BlockSpec(shape, lambda i, p: (0,) * len(shape))

    def per_block(rows, width, shift=0):
        return pl.BlockSpec((1, rows, width), lambda i, p: (i + shift, 0, 0))

    def per_block_back(rows, width):
        return pl.BlockSpec((1, rows, width), lambda i, p: (blocks - 1 - i, 0, 0))

    def half_of(width, own):
        def index(i, p):
            return (
                jnp.where(p[1] == own, jnp.maximum(i - half, 0), jnp.minimum(i, half - 1)), 0
            )

        return pl.BlockSpec((Q, width), index)

    def half_of_back(width, own):
        def index(i, p):
            at = blocks - 1 - i
            return (
                jnp.where(p[1] == own, jnp.maximum(at - half, 0), jnp.minimum(at, half - 1)), 0
            )

        return pl.BlockSpec((Q, width), index)

    across = pl.BlockSpec((8, Q), lambda i, p: (0, i))
    across_back = pl.BlockSpec((8, Q), lambda i, p: (0, blocks - 1 - i))
    anywhere = pl.BlockSpec(memory_space=pl.ANY)

    def call(kernel, steps, in_specs, out_specs, out_shape, scratch=(), aliases=None):
        return pl.pallas_call(
            kernel,
            grid_spec=pltpu.PrefetchScalarGridSpec(
                num_scalar_prefetch=1,
                grid=(steps,),
                in_specs=in_specs,
                out_specs=out_specs,
                scratch_shapes=list(scratch),
            ),
            out_shape=out_shape,
            input_output_aliases=aliases or {},
            compiler_params=pltpu.CompilerParams(dimension_semantics=("arbitrary",)),
        )

    small = jnp.concatenate(
        [
            conv_inner_weight.reshape(KW, HG * PF),
            conv_inner_bias.reshape(1, HG * PF),
            gate_gain.reshape(1, HG * PF),
        ],
        axis=0,
    )
    small = jnp.pad(small, ((0, 0), (0, 128 - HG * PF)))
    heads_row = jnp.concatenate([step_bias, decay_log, skip_gain])
    heads_row = jnp.pad(heads_row, (0, 128 - 3 * HG))[None]
    small = jnp.concatenate([small, heads_row, jnp.zeros((1, 128), f32)], axis=0)
    small_all = spread(small, everyone, devices)
    small_here = lax.dynamic_slice(small_all, (member * F, 0, 0), (F, 8, 128))
    chan = small_here[:, : KW + 2, : HG * PF].reshape(F, KW + 2, HG, PF)
    chan = jnp.transpose(chan, (1, 2, 0, 3)).reshape(KW + 2, GW)
    heads_here = small_here[0, KW + 2]
    bias_h = heads_here[:HG]
    rate_h = jnp.exp(heads_here[HG : 2 * HG])
    skip_h = heads_here[2 * HG : 3 * HG]

    hidden = block_in.astype(f32)
    inverse_scale = lax.rsqrt(jnp.mean(hidden * hidden, axis=1, keepdims=True) + norm_epsilon)
    normed = (hidden * inverse_scale * norm_gain[None, :]).astype(bf16)
    x_line = line_chain(normed)
    x_other = twin(x_line)
    last_rows = x_line[F * tokens - 16 :]
    edge_own = lax.ppermute(last_rows, "seq", [(i, i + R) for i in range(S - R) if i % R == R - 1])
    edge_twin = lax.ppermute(last_rows, "seq", [(i, i + 1) for i in range(S - R) if i % R == R - 1])

    columns = jnp.transpose(in_weight)
    HA = QW // 2 if QW % 32 == 0 else QW

    def rows_for(place):
        group = c * F + place
        inner = lax.dynamic_slice(columns, (DI + group * GW + q * QW, 0), (QW, Dl))
        pair = lax.dynamic_slice(columns, (2 * DI + q * 2 * PH, 0), (2 * PH, Dl))
        step = lax.dynamic_slice(columns, (2 * DI + NP + group * HG, 0), (HG, Dl))
        step = jnp.pad(step, ((0, 8 - HG), (0, 0)))
        return jnp.concatenate([inner[:HA], pair[:PH], inner[HA:], pair[PH:], step], axis=0)

    def later_rows_for(place):
        group = c * F + place
        gate_part = lax.dynamic_slice(columns, (group * GW + q * QW, 0), (QW, Dl))
        out_part = lax.dynamic_slice(out_weight, (group * GW + q * QW, 0), (QW, Dl))
        return jnp.concatenate([gate_part, out_part], axis=0)

    def line_rows(pick):
        return [pick(f)] + [from_line(pick(lax.rem(f + k, F)), k) for k in range(1, F)]

    first_rows = line_rows(rows_for)
    rows_a = jnp.stack([value[: HA + PH] for value in first_rows])
    rows_b = jnp.stack([value[HA + PH :] for value in first_rows])
    if F == 4:
        beside_a, beside_b = from_part(rows_a, 1), from_part(rows_b, 2)
        pieces_a = [rows_a, beside_a, from_part(rows_a, 2), from_part(beside_a, 2)]
        pieces_b = [rows_b, from_part(rows_b, 1), beside_b, from_part(beside_b, 1)]
    else:
        pieces_a, pieces_b = gather_parts(rows_a, bits), gather_parts(rows_b, bits)
    pieces_a, pieces_b = in_order(pieces_a), in_order(pieces_b)

    later = line_rows(later_rows_for)
    later = jnp.stack(later)
    cot_rel = [from_line(cotangent, k) for k in range(1, F)]

    conv_x = jnp.concatenate([chan[: KW + 1], jnp.zeros((7 - KW, GW), f32)], axis=0)
    conv_p = jnp.concatenate(
        [conv_pair_weight, conv_pair_bias[None], jnp.zeros((7 - KW, NP), f32)], axis=0
    )
    heads = jnp.pad(jnp.stack([bias_h, rate_h]), ((0, 6), (0, 128 - HG)))
    wide_rows = jnp.concatenate(
        [
            chan[KW + 1][None],
            jnp.repeat(skip_h, P_SIZE)[None],
            jnp.full((1, GW), 1.0 / DI, f32),
            jnp.zeros((5, GW), f32),
        ],
        axis=0,
    )
    weight_pieces = [piece for pair in zip(pieces_a, pieces_b, strict=True) for piece in pair]
    (
        x_group, in_rows, pair_in, rawx, rawp, actx, actp, slopex, slopep, dt, cum, cumt,
        step_in, local, total, final,
    ) = call(
        functools.partial(project_kernel, absolute, QW),
        blocks,
        [rows_half(D), rows_half(D), fixed(16, D), fixed(16, D)]
        + [fixed(F, HA + PH, Dl), fixed(F, QW - HA + PH + 8, Dl)] * F
        + [fixed(8, GW), fixed(8, NP), fixed(8, 128)],
        [
            rows_of(D), fixed(GW + 8, D), fixed(NP, D),
            rows_of(GW), rows_of(NP), rows_of(GW), rows_of(NP), rows_of(GW),
            rows_of(NP), rows_of(8), rows_of(8), across, rows_of(8), per_block(N, GW),
            per_block(8, GW), fixed(N + 8, GW),
        ],
        [
            struct((TL, D), bf16), struct((GW + 8, D), bf16), struct((NP, D), bf16),
            struct((TL, GW), bf16), struct((TL, NP), bf16),
            struct((TL, GW), bf16), struct((TL, NP), bf16), struct((TL, GW), bf16),
            struct((TL, NP), bf16), struct((TL, 8), f32), struct((TL, 8), f32),
            struct((8, TL), f32), struct((TL, 8), f32), struct((blocks, N, GW), f32),
            struct((blocks, 8, GW), f32), struct((N + 8, GW), f32),
        ],
        [
            pltpu.VMEM((N, GW), f32), pltpu.VMEM((8, GW), f32),
            pltpu.VMEM((Q + 8, GW), f32), pltpu.VMEM((Q + 8, NP), f32),
        ],
    )(spot, x_line, x_other, edge_own, edge_twin, *weight_pieces, conv_x, conv_p, heads)

    finals = [from_part(final, k) for k in range(1, F)]
    later_pieces = in_order([later] + [from_part(later, k) for k in range(1, F)])
    *cot_rel, final_low = lax.optimization_barrier((*cot_rel, final[:8]))
    cot_line = line_ordered([cotangent] + cot_rel)
    cot_other = twin(cot_line)
    y_intra = call(
        intra_kernel,
        blocks,
        [rows_of(GW), rows_of(NP), rows_of(8), rows_of(8), across],
        rows_of(GW),
        struct((TL, GW), f32),
    )(spot, actx, actp, dt, cum, cumt)
    cot_group, gate_rows, out_rows, gate, back_normed = call(
        functools.partial(cotangent_kernel, absolute),
        blocks,
        [rows_half(D), rows_half(D), rows_of(D)] + [fixed(F, 2 * QW, Dl)] * F,
        [rows_of(D), fixed(GW, D), fixed(GW, D), rows_of(GW), rows_of(GW)],
        [
            struct((TL, D), bf16), struct((GW, D), bf16), struct((GW, D), bf16),
            struct((TL, GW), bf16), struct((TL, GW), bf16),
        ],
    )(spot, cot_line, cot_other, x_group, *later_pieces)
    y_inter, states, sums = call(
        inter_kernel,
        blocks,
        [
            rows_of(GW), rows_of(NP), rows_of(8), per_block(8, GW), per_block(N, GW),
            rows_of(GW), rows_of(GW), rows_of(GW), fixed(8, GW),
        ]
        + [fixed(N + 8, GW)] * (F - 1),
        [rows_of(GW), per_block(N, GW), across],
        [struct((TL, GW), f32), struct((blocks, N, GW), bf16), struct((8, TL), f32)],
        [pltpu.VMEM((8, GW), f32), pltpu.VMEM((N, GW), f32)],
    )(spot, actx, actp, cum, total, local, y_intra, gate, back_normed, wide_rows, *finals)

    sums = sums + twin(sums)
    sums = [sums] + [from_line(sums, k) for k in range(1, F)]
    gated_normed, back_gate, dy, local_back, first_back, small_sums, away, mine = call(
        gate_kernel,
        blocks,
        [
            rows_back(GW), rows_back(NP), rows_back(8), per_block_back(8, GW), rows_back(GW),
            rows_back(GW), rows_back(GW), rows_back(GW), fixed(8, GW),
        ]
        + [across_back] * F
        + [fixed(GW, D)],
        [
            rows_back(GW), rows_back(GW), rows_back(GW), per_block_back(N, GW), fixed(N, GW),
            fixed(8, GW), half_of_back(D, 0), half_of_back(D, 1),
        ],
        [
            struct((TL, GW), bf16), struct((TL, GW), bf16), struct((TL, GW), bf16),
            struct((blocks, N, GW), f32), struct((N, GW), f32), struct((8, GW), f32),
            struct((TL // 2, D), bf16), struct((TL // 2, D), bf16),
        ],
        [pltpu.VMEM((N, GW), f32)],
    )(
        spot, actx, actp, cum, total, y_intra, y_inter, gate, back_normed, wide_rows, *sums,
        out_rows,
    )
    skip_part = jnp.sum(small_sums[1].reshape(HG, P_SIZE), axis=1)
    firsts = [from_part(first_back, k) for k in range(1, F)]

    def by_line(arrays):
        rows, width = arrays[0].shape[1:]
        block = pl.BlockSpec((1, rows, width), lambda i, p: (lax.rem(p[2] + i, F), 0, 0))
        sums = call(
            functools.partial(sum_kernel, F),
            F,
            [block] * len(arrays),
            [fixed(rows, width)] * F,
            [struct((rows, width), bf16)] * F,
        )(spot, *arrays)
        return [sums[0]] + [from_line(sums[k], k) for k in range(1, F)]

    def add_group(away, mine):
        shape = (F, tokens, mine.shape[1])
        pieces = by_line([mine.reshape(shape), twin(away).reshape(shape)])
        return sum(piece.astype(f32) for piece in pieces)

    def partial_sums(lefts, rights, step):
        pairs = len(lefts)
        rows = pairs * QW + (0 if step is None else 8)
        extra = [] if step is None else [step]
        if Dl % 128 == 0:
            columns_of = pl.BlockSpec((TL, Dl), lambda i, p: (0, i))
            return call(
                functools.partial(partial_blocks_kernel, F, pairs),
                F,
                [fixed(TL, GW)] * pairs + [columns_of] * pairs + [fixed(TL, 8)] * len(extra),
                [pl.BlockSpec((1, rows, Dl), lambda i, p: (i, 0, 0))] * F,
                [struct((F, rows, Dl), bf16)] * F,
                [pltpu.VMEM((pairs, GW, TL), bf16), pltpu.VMEM((GW, Dl), f32)],
            )(spot, *lefts, *rights, *extra)
        return call(
            functools.partial(partial_kernel, F, pairs),
            blocks,
            [rows_of(GW)] * pairs + [rows_of(D)] * pairs + [rows_of(8)] * len(extra),
            [fixed(F, rows, Dl)] * F,
            [struct((F, rows, Dl), bf16)] * F,
            [pltpu.VMEM((GW, D), f32)] * pairs + [pltpu.VMEM((8, D), f32)] * len(extra),
        )(spot, *lefts, *rights, *extra)

    def share(pieces):
        piece = jnp.stack(pieces)
        mine = [piece] + [from_part(piece, k) for k in range(1, F)]
        return mine + [twin(jnp.stack(mine))]

    block_out = (hidden + add_group(away, mine)).astype(bf16)

    early = partial_sums([gated_normed, back_gate], [cot_group, x_group], None)
    early = [early[0]] + [from_part(early[k], k) for k in range(1, F)]
    early = share(by_line(early))

    du_intra, dbc = call(
        back_intra_kernel,
        blocks,
        [
            rows_of(GW), rows_of(NP), rows_of(8), rows_of(8), across, rows_of(GW),
            per_block(N, GW),
        ],
        [rows_of(GW), rows_of(NP)],
        [struct((TL, GW), f32), struct((TL, NP), f32)],
    )(spot, actx, actp, dt, cum, cumt, dy, states)

    dprex, dprep, back_step, head_sums, edge_back = call(
        back_inter_kernel,
        blocks,
        [
            rows_of(GW), rows_of(NP), rows_of(GW), rows_of(NP), rows_of(8), rows_of(8),
            rows_of(8), per_block(8, GW), fixed(8, GW), per_block(N, GW), per_block(N, GW),
            rows_of(GW), rows_of(GW), rows_of(GW), rows_of(GW), rows_of(NP), fixed(8, 128),
            fixed(8, GW),
        ]
        + [fixed(N + 8, GW)] * (F - 1)
        + [fixed(N, GW)] * (F - 1),
        [rows_of(GW), rows_of(NP), rows_of(8), fixed(8, 8), fixed(8, GW + NP)],
        [
            struct((TL, GW), f32), struct((TL, NP), f32), struct((TL, 8), f32),
            struct((8, 8), f32), struct((8, GW + NP), f32),
        ],
        [pltpu.VMEM((8, GW), f32), pltpu.VMEM((N, GW), f32)],
    )(
        spot, actx, actp, slopex, slopep, dt, cum, step_in, total, final[N:], local_back,
        states, dy, y_intra, y_inter, du_intra, dbc, heads, wide_rows, *finals, *firsts,
    )
    halo_back = lax.ppermute(edge_back, "seq", back)

    def following(width):
        return pl.BlockSpec(
            (8, width), lambda i, p: (jnp.minimum((i + 1) * (Q // 8), TL // 8 - 1), 0)
        )

    (
        back_inner, pair_away, pair_mine, conv_x_part, conv_p_part, away, mine, gain_rows,
    ) = call(
        back_conv_kernel,
        blocks,
        [
            rows_of(GW), rows_of(NP), following(GW), following(NP), fixed(8, GW + NP),
            rows_of(GW), rows_of(NP), fixed(8, GW), fixed(8, NP), rows_of(GW), rows_of(8),
            rows_of(D), fixed(GW, D), fixed(GW + 8, D),
        ],
        [
            rows_of(GW), half_of(NP, 0), half_of(NP, 1), fixed(8, GW), fixed(8, NP),
            half_of(D, 0), half_of(D, 1), fixed(8, D),
        ],
        [
            struct((TL, GW), bf16), struct((TL // 2, NP), bf16), struct((TL // 2, NP), bf16),
            struct((8, GW), f32), struct((8, NP), f32), struct((TL // 2, D), bf16),
            struct((TL // 2, D), bf16), struct((8, D), f32),
        ],
        [pltpu.VMEM((Q + 8, GW), f32), pltpu.VMEM((Q + 8, NP), f32)],
    )(
        spot, dprex, dprep, dprex, dprep, halo_back, rawx, rawp, conv_x, conv_p, back_gate,
        back_step, x_group, gate_rows, in_rows,
    )

    late = partial_sums([back_inner], [x_group], back_step)
    late = [late[0]] + [from_part(late[k], k) for k in range(1, F)]
    pair_own = add_group(pair_away, pair_mine).astype(bf16)
    back_in = add_group(away, mine)
    late = share(by_line(late))

    rest_rel = [pair_own] + [from_line(pair_own, k) for k in range(1, F)]
    rest_line = []
    for j in range(F):
        here = pair_own
        for k in range(1, F):
            here = jnp.where(lax.rem(f - k + F, F) == j, rest_rel[k], here)
        rest_line.append(here)
    rest_line = jnp.stack(rest_line)
    rest_other = twin(rest_line)
    rest = jnp.concatenate(
        [jnp.where(c == 0, rest_line, rest_other), jnp.where(c == 0, rest_other, rest_line)],
        axis=0,
    )
    pair_all = rest.reshape(TL, NP)
    x_rows = lax.dynamic_slice(x_group, (0, f * Dl), (TL, Dl))
    grad_rest = dot_f32(pair_all, x_rows, ((0,), (0,)))
    for bit in bits:
        grad_rest = grad_rest.astype(bf16)
        grad_rest = grad_rest.astype(f32) + from_part(grad_rest, bit).astype(f32)

    pair_again = lax.optimization_barrier(pair_own)
    back_pair_in = dot_f32(pair_own, pair_in, ((1,), (0,)))
    gain_part = gain_rows[0] + jnp.sum(
        dot_f32(pair_again, pair_in, ((1,), (0,))) * normed.astype(f32), axis=0
    )
    gain_part = lax.optimization_barrier(gain_part / norm_gain)
    per_channel = jnp.concatenate([conv_x_part[: KW + 1], small_sums[:1]], axis=0)
    per_channel = jnp.transpose(per_channel.reshape(KW + 2, HG, F, PF), (2, 0, 1, 3))
    per_channel = jnp.pad(
        per_channel.reshape(F, KW + 2, HG * PF), ((0, 0), (0, 0), (0, 128 - HG * PF))
    )
    per_head = jnp.concatenate([head_sums[0, :HG], head_sums[1, :HG], skip_part])
    per_head = jnp.broadcast_to(jnp.pad(per_head, (0, 128 - 3 * HG))[None, None], (F, 1, 128))
    slots = jnp.concatenate([per_channel, per_head, jnp.zeros((F, 1, 128), f32)], axis=1)
    shared = jnp.concatenate([conv_p_part[: KW + 1].reshape(-1), gain_part])
    count = shared.shape[0]
    lines = -(-count // 1024) * 8
    shared = jnp.pad(shared, (0, lines * 128 - count)).reshape(lines, 128)
    shared = shared + twin(shared)
    small = jnp.concatenate([slots.reshape(F * 8, 128), shared], axis=0)
    for bit in bits:
        small = small + from_part(small, bit)
    slots, shared = small[: F * 8].reshape(F, 8, 128), small[F * 8 :]
    for bit in bits:
        shared = shared + lax.ppermute(shared, "fsdp", [(i, i ^ bit) for i in range(F)])
    owners = [
        ((qq * R + cc) * F + ff, (cc * F + ff) * F + qq)
        for qq in range(F)
        for cc in range(R)
        for ff in range(F)
    ]
    mine_small = lax.ppermute(take(slots, q), everyone, owners)
    shared = shared.reshape(-1)
    pair_grads = shared[: (KW + 1) * NP].reshape(KW + 1, NP)
    gain_sum = shared[(KW + 1) * NP : count]
    channel_grads = mine_small[: KW + 2, : HG * PF].reshape(KW + 2, HG, PF)
    head_grads = mine_small[KW + 2]

    back_in = back_in + back_pair_in
    scaled_back = back_in * norm_gain[None, :]
    inverse_cubed = inverse_scale * inverse_scale * inverse_scale
    grad_input = (
        cotangent.astype(f32)
        + inverse_scale * scaled_back
        - hidden * inverse_cubed * jnp.mean(scaled_back * hidden, axis=1, keepdims=True)
    ).astype(bf16)

    E = in_weight.shape[1]
    grad_in_weight = call(
        functools.partial(late_grads_kernel, F, QW, HG),
        S + -(-(E - 2 * DI) // GW),
        [fixed(F, QW + 8, Dl)] * F + [fixed(F, F, QW + 8, Dl)],
        pl.BlockSpec((GW, Dl), lambda i, p: (S + i, 0)),
        struct((E, Dl), f32),
    )(spot, *late)
    grad_in_weight, grad_out_weight = call(
        functools.partial(early_grads_kernel, F),
        S,
        [fixed(F, 2 * QW, Dl)] * F + [fixed(F, F, 2 * QW, Dl), anywhere],
        [pl.BlockSpec((GW, Dl), lambda i, p: (i, 0))] * 2,
        [struct((E, Dl), f32), struct((DI, Dl), f32)],
        aliases={F + 2: 0},
    )(spot, *early, grad_in_weight)
    grad_in_weight = call(
        pair_grads_kernel,
        1,
        [fixed(NP, Dl), anywhere],
        pl.BlockSpec((NP, Dl), lambda i, p: (2 * DI // NP, 0)),
        struct((E, Dl), f32),
        aliases={2: 0},
    )(spot, grad_rest, grad_in_weight)
    grad_in_weight = jnp.transpose(grad_in_weight)
    return (
        block_out,
        grad_input,
        gain_sum,
        grad_in_weight,
        channel_grads[:KW],
        channel_grads[KW],
        pair_grads[:KW],
        pair_grads[KW],
        head_grads[:HG],
        head_grads[HG : 2 * HG],
        head_grads[2 * HG : 3 * HG],
        channel_grads[KW + 1],
        grad_out_weight,
    )


def solution(mesh):
    in_specs = (
        P(("seq", "fsdp"), None),
        P(),
        P("fsdp", None),
        P(None, "seq", "fsdp"),
        P("seq", "fsdp"),
        P(),
        P(),
        P("seq"),
        P("seq"),
        P("seq"),
        P("seq", "fsdp"),
        P(None, "fsdp"),
        P(("seq", "fsdp"), None),
    )
    out_specs = (
        P(("seq", "fsdp"), None),
        P(("seq", "fsdp"), None),
        P(),
        P("fsdp", None),
        P(None, "seq", "fsdp"),
        P("seq", "fsdp"),
        P(),
        P(),
        P("seq"),
        P("seq"),
        P("seq"),
        P("seq", "fsdp"),
        P(None, "fsdp"),
    )

    return jax.shard_map(body, mesh=mesh, in_specs=in_specs, out_specs=out_specs, check_vma=False)
```

```python
import functools

import jax
import jax.numpy as jnp
from jax import lax
from jax.experimental import pallas as pl
from jax.experimental.pallas import tpu as pltpu
from jax.sharding import PartitionSpec as P


H = 48
P_SIZE = 64
N = 128
KW = 4
Q = 256

norm_epsilon = 1e-05
far_below = -1e30
highest = lax.Precision.HIGHEST
f32 = jnp.float32
bf16 = jnp.bfloat16
everyone = ("seq", "fsdp")


def spread(value, axis, count):
    copies = jnp.broadcast_to(value[None], (count,) + value.shape)
    return lax.all_to_all(copies, axis, 0, 0, tiled=True)


def mm(left, right, dims, precision=None):
    return lax.dot_general(
        left, right, (dims, ((), ())), preferred_element_type=f32, precision=precision
    )


def split3(value):
    first = value.astype(bf16)
    rest = value - first.astype(f32)
    second = rest.astype(bf16)
    return first, second, (rest - second.astype(f32)).astype(bf16)


def mm_ones(ones, value, dims, flip=False):
    ones = ones.astype(bf16)
    parts = [
        mm(part, ones, dims) if flip else mm(ones, part, dims) for part in reversed(split3(value))
    ]
    return sum(parts[1:], parts[0])


def lanes_of(width):
    return [(at, min(2 * P_SIZE, width - at)) for at in range(0, width, 2 * P_SIZE)]


def widen(per_head, width):
    rows = per_head.shape[0]
    out = []
    for at, wide in lanes_of(width):
        h = at // P_SIZE
        first = jnp.broadcast_to(per_head[:, h : h + 1], (rows, wide))
        if wide > P_SIZE:
            second = jnp.broadcast_to(per_head[:, h + 1 : h + 2], (rows, wide))
            lane = lax.broadcasted_iota(jnp.int32, (rows, wide), 1)
            first = jnp.where(lane < P_SIZE, first, second)
        out.append(first)
    return out[0] if len(out) == 1 else jnp.concatenate(out, axis=1)


def pick_heads(width):
    row = lax.broadcasted_iota(jnp.int32, (width, 8), 0)
    col = lax.broadcasted_iota(jnp.int32, (width, 8), 1)
    return ((row >= col * P_SIZE) & (row < (col + 1) * P_SIZE)).astype(f32)


def lower_ones(strict=False):
    row = lax.broadcasted_iota(jnp.int32, (Q, Q), 0)
    col = lax.broadcasted_iota(jnp.int32, (Q, Q), 1)
    return (row > col) if strict else (row >= col)


def upper_ones():
    row = lax.broadcasted_iota(jnp.int32, (Q, Q), 0)
    col = lax.broadcasted_iota(jnp.int32, (Q, Q), 1)
    return row <= col


def split_heads(value):
    if value.shape[1] == P_SIZE:
        return [value]
    lane = lax.broadcasted_iota(jnp.int32, value.shape, 1)
    zero = jnp.zeros_like(value)
    return [jnp.where(lane < P_SIZE, value, zero), jnp.where(lane < P_SIZE, zero, value)]


def soft_plus(value):
    small = jnp.exp(-jnp.abs(value))
    series = small * (1.0 - small * (0.5 - small * (1.0 / 3.0 - 0.25 * small)))
    return jnp.maximum(value, 0.0) + jnp.where(small < 0.01, series, jnp.log(1.0 + small))


def choose_half(spot_ref, mine_ref, other_ref, out_ref):
    half = pl.program_id(0) // (pl.num_programs(0) // 2)
    mine = half == spot_ref[1]

    @pl.when(mine)
    def _():
        out_ref[...] = mine_ref[...]

    @pl.when(jnp.logical_not(mine))
    def _():
        out_ref[...] = other_ref[...]


def to_halves(spot_ref, block, value, away_ref, mine_ref):
    mine = (block // (pl.num_programs(0) // 2)) == spot_ref[1]

    @pl.when(mine)
    def _():
        mine_ref[...] = value

    @pl.when(jnp.logical_not(mine))
    def _():
        away_ref[...] = value


def params_kernel(
    places, width, spot_ref, small_ref, pair_ref, convx_ref, convp_ref, heads_ref, rows_ref
):
    GW = convx_ref.shape[1]
    heads = GW // P_SIZE
    lane = lax.broadcasted_iota(jnp.int32, (128, GW), 0)
    chan = lax.broadcasted_iota(jnp.int32, (128, GW), 1)
    inside = chan % P_SIZE
    total = jnp.zeros((8, GW), f32)
    for place in range(places):
        hot = (inside // width == place) & (
            lane == (chan // P_SIZE) * width + inside % width
        )
        total = total + mm_ones(hot.astype(f32), small_ref[place], ((1,), (0,)), True)
    row = lax.broadcasted_iota(jnp.int32, (8, GW), 0)
    convx_ref[...] = jnp.where(row <= KW, total, 0.0)
    convp_ref[...] = pair_ref[...]
    line = small_ref[0, KW + 2 : KW + 3]
    at = lax.broadcasted_iota(jnp.int32, (128, 128), 0)
    to = lax.broadcasted_iota(jnp.int32, (128, 128), 1)

    def shifted(start):
        hot = (at == to + start) & (to < heads)
        return mm_ones(hot.astype(f32), jnp.broadcast_to(line, (8, 128)), ((1,), (0,)), True)

    used = lax.broadcasted_iota(jnp.int32, (8, 128), 1) < heads
    rate = jnp.where(used, jnp.exp(shifted(heads)), 0.0)
    down = lax.broadcasted_iota(jnp.int32, (8, 128), 0)
    heads_ref[...] = jnp.where(down == 0, shifted(0), jnp.where(down == 1, rate, 0.0))
    skip = widen(shifted(2 * heads)[:, 0:8], GW)
    gain = jnp.broadcast_to(total[KW + 1 : KW + 2], (8, GW))
    share = jnp.full((8, GW), 1.0 / (H * P_SIZE), f32)
    rows_ref[...] = jnp.where(
        row == 0, gain, jnp.where(row == 1, skip, jnp.where(row == 2, share, 0.0))
    )


def pack_kernel(
    places, width, spot_ref, convx_ref, sums_ref, heads_ref, convp_ref, gain_ref, norm_ref, out_ref
):
    GW = convx_ref.shape[1]
    heads = GW // P_SIZE
    row = lax.broadcasted_iota(jnp.int32, (8, GW), 0)
    gate = jnp.broadcast_to(sums_ref[0:1], (8, GW))
    value = jnp.where(row <= KW, convx_ref[...], jnp.where(row == KW + 1, gate, 0.0))
    lane = lax.broadcasted_iota(jnp.int32, (GW, 128), 1)
    chan = lax.broadcasted_iota(jnp.int32, (GW, 128), 0)
    inside = chan % P_SIZE
    at = lax.broadcasted_iota(jnp.int32, (8, 128), 0)
    to = lax.broadcasted_iota(jnp.int32, (8, 128), 1)
    line = mm_ones(((to == at) & (at < heads)).astype(f32), heads_ref[...], ((1,), (0,)), True)
    both = line[0:1]
    line = mm_ones(
        ((to == at + heads) & (at < heads)).astype(f32), heads_ref[...], ((1,), (0,)), True
    )
    both = both + line[1:2]
    skip = (lane == 2 * heads + chan // P_SIZE).astype(f32)
    both = both + mm_ones(skip, sums_ref[...], ((1,), (0,)), True)[1:2]
    down = lax.broadcasted_iota(jnp.int32, (8, 128), 0)
    both = jnp.where(down == KW + 2, jnp.broadcast_to(both, (8, 128)), 0.0)
    for place in range(places):
        hot = (inside // width == place) & (
            lane == (chan // P_SIZE) * width + inside % width
        )
        out_ref[place * 8 : place * 8 + 8] = (
            mm_ones(hot.astype(f32), value, ((1,), (0,)), True) + both
        )
    at = places * 8
    out_ref[at : at + 8] = convp_ref[:, 0:128]
    out_ref[at + 8 : at + 16] = convp_ref[:, 128:256]
    out_ref[at + 16 :] = jnp.zeros((out_ref.shape[0] - at - 16, 128), f32)
    gain = gain_ref[0:1] / norm_ref[...]
    for j in range(gain_ref.shape[1] // 128):
        out_ref[at + 16 + j : at + 17 + j] = gain[:, j * 128 : (j + 1) * 128]


def project_kernel(
    absolute, QW, spot_ref, mine_ref, other_ref, halo0_ref, halo1_ref, *refs
):
    count = (len(refs) - 23) // 2
    pieces = refs[: 2 * count]
    (
        cwx_ref, cwp_ref, heads_ref,
        x_ref, win_ref, wpair_ref, rawx_ref, rawp_ref, actx_ref, actp_ref, slopex_ref,
        slopep_ref, dt_ref, cum_ref, cumt_ref, stepin_ref, local_ref, total_ref, final_ref,
        state, whole, extx, extp,
    ) = refs[2 * count :]
    b = pl.program_id(0)
    GW = rawx_ref.shape[1]
    PH = N // count
    Dl = win_ref.shape[1] // count
    HA = pieces[0].shape[1] - PH

    @pl.when(b == 0)
    def _():
        def place(ref, at, rows, value):
            if absolute:
                ref[at : at + rows.stop - rows.start, cols] = value[far, rows]
            else:
                at = pl.multiple_of(at, 16)
                ref[pl.ds(at, rows.stop - rows.start), cols] = value[far, rows]

        for k in range(count):
            first, second = pieces[2 * k], pieces[2 * k + 1]
            here = k if absolute else spot_ref[0] ^ k
            for src in range(count):
                cols = slice(src * Dl, (src + 1) * Dl)
                far = lax.rem(spot_ref[2] - src + count, count)
                place(win_ref, here * QW, slice(0, HA), first)
                place(wpair_ref, here * 2 * PH, slice(HA, HA + PH), first)
                if HA < QW:
                    place(win_ref, here * QW + HA, slice(0, QW - HA), second)
                place(
                    wpair_ref, here * 2 * PH + PH, slice(QW - HA, QW - HA + PH), second
                )
                if k == 0:
                    win_ref[GW : GW + 8, cols] = second[far, QW - HA + PH : QW - HA + PH + 8]
        state[...] = jnp.zeros_like(state)
        whole[...] = jnp.zeros_like(whole)
        edge = halo0_ref[...] + halo1_ref[...]
        ex = mm(edge, win_ref[0:GW], ((1,), (1,))).astype(bf16).astype(f32)
        ep = mm(edge, wpair_ref[...], ((1,), (1,))).astype(bf16).astype(f32)
        extx[0:8] = ex[8:16]
        extp[0:8] = ep[8:16]

    @pl.when(b > 0)
    def _():
        extx[0:8] = extx[Q : Q + 8]
        extp[0:8] = extp[Q : Q + 8]

    choose_half(spot_ref, mine_ref, other_ref, x_ref)
    x = x_ref[...]
    rx = mm(x, win_ref[0:GW], ((1,), (1,))).astype(bf16)
    rp = mm(x, wpair_ref[...], ((1,), (1,))).astype(bf16)
    st = mm(x, win_ref[GW : GW + 8], ((1,), (1,))).astype(bf16).astype(f32)
    rawx_ref[...] = rx
    rawp_ref[...] = rp
    extx[8 : Q + 8] = rx.astype(f32)
    extp[8 : Q + 8] = rp.astype(f32)

    def conv(ext, cw, act_out, slope_out):
        pre = cw[KW : KW + 1, :]
        for k in range(KW):
            pre = pre + cw[k : k + 1, :] * ext[9 - KW + k : 9 - KW + k + Q]
        sig = jax.nn.sigmoid(pre)
        act_out[...] = (pre * sig).astype(bf16)
        slope_out[...] = (sig * (1.0 + pre * (1.0 - sig))).astype(bf16)

    conv(extx, cwx_ref, actx_ref, slopex_ref)
    conv(extp, cwp_ref, actp_ref, slopep_ref)
    step_in = st + heads_ref[0:1, 0:8]
    dt = soft_plus(step_in)
    ld = -dt * heads_ref[1:2, 0:8]
    cum = mm_ones(lower_ones().astype(f32), ld, ((1,), (0,)))
    dt_ref[...] = dt
    cum_ref[...] = cum
    stepin_ref[...] = step_in
    eye = (
        lax.broadcasted_iota(jnp.int32, (8, 8), 0) == lax.broadcasted_iota(jnp.int32, (8, 8), 1)
    ).astype(f32)
    cumt_ref[...] = mm(eye, cum, ((1,), (1,)), highest)
    total = cum[Q - 1 : Q]
    total_wide = widen(total, GW)
    total_ref[0] = jnp.broadcast_to(total_wide, (8, GW))
    u32 = actx_ref[...].astype(f32) * widen(dt, GW)
    uw = (u32 * widen(jnp.exp(total - cum), GW)).astype(bf16)
    local_ref[0] = state[...]
    state[...] = state[...] * jnp.exp(total_wide) + mm(actp_ref[:, 0:N], uw, ((0,), (0,)))
    whole[...] = whole[...] + total_wide

    @pl.when(b == pl.num_programs(0) - 1)
    def _():
        final_ref[0:N] = state[...]
        final_ref[N : N + 8] = whole[...]


def intra_kernel(spot_ref, actx_ref, actp_ref, dt_ref, cum_ref, cumt_ref, y_ref):
    GW = y_ref.shape[1]
    scores = mm(actp_ref[:, N : 2 * N], actp_ref[:, 0:N], ((1,), (1,)))
    causal = lower_ones()
    for at, wide in lanes_of(GW):
        u = (
            actx_ref[:, at : at + wide].astype(f32)
            * widen(dt_ref[...], GW)[:, at : at + wide]
        ).astype(bf16)
        mixes = []
        for h in range(at // P_SIZE, (at + wide) // P_SIZE):
            gap = cum_ref[:, h : h + 1] - cumt_ref[h : h + 1, :]
            mixes.append((scores * jnp.exp(jnp.where(causal, gap, far_below))).astype(bf16))
        y_ref[:, at : at + wide] = sum(
            mm(m, p, ((1,), (0,))) for m, p in zip(mixes, split_heads(u), strict=True)
        )


def merge_states(spot_ref, states, totals, forward):
    q = spot_ref[0]
    out = jnp.zeros(states[0].shape, f32)
    count = len(states) + 1
    for k in range(1, count):
        p = q ^ k
        between = jnp.zeros(totals[0].shape, f32)
        for j in range(1, count):
            if j != k:
                o = q ^ j
                inside = ((o > p) & (o < q)) if forward else ((o < p) & (o > q))
                between = between + totals[j - 1] * inside.astype(f32)
        reaches = (p < q) if forward else (p > q)
        out = out + states[k - 1] * (jnp.exp(between) * reaches.astype(f32))
    return out


def inter_kernel(
    spot_ref, actx_ref, actp_ref, cum_ref, total_ref, local_ref, y_ref, z_ref, bn_ref, rows_ref,
    *refs,
):
    finals = refs[:-5]
    yx_ref, states_ref, sums_ref, prefix, before_ref = refs[-5:]
    GW = y_ref.shape[1]

    @pl.when(pl.program_id(0) == 0)
    def _():
        prefix[...] = jnp.zeros_like(prefix)
        before_ref[...] = merge_states(
            spot_ref, [r[0:N] for r in finals], [r[N : N + 1] for r in finals], True
        )

    low = (local_ref[0] + jnp.exp(prefix[0:1]) * before_ref[...]).astype(bf16)
    prefix[...] = prefix[...] + total_ref[0]
    states_ref[0] = low
    yx = mm(actp_ref[:, N : 2 * N], low, ((1,), (0,))) * widen(jnp.exp(cum_ref[...]), GW)
    yx_ref[...] = yx
    mixer = y_ref[...] + yx + rows_ref[1:2] * actx_ref[...].astype(f32)
    z = z_ref[...].astype(f32)
    gated = mixer * (z * jax.nn.sigmoid(z))
    row = lax.broadcasted_iota(jnp.int32, (8, GW), 0)
    squares = mm_ones((row == 0).astype(f32), gated * gated, ((1,), (1,)))
    cross = mm_ones(
        (row == 1).astype(f32), bn_ref[...].astype(f32) * rows_ref[0:1] * gated, ((1,), (1,))
    )
    sums_ref[...] = squares + cross


def gate_kernel(
    spot_ref, actx_ref, actp_ref, cum_ref, total_ref, y_ref, yx_ref, z_ref, bn_ref, rows_ref, *refs
):
    sums = sum(r[...] for r in refs[:-10])
    out_rows_ref, gn_ref, bgate_ref, dy_ref, local_ref, first_ref, small_ref = refs[-10:-3]
    away_ref, mine_ref, state = refs[-3:]
    GW = y_ref.shape[1]
    b = pl.program_id(0)

    @pl.when(b == 0)
    def _():
        state[...] = jnp.zeros_like(state)
        small_ref[...] = jnp.zeros_like(small_ref)

    eye = (
        lax.broadcasted_iota(jnp.int32, (8, 8), 0) == lax.broadcasted_iota(jnp.int32, (8, 8), 1)
    ).astype(f32)
    cols = mm(sums, eye, ((0,), (0,)), highest)
    scale = lax.rsqrt(cols[:, 0:1] * rows_ref[2:3, 0:1] + norm_epsilon)
    cross = cols[:, 1:2] * scale * scale * scale * rows_ref[2:3, 0:1]
    x = actx_ref[...].astype(f32)
    mixer = y_ref[...] + yx_ref[...] + rows_ref[1:2] * x
    z = z_ref[...].astype(f32)
    sig = jax.nn.sigmoid(z)
    silu = z * sig
    gated = mixer * silu
    bn = bn_ref[...].astype(f32)
    gain = rows_ref[0:1]
    gn = (gated * scale * gain).astype(bf16)
    gn_ref[...] = gn
    to_halves(
        spot_ref,
        pl.num_programs(0) - 1 - b,
        mm(gn, out_rows_ref[...], ((1,), (0,))).astype(bf16),
        away_ref,
        mine_ref,
    )
    back_gated = scale * (bn * gain) - gated * cross
    dy = (back_gated * silu).astype(bf16)
    dy_ref[...] = dy
    bgate_ref[...] = (back_gated * mixer * sig * (1.0 + z * (1.0 - sig))).astype(bf16)
    dyf = dy.astype(f32)
    small_ref[0:1] += jnp.sum(bn * gated * scale, axis=0, keepdims=True)
    small_ref[1:2] += jnp.sum(dyf * x, axis=0, keepdims=True)
    dyh = (dyf * widen(jnp.exp(cum_ref[...]), GW)).astype(bf16)
    local_ref[0] = state[...]
    state[...] = state[...] * jnp.exp(total_ref[0, 0:1]) + mm(
        actp_ref[:, N : 2 * N], dyh, ((0,), (0,))
    )

    @pl.when(b == pl.num_programs(0) - 1)
    def _():
        first_ref[...] = state[...]


def back_intra_kernel(
    spot_ref, actx_ref, actp_ref, dt_ref, cum_ref, cumt_ref, dy_ref, states_ref,
    du_ref, dbc_ref,
):
    GW = dy_ref.shape[1]
    bs = actp_ref[:, 0:N]
    cs = actp_ref[:, N : 2 * N]
    scores = mm(cs, bs, ((1,), (1,)))
    causal = lower_ones()
    dscores = jnp.zeros((Q, Q), f32)
    dt_wide = widen(dt_ref[...], GW)
    for at, wide in lanes_of(GW):
        u = (actx_ref[:, at : at + wide].astype(f32) * dt_wide[:, at : at + wide]).astype(bf16)
        du = jnp.zeros((Q, wide), f32)
        for k, dyk in enumerate(split_heads(dy_ref[:, at : at + wide])):
            h = at // P_SIZE + k
            gap = cum_ref[:, h : h + 1] - cumt_ref[h : h + 1, :]
            decay = jnp.exp(jnp.where(causal, gap, far_below))
            mix = (scores * decay).astype(bf16)
            dscores = dscores + mm(dyk, u, ((1,), (1,))) * decay
            du = du + mm(mix, dyk, ((0,), (0,)))
        du_ref[:, at : at + wide] = du
    dlow = dscores.astype(bf16)
    dyh = (dy_ref[...].astype(f32) * widen(jnp.exp(cum_ref[...]), GW)).astype(bf16)
    dbc_ref[:, 0:N] = mm(dlow, cs, ((0,), (0,)))
    dbc_ref[:, N : 2 * N] = mm(dlow, bs, ((1,), (0,))) + mm(dyh, states_ref[0], ((1,), (1,)))


def back_inter_kernel(
    spot_ref, actx_ref, actp_ref, slopex_ref, slopep_ref, dt_ref, cum_ref, stepin_ref, total_ref, whole_ref,
    local_ref, states_ref, dy_ref, y_ref, yx_ref, du_ref, dbc_ref, heads_ref, rows_ref, *refs,
):
    others, refs = refs[:-7], refs[-7:]
    dprex_ref, dprep_ref, dstep_ref, hsum_ref, edge_ref, seen, after_ref = refs
    finals, firsts = others[: len(others) // 2], others[len(others) // 2 :]
    GW = dy_ref.shape[1]
    b = pl.program_id(0)

    @pl.when(b == 0)
    def _():
        seen[...] = jnp.zeros_like(seen)
        hsum_ref[...] = jnp.zeros_like(hsum_ref)
        after_ref[...] = merge_states(
            spot_ref, [r[...] for r in firsts], [r[N : N + 1] for r in finals], False
        )

    seen[...] = seen[...] + total_ref[0]
    left = jnp.exp(whole_ref[0:1] - seen[0:1])
    grown = local_ref[0] + left * after_ref[...]
    low = grown.astype(bf16)
    cum = cum_ref[...]
    total = cum[Q - 1 : Q]
    dt = dt_ref[...]
    dt_wide = widen(dt, GW)
    tail = widen(jnp.exp(total - cum), GW)
    x = actx_ref[...].astype(f32)
    u32 = x * dt_wide
    ub = u32.astype(bf16).astype(f32)
    uw = (u32 * tail).astype(bf16)
    bs = actp_ref[:, 0:N]
    du_inter = mm(bs, low, ((1,), (0,))) * tail
    dui = du_ref[...]
    du = dui + du_inter
    dy = dy_ref[...].astype(f32)
    dprex_ref[...] = (du * dt_wide + rows_ref[1:2] * dy) * slopex_ref[...].astype(f32)
    db = dbc_ref[:, 0:N] + mm(uw, low, ((1,), (1,)))
    dprep_ref[:, 0:N] = db * slopep_ref[:, 0:N].astype(f32)
    dprep_ref[:, N : 2 * N] = dbc_ref[:, N : 2 * N] * slopep_ref[:, N : 2 * N].astype(f32)

    @pl.when(b == 0)
    def _():
        edge_ref[:, 0:GW] = dprex_ref[0:8]
        edge_ref[:, GW:] = dprep_ref[0:8]

    sel = pick_heads(GW)
    ddt = mm_ones(sel, x * du, ((1,), (0,)), True)
    later = mm_ones(sel, dy * (y_ref[...] + yx_ref[...]) - ub * dui, ((1,), (0,)), True)
    earlier = mm_ones(sel, u32 * du_inter, ((1,), (0,)), True)
    over = jnp.sum(grown * states_ref[0].astype(f32), axis=0, keepdims=True)
    over = mm(jnp.broadcast_to(over, (8, GW)), sel, ((1,), (0,)), highest)[0:1] * jnp.exp(total)
    dld = (
        mm_ones(upper_ones().astype(f32), later, ((1,), (0,)))
        + mm_ones(lower_ones(True).astype(f32), earlier, ((1,), (0,)))
        + over
    )
    rate = heads_ref[1:2, 0:8]
    dstep = (ddt - rate * dld) * jax.nn.sigmoid(stepin_ref[...])
    dstep_ref[...] = dstep
    hsum_ref[0:1] += jnp.sum(dstep, axis=0, keepdims=True)
    hsum_ref[1:2] += jnp.sum(-dld * dt * rate, axis=0, keepdims=True)


def back_conv_kernel(
    spot_ref, dprex_ref, dprep_ref, nextx_ref, nextp_ref, halo_ref, rawx_ref, rawp_ref,
    cwx_ref, cwp_ref, bgate_ref, step_ref, x_ref, wgate_ref, win_ref, wpair_ref,
    backx_ref, backp_ref, gradx_ref, gradp_ref, away_ref, mine_ref, gain_ref,
    extx, extp,
):
    b = pl.program_id(0)
    last = b == pl.num_programs(0) - 1

    @pl.when(b == 0)
    def _():
        gradx_ref[...] = jnp.zeros_like(gradx_ref)
        gradp_ref[...] = jnp.zeros_like(gradp_ref)
        gain_ref[...] = jnp.zeros_like(gain_ref)

    def conv(dpre, following, halo, raw, cw, ext, grad):
        ext[0:Q] = dpre[...]
        ext[Q : Q + 8] = jnp.where(last, halo, following[...])
        value = raw[...].astype(f32)
        total = jnp.zeros(dpre.shape, f32)
        for k in range(KW):
            shifted = ext[KW - 1 - k : KW - 1 - k + Q]
            total = total + cw[k : k + 1, :] * shifted
            grad[k : k + 1] += jnp.sum(value * shifted, axis=0, keepdims=True)
        grad[KW : KW + 1] += jnp.sum(dpre[...], axis=0, keepdims=True)
        return total.astype(bf16)

    GW = dprex_ref.shape[1]
    inner = conv(dprex_ref, nextx_ref, halo_ref[:, 0:GW], rawx_ref, cwx_ref, extx, gradx_ref)
    backx_ref[...] = inner
    pair = conv(dprep_ref, nextp_ref, halo_ref[:, GW:], rawp_ref, cwp_ref, extp, gradp_ref)
    backp_ref[...] = pair
    value = mm(bgate_ref[...], wgate_ref[...], ((1,), (0,)))
    value = value + mm(step_ref[...].astype(bf16), win_ref[GW : GW + 8], ((1,), (0,)))
    value = value + mm(inner, win_ref[0:GW], ((1,), (0,)))
    value = value + mm(pair, wpair_ref[...], ((1,), (0,)))
    gain_ref[0:1] += jnp.sum(value * x_ref[...].astype(f32), axis=0, keepdims=True)
    to_halves(spot_ref, b, value.astype(bf16), away_ref, mine_ref)


def cotangent_kernel(absolute, spot_ref, mine_ref, other_ref, x_ref, *refs):
    pieces = refs[:-5]
    cot_ref, gate_rows_ref, rows_ref, z_ref, bn_ref = refs[-5:]
    count = len(pieces)
    QW = rows_ref.shape[0] // count
    Dl = rows_ref.shape[1] // count

    @pl.when(pl.program_id(0) == 0)
    def _():
        for k, piece in enumerate(pieces):
            for src in range(count):
                cols = slice(src * Dl, (src + 1) * Dl)
                far = lax.rem(spot_ref[2] - src + count, count)
                if absolute:
                    gate_rows_ref[k * QW : (k + 1) * QW, cols] = piece[far, 0:QW]
                    rows_ref[k * QW : (k + 1) * QW, cols] = piece[far, QW : 2 * QW]
                else:
                    at = pl.multiple_of((spot_ref[0] ^ k) * QW, 16)
                    gate_rows_ref[pl.ds(at, QW), cols] = piece[far, 0:QW]
                    rows_ref[pl.ds(at, QW), cols] = piece[far, QW : 2 * QW]

    choose_half(spot_ref, mine_ref, other_ref, cot_ref)
    z_ref[...] = mm(x_ref[...], gate_rows_ref[...], ((1,), (1,))).astype(bf16)
    bn_ref[...] = mm(cot_ref[...], rows_ref[...], ((1,), (1,))).astype(bf16)


def partial_blocks_kernel(count, pairs, spot_ref, *refs):
    lefts, rights = refs[:pairs], refs[pairs : 2 * pairs]
    step_ref, pair_ref = refs[2:4] if pairs == 1 else (None, None)
    held = 4 if pairs == 1 else 2
    outs, turned, total = refs[-count - held : -held], refs[-held], refs[1 - held]
    GW = total.shape[0]
    QW = GW // count

    @pl.when(pl.program_id(0) == 0)
    def _():
        for at in range(pairs):
            turned[at] = lefts[at][...].T
        if pair_ref is not None:
            refs[-2][...] = pair_ref[...].T

    for at in range(pairs):
        right = rights[at][...]
        total[...] = mm(turned[at], right, ((1,), (0,)))
        for k in range(count):
            start = pl.multiple_of((spot_ref[0] ^ k) * QW, 8)
            outs[k][0, at * QW : (at + 1) * QW] = total[pl.ds(start, QW)].astype(bf16)
    if step_ref is not None:
        value = mm(step_ref[...].astype(bf16), rights[0][...], ((0,), (0,)))
        for k in range(count):
            keep = ((spot_ref[0] ^ k) == 0).astype(f32)
            outs[k][0, QW : QW + 8] = (value * keep).astype(bf16)
        refs[-1][...] = mm(refs[-2][...], rights[0][...], ((1,), (0,)))
        PW = refs[-1].shape[0] // count
        for k in range(count):
            start = pl.multiple_of((spot_ref[0] ^ k) * PW, 8)
            outs[k][0, QW + 8 : QW + 8 + PW] = refs[-1][pl.ds(start, PW)].astype(bf16)


def partial_kernel(count, pairs, spot_ref, *refs):
    lefts, rights = refs[:pairs], refs[pairs : 2 * pairs]
    step_ref, pair_ref = refs[2:4] if pairs == 1 else (None, None)
    held = 3 if pairs == 1 else pairs
    outs, sums = refs[len(refs) - count - held : len(refs) - held], refs[len(refs) - held :]
    b = pl.program_id(0)
    lefts = [r[...] for r in lefts]
    rights = [r[...] for r in rights]
    if step_ref is not None:
        lefts.extend([step_ref[...].astype(bf16), pair_ref[...]])
        rights.extend([rights[0], rights[0]])
    for left, right, total in zip(lefts, rights, sums, strict=True):
        value = mm(left, right, ((0,), (0,)))

        @pl.when(b == 0)
        def _(value=value, total=total):
            total[...] = value

        @pl.when(b > 0)
        def _(value=value, total=total):
            total[...] += value

    @pl.when(b == pl.num_programs(0) - 1)
    def _():
        GW, D = sums[0].shape
        QW, Dl = GW // count, D // count
        for k in range(count):
            part = spot_ref[0] ^ k
            start = pl.multiple_of(part * QW, 8)
            for j in range(count):
                cols = slice(j * Dl, (j + 1) * Dl)
                for at in range(pairs):
                    outs[k][j, at * QW : (at + 1) * QW] = sums[at][pl.ds(start, QW), cols].astype(
                        bf16
                    )
                if step_ref is not None:
                    keep = (part == 0).astype(f32)
                    outs[k][j, QW : QW + 8] = (sums[1][:, cols] * keep).astype(bf16)
                    PW = sums[2].shape[0] // count
                    at = pl.multiple_of(part * PW, 8)
                    outs[k][j, QW + 8 : QW + 8 + PW] = sums[2][pl.ds(at, PW), cols].astype(bf16)


def sum_kernel(outs_count, spot_ref, *refs):
    i = pl.program_id(0)
    outs = refs[len(refs) - outs_count :]
    total = sum(r[0].astype(f32) for r in refs[: len(refs) - outs_count]).astype(bf16)
    for k, out in enumerate(outs):

        @pl.when(i == k)
        def _(out=out):
            out[...] = total


def place_rows(count, spot_ref, step, own, other, rows, out_ref):
    q, c, f = spot_ref[0], spot_ref[1], spot_ref[2]
    far = lax.rem(f - lax.rem(step, count) + count, count)
    width = rows.stop - rows.start
    for side in range(2):
        owner = c if side == 0 else 1 - c

        @pl.when((step >= owner * count) & (step < (owner + 1) * count))
        def _(side=side):
            for k in range(count):
                value = own[k][far, rows] if side == 0 else other[k, far, rows]
                out_ref[pl.ds(pl.multiple_of((q ^ k) * width, 8), width)] = value.astype(f32)


def early_grads_kernel(count, spot_ref, *refs):
    own, other, in_ref, out_ref = refs[:count], refs[count], refs[-2], refs[-1]
    QW = own[0].shape[1] // 2
    step = pl.program_id(0)
    place_rows(count, spot_ref, step, own, other, slice(0, QW), out_ref)
    place_rows(count, spot_ref, step, own, other, slice(QW, 2 * QW), in_ref)


def late_grads_kernel(count, QW, heads, spot_ref, *refs):
    own, other, in_ref = refs[:count], refs[count], refs[-1]
    step = pl.program_id(0)
    place_rows(count, spot_ref, step, own, other, slice(0, QW), in_ref)
    q, c, f = spot_ref[0], spot_ref[1], spot_ref[2]
    GW = in_ref.shape[0]
    groups = 2 * count
    for block in range(-(-(2 * N + H) // GW)):

        @pl.when(step == groups + block)
        def _(block=block):
            first = block * GW
            PW = 2 * N // count
            base = QW + 8
            for k in range(count):
                total = sum(
                    own[k][g, base : base + PW].astype(f32)
                    + other[k, g, base : base + PW].astype(f32)
                    for g in range(count)
                )
                start = (q ^ k) * PW - first

                @pl.when((start >= 0) & (start < GW))
                def _(total=total, start=start):
                    in_ref[pl.ds(pl.multiple_of(start, 8), PW)] = total


                @pl.when((q ^ k) == 0)
                def _(k=k):
                    for g in range(groups):
                        at = 2 * N + g * heads - first
                        if at < 0 or at >= GW:
                            continue
                        far = lax.rem(f - g % count + count, count)
                        mine = own[k][far, QW : QW + 8].astype(f32)
                        theirs = other[k, far, QW : QW + 8].astype(f32)
                        value = jnp.where(c == g // count, mine, theirs)
                        in_ref[at : at + heads] = value[0:heads]


def body(
    block_in,
    norm_gain,
    in_weight,
    conv_inner_weight,
    conv_inner_bias,
    conv_pair_weight,
    conv_pair_bias,
    step_bias,
    decay_log,
    skip_gain,
    gate_gain,
    out_weight,
    cotangent,
):
    S = lax.axis_size("seq")
    F = lax.axis_size("fsdp")
    devices = S * F
    R = S // F
    s = lax.axis_index("seq")
    f = lax.axis_index("fsdp")
    q = s // R
    c = s % R
    member = c * F + f
    spot = jnp.stack([q, c, f]).astype(jnp.int32)
    tokens, D = block_in.shape
    TL = tokens * S
    blocks = TL // Q
    half = blocks // 2
    HG = H // S
    GW = HG * P_SIZE
    QW = GW // F
    DI = H * P_SIZE
    Dl = in_weight.shape[0]
    PF = P_SIZE // F
    NP = 2 * N
    PH = N // F
    absolute = QW % 16 != 0 or PH % 16 != 0
    twins = [(i, i ^ 1) for i in range(S)]
    back = [(i + R, i) for i in range(S - R)]
    bits = [1 << i for i in range(F.bit_length() - 1)]
    struct = jax.ShapeDtypeStruct

    def twin(value):
        return lax.ppermute(value, "seq", twins)

    def from_part(value, k):
        return lax.ppermute(value, "seq", [(i, i ^ (k * R)) for i in range(S)])

    def from_line(value, k):
        return lax.ppermute(value, "fsdp", [(i, (i + k) % F) for i in range(F)])

    def take(value, at, axis=0):
        return lax.dynamic_index_in_dim(value, at, axis, keepdims=False)

    def line_chain(value):
        up, down, ups, downs = value, value, [], []
        for k in range(1, F):
            up = lax.ppermute(up, "fsdp", [(i, i + 1) for i in range(k - 1, F - 1)])
            down = lax.ppermute(down, "fsdp", [(i, i - 1) for i in range(1, F - k + 1)])
            ups.append(up)
            downs.append(down)
        line = []
        for j in range(F):
            here = value
            for k in range(1, F):
                if j + k < F:
                    here = jnp.where(f == j + k, ups[k - 1], here)
                if j - k >= 0:
                    here = jnp.where(f == j - k, downs[k - 1], here)
            line.append(here)
        return jnp.concatenate(line, axis=0)

    def line_ordered(rel):
        line = []
        for j in range(F):
            here = rel[0]
            for k in range(1, F):
                here = jnp.where(lax.rem(f - k + F, F) == j, rel[k], here)
            line.append(here)
        return jnp.concatenate(line, axis=0)

    def gather_parts(value, order):
        pieces = {0: value}
        for bit in order:
            pieces.update({k ^ bit: from_part(v, bit) for k, v in list(pieces.items())})
        return [pieces[k] for k in range(F)]

    def in_order(pieces):
        if not absolute:
            return pieces
        out = []
        for j in range(F):
            here = pieces[0]
            for k in range(1, F):
                here = jnp.where(q == (j ^ k), pieces[k], here)
            out.append(here)
        return out

    def rows_of(width, shift=0):
        return pl.BlockSpec((Q, width), lambda i, p: (i + shift, 0))

    def rows_back(width):
        return pl.BlockSpec((Q, width), lambda i, p: (blocks - 1 - i, 0))

    def rows_half(width):
        return pl.BlockSpec((Q, width), lambda i, p: (lax.rem(i, half), 0))

    def fixed(*shape):
        return pl.BlockSpec(shape, lambda i, p: (0,) * len(shape))

    def per_block(rows, width, shift=0):
        return pl.BlockSpec((1, rows, width), lambda i, p: (i + shift, 0, 0))

    def per_block_back(rows, width):
        return pl.BlockSpec((1, rows, width), lambda i, p: (blocks - 1 - i, 0, 0))

    def half_of(width, own):
        def index(i, p):
            return (
                jnp.where(p[1] == own, jnp.maximum(i - half, 0), jnp.minimum(i, half - 1)), 0
            )

        return pl.BlockSpec((Q, width), index)

    def half_of_back(width, own):
        def index(i, p):
            at = blocks - 1 - i
            return (
                jnp.where(p[1] == own, jnp.maximum(at - half, 0), jnp.minimum(at, half - 1)), 0
            )

        return pl.BlockSpec((Q, width), index)

    across = pl.BlockSpec((8, Q), lambda i, p: (0, i))
    across_back = pl.BlockSpec((8, Q), lambda i, p: (0, blocks - 1 - i))
    anywhere = pl.BlockSpec(memory_space=pl.ANY)

    def call(kernel, steps, in_specs, out_specs, out_shape, scratch=(), aliases=None):
        return pl.pallas_call(
            kernel,
            grid_spec=pltpu.PrefetchScalarGridSpec(
                num_scalar_prefetch=1,
                grid=(steps,),
                in_specs=in_specs,
                out_specs=out_specs,
                scratch_shapes=list(scratch),
            ),
            out_shape=out_shape,
            input_output_aliases=aliases or {},
            compiler_params=pltpu.CompilerParams(dimension_semantics=("arbitrary",)),
        )

    small = jnp.concatenate(
        [
            conv_inner_weight.reshape(KW, HG * PF),
            conv_inner_bias.reshape(1, HG * PF),
            gate_gain.reshape(1, HG * PF),
        ],
        axis=0,
    )
    small = jnp.pad(small, ((0, 0), (0, 128 - HG * PF)))
    heads_row = jnp.concatenate([step_bias, decay_log, skip_gain])
    heads_row = jnp.pad(heads_row, (0, 128 - 3 * HG))[None]
    small = jnp.concatenate([small, heads_row, jnp.zeros((1, 128), f32)], axis=0)
    small_all = spread(small, everyone, devices)
    small_here = lax.dynamic_slice(small_all, (member * F, 0, 0), (F, 8, 128))
    hidden = block_in.astype(f32)
    inverse_scale = lax.rsqrt(jnp.mean(hidden * hidden, axis=1, keepdims=True) + norm_epsilon)
    normed = (hidden * inverse_scale * norm_gain[None, :]).astype(bf16)
    x_line = line_chain(normed)
    x_other = twin(x_line)
    last_rows = x_line[F * tokens - 16 :]
    edge_own = lax.ppermute(last_rows, "seq", [(i, i + R) for i in range(S - R) if i % R == R - 1])
    edge_twin = lax.ppermute(last_rows, "seq", [(i, i + 1) for i in range(S - R) if i % R == R - 1])

    columns = jnp.transpose(in_weight)
    HA = QW // 2 if QW % 32 == 0 else QW

    def rows_for(place):
        group = c * F + place
        inner = lax.dynamic_slice(columns, (DI + group * GW + q * QW, 0), (QW, Dl))
        pair = lax.dynamic_slice(columns, (2 * DI + q * 2 * PH, 0), (2 * PH, Dl))
        step = lax.dynamic_slice(columns, (2 * DI + NP + group * HG, 0), (HG, Dl))
        step = jnp.pad(step, ((0, 8 - HG), (0, 0)))
        return jnp.concatenate([inner[:HA], pair[:PH], inner[HA:], pair[PH:], step], axis=0)

    def later_rows_for(place):
        group = c * F + place
        gate_part = lax.dynamic_slice(columns, (group * GW + q * QW, 0), (QW, Dl))
        out_part = lax.dynamic_slice(out_weight, (group * GW + q * QW, 0), (QW, Dl))
        return jnp.concatenate([gate_part, out_part], axis=0)

    def line_rows(pick):
        return [pick(f)] + [from_line(pick(lax.rem(f + k, F)), k) for k in range(1, F)]

    first_rows = line_rows(rows_for)
    rows_a = jnp.stack([value[: HA + PH] for value in first_rows])
    rows_b = jnp.stack([value[HA + PH :] for value in first_rows])
    if F == 4:
        beside_a, beside_b = from_part(rows_a, 1), from_part(rows_b, 2)
        pieces_a = [rows_a, beside_a, from_part(rows_a, 2), from_part(beside_a, 2)]
        pieces_b = [rows_b, from_part(rows_b, 1), beside_b, from_part(beside_b, 1)]
    else:
        pieces_a, pieces_b = gather_parts(rows_a, bits), gather_parts(rows_b, bits)
    pieces_a, pieces_b = in_order(pieces_a), in_order(pieces_b)

    later = line_rows(later_rows_for)
    later = jnp.stack(later)
    cot_rel = [from_line(cotangent, k) for k in range(1, F)]

    pair_params = jnp.concatenate(
        [conv_pair_weight, conv_pair_bias[None], jnp.zeros((7 - KW, NP), f32)], axis=0
    )
    conv_x, conv_p, heads, wide_rows = call(
        functools.partial(params_kernel, F, PF),
        1,
        [fixed(F, 8, 128), fixed(8, NP)],
        [fixed(8, GW), fixed(8, NP), fixed(8, 128), fixed(8, GW)],
        [
            struct((8, GW), f32), struct((8, NP), f32), struct((8, 128), f32),
            struct((8, GW), f32),
        ],
    )(spot, small_here, pair_params)
    weight_pieces = [piece for pair in zip(pieces_a, pieces_b, strict=True) for piece in pair]
    (
        x_group, in_rows, pair_in, rawx, rawp, actx, actp, slopex, slopep, dt, cum, cumt,
        step_in, local, total, final,
    ) = call(
        functools.partial(project_kernel, absolute, QW),
        blocks,
        [rows_half(D), rows_half(D), fixed(16, D), fixed(16, D)]
        + [fixed(F, HA + PH, Dl), fixed(F, QW - HA + PH + 8, Dl)] * F
        + [fixed(8, GW), fixed(8, NP), fixed(8, 128)],
        [
            rows_of(D), fixed(GW + 8, D), fixed(NP, D),
            rows_of(GW), rows_of(NP), rows_of(GW), rows_of(NP), rows_of(GW),
            rows_of(NP), rows_of(8), rows_of(8), across, rows_of(8), per_block(N, GW),
            per_block(8, GW), fixed(N + 8, GW),
        ],
        [
            struct((TL, D), bf16), struct((GW + 8, D), bf16), struct((NP, D), bf16),
            struct((TL, GW), bf16), struct((TL, NP), bf16),
            struct((TL, GW), bf16), struct((TL, NP), bf16), struct((TL, GW), bf16),
            struct((TL, NP), bf16), struct((TL, 8), f32), struct((TL, 8), f32),
            struct((8, TL), f32), struct((TL, 8), f32), struct((blocks, N, GW), f32),
            struct((blocks, 8, GW), f32), struct((N + 8, GW), f32),
        ],
        [
            pltpu.VMEM((N, GW), f32), pltpu.VMEM((8, GW), f32),
            pltpu.VMEM((Q + 8, GW), f32), pltpu.VMEM((Q + 8, NP), f32),
        ],
    )(spot, x_line, x_other, edge_own, edge_twin, *weight_pieces, conv_x, conv_p, heads)

    finals = [from_part(final, k) for k in range(1, F)]
    later_pieces = in_order([later] + [from_part(later, k) for k in range(1, F)])
    *cot_rel, final_low = lax.optimization_barrier((*cot_rel, final[:8]))
    cot_line = line_ordered([cotangent] + cot_rel)
    cot_other = twin(cot_line)
    y_intra = call(
        intra_kernel,
        blocks,
        [rows_of(GW), rows_of(NP), rows_of(8), rows_of(8), across],
        rows_of(GW),
        struct((TL, GW), f32),
    )(spot, actx, actp, dt, cum, cumt)
    cot_group, gate_rows, out_rows, gate, back_normed = call(
        functools.partial(cotangent_kernel, absolute),
        blocks,
        [rows_half(D), rows_half(D), rows_of(D)] + [fixed(F, 2 * QW, Dl)] * F,
        [rows_of(D), fixed(GW, D), fixed(GW, D), rows_of(GW), rows_of(GW)],
        [
            struct((TL, D), bf16), struct((GW, D), bf16), struct((GW, D), bf16),
            struct((TL, GW), bf16), struct((TL, GW), bf16),
        ],
    )(spot, cot_line, cot_other, x_group, *later_pieces)
    y_inter, states, sums = call(
        inter_kernel,
        blocks,
        [
            rows_of(GW), rows_of(NP), rows_of(8), per_block(8, GW), per_block(N, GW),
            rows_of(GW), rows_of(GW), rows_of(GW), fixed(8, GW),
        ]
        + [fixed(N + 8, GW)] * (F - 1),
        [rows_of(GW), per_block(N, GW), across],
        [struct((TL, GW), f32), struct((blocks, N, GW), bf16), struct((8, TL), f32)],
        [pltpu.VMEM((8, GW), f32), pltpu.VMEM((N, GW), f32)],
    )(spot, actx, actp, cum, total, local, y_intra, gate, back_normed, wide_rows, *finals)

    sums = sums + twin(sums)
    sums = [sums] + [from_line(sums, k) for k in range(1, F)]
    gated_normed, back_gate, dy, local_back, first_back, small_sums, away, mine = call(
        gate_kernel,
        blocks,
        [
            rows_back(GW), rows_back(NP), rows_back(8), per_block_back(8, GW), rows_back(GW),
            rows_back(GW), rows_back(GW), rows_back(GW), fixed(8, GW),
        ]
        + [across_back] * F
        + [fixed(GW, D)],
        [
            rows_back(GW), rows_back(GW), rows_back(GW), per_block_back(N, GW), fixed(N, GW),
            fixed(8, GW), half_of_back(D, 0), half_of_back(D, 1),
        ],
        [
            struct((TL, GW), bf16), struct((TL, GW), bf16), struct((TL, GW), bf16),
            struct((blocks, N, GW), f32), struct((N, GW), f32), struct((8, GW), f32),
            struct((TL // 2, D), bf16), struct((TL // 2, D), bf16),
        ],
        [pltpu.VMEM((N, GW), f32)],
    )(
        spot, actx, actp, cum, total, y_intra, y_inter, gate, back_normed, wide_rows, *sums,
        out_rows,
    )
    firsts = [from_part(first_back, k) for k in range(1, F)]

    def by_line(arrays):
        rows, width = arrays[0].shape[1:]
        block = pl.BlockSpec((1, rows, width), lambda i, p: (lax.rem(p[2] + i, F), 0, 0))
        sums = call(
            functools.partial(sum_kernel, F),
            F,
            [block] * len(arrays),
            [fixed(rows, width)] * F,
            [struct((rows, width), bf16)] * F,
        )(spot, *arrays)
        return [sums[0]] + [from_line(sums[k], k) for k in range(1, F)]

    def add_group(away, mine):
        shape = (F, tokens, mine.shape[1])
        pieces = by_line([mine.reshape(shape), twin(away).reshape(shape)])
        return sum(piece.astype(f32) for piece in pieces)

    def partial_sums(lefts, rights, extra):
        pairs = len(lefts)
        rows = pairs * QW + (8 + 2 * PH if extra else 0)
        if Dl % 128 == 0:
            columns_of = pl.BlockSpec((TL, Dl), lambda i, p: (0, i))
            return call(
                functools.partial(partial_blocks_kernel, F, pairs),
                F,
                [fixed(TL, GW)] * pairs
                + [columns_of] * pairs
                + [fixed(*value.shape) for value in extra],
                [pl.BlockSpec((1, rows, Dl), lambda i, p: (i, 0, 0))] * F,
                [struct((F, rows, Dl), bf16)] * F,
                [pltpu.VMEM((pairs, GW, TL), bf16), pltpu.VMEM((GW, Dl), f32)]
                + [pltpu.VMEM((NP, TL), bf16), pltpu.VMEM((NP, Dl), f32)] * bool(extra),
            )(spot, *lefts, *rights, *extra)
        return call(
            functools.partial(partial_kernel, F, pairs),
            blocks,
            [rows_of(GW)] * pairs
            + [rows_of(D)] * pairs
            + [rows_of(value.shape[1]) for value in extra],
            [fixed(F, rows, Dl)] * F,
            [struct((F, rows, Dl), bf16)] * F,
            [pltpu.VMEM((GW, D), f32)] * pairs
            + [pltpu.VMEM((value.shape[1], D), f32) for value in extra],
        )(spot, *lefts, *rights, *extra)

    def share(pieces):
        piece = jnp.stack(pieces)
        mine = [piece] + [from_part(piece, k) for k in range(1, F)]
        return mine + [twin(jnp.stack(mine))]

    block_out = (hidden + add_group(away, mine)).astype(bf16)

    early = partial_sums([gated_normed, back_gate], [cot_group, x_group], ())
    early = [early[0]] + [from_part(early[k], k) for k in range(1, F)]
    early = share(by_line(early))

    du_intra, dbc = call(
        back_intra_kernel,
        blocks,
        [
            rows_of(GW), rows_of(NP), rows_of(8), rows_of(8), across, rows_of(GW),
            per_block(N, GW),
        ],
        [rows_of(GW), rows_of(NP)],
        [struct((TL, GW), f32), struct((TL, NP), f32)],
    )(spot, actx, actp, dt, cum, cumt, dy, states)

    dprex, dprep, back_step, head_sums, edge_back = call(
        back_inter_kernel,
        blocks,
        [
            rows_of(GW), rows_of(NP), rows_of(GW), rows_of(NP), rows_of(8), rows_of(8),
            rows_of(8), per_block(8, GW), fixed(8, GW), per_block(N, GW), per_block(N, GW),
            rows_of(GW), rows_of(GW), rows_of(GW), rows_of(GW), rows_of(NP), fixed(8, 128),
            fixed(8, GW),
        ]
        + [fixed(N + 8, GW)] * (F - 1)
        + [fixed(N, GW)] * (F - 1),
        [rows_of(GW), rows_of(NP), rows_of(8), fixed(8, 8), fixed(8, GW + NP)],
        [
            struct((TL, GW), f32), struct((TL, NP), f32), struct((TL, 8), f32),
            struct((8, 8), f32), struct((8, GW + NP), f32),
        ],
        [pltpu.VMEM((8, GW), f32), pltpu.VMEM((N, GW), f32)],
    )(
        spot, actx, actp, slopex, slopep, dt, cum, step_in, total, final[N:], local_back,
        states, dy, y_intra, y_inter, du_intra, dbc, heads, wide_rows, *finals, *firsts,
    )
    halo_back = lax.ppermute(edge_back, "seq", back)

    def following(width):
        return pl.BlockSpec(
            (8, width), lambda i, p: (jnp.minimum((i + 1) * (Q // 8), TL // 8 - 1), 0)
        )

    (
        back_inner, back_pair, conv_x_part, conv_p_part, away, mine, gain_rows,
    ) = call(
        back_conv_kernel,
        blocks,
        [
            rows_of(GW), rows_of(NP), following(GW), following(NP), fixed(8, GW + NP),
            rows_of(GW), rows_of(NP), fixed(8, GW), fixed(8, NP), rows_of(GW), rows_of(8),
            rows_of(D), fixed(GW, D), fixed(GW + 8, D), fixed(NP, D),
        ],
        [
            rows_of(GW), rows_of(NP), fixed(8, GW), fixed(8, NP),
            half_of(D, 0), half_of(D, 1), fixed(8, D),
        ],
        [
            struct((TL, GW), bf16), struct((TL, NP), bf16), struct((8, GW), f32), struct((8, NP), f32), struct((TL // 2, D), bf16),
            struct((TL // 2, D), bf16), struct((8, D), f32),
        ],
        [pltpu.VMEM((Q + 8, GW), f32), pltpu.VMEM((Q + 8, NP), f32)],
    )(
        spot, dprex, dprep, dprex, dprep, halo_back, rawx, rawp, conv_x, conv_p, back_gate,
        back_step, x_group, gate_rows, in_rows, pair_in,
    )

    late = partial_sums([back_inner], [x_group], (back_step, back_pair))
    late = [late[0]] + [from_part(late[k], k) for k in range(1, F)]
    back_in = add_group(away, mine)
    late = share(by_line(late))

    rows = F * 8 + 16 + -(-D // 1024) * 8
    small = call(
        functools.partial(pack_kernel, F, PF),
        1,
        [fixed(8, GW), fixed(8, GW), fixed(8, 8), fixed(8, NP), fixed(8, D), fixed(1, D)],
        fixed(rows, 128),
        struct((rows, 128), f32),
    )(spot, conv_x_part, small_sums, head_sums, conv_p_part, gain_rows, norm_gain[None])
    for bit in bits:
        small = small + from_part(small, bit)
    slots, shared = small[: F * 8].reshape(F, 8, 128), small[F * 8 :]
    shared = shared + twin(shared)
    for bit in bits:
        shared = shared + lax.ppermute(shared, "fsdp", [(i, i ^ bit) for i in range(F)])
    owners = [
        ((qq * R + cc) * F + ff, (cc * F + ff) * F + qq)
        for qq in range(F)
        for cc in range(R)
        for ff in range(F)
    ]
    mine_small = lax.ppermute(take(slots, q), everyone, owners)
    pair_grads = jnp.concatenate([shared[:8], shared[8:16]], axis=1)[: KW + 1]
    gain_sum = shared[16:].reshape(-1)[:D]
    channel_grads = mine_small[: KW + 2, : HG * PF].reshape(KW + 2, HG, PF)
    head_grads = mine_small[KW + 2]

    scaled_back = back_in * norm_gain[None, :]
    inverse_cubed = inverse_scale * inverse_scale * inverse_scale
    grad_input = (
        cotangent.astype(f32)
        + inverse_scale * scaled_back
        - hidden * inverse_cubed * jnp.mean(scaled_back * hidden, axis=1, keepdims=True)
    ).astype(bf16)

    E = in_weight.shape[1]
    grad_in_weight, grad_out_weight = call(
        functools.partial(early_grads_kernel, F),
        S,
        [fixed(F, 2 * QW, Dl)] * F + [fixed(F, F, 2 * QW, Dl)],
        [pl.BlockSpec((GW, Dl), lambda i, p: (i, 0))] * 2,
        [struct((E, Dl), f32), struct((DI, Dl), f32)],
    )(spot, *early)
    grad_in_weight = call(
        functools.partial(late_grads_kernel, F, QW, HG),
        S + -(-(E - 2 * DI) // GW),
        [fixed(F, QW + 8 + 2 * PH, Dl)] * F + [fixed(F, F, QW + 8 + 2 * PH, Dl), anywhere],
        pl.BlockSpec((GW, Dl), lambda i, p: (S + i, 0)),
        struct((E, Dl), f32),
        aliases={F + 2: 0},
    )(spot, *late, grad_in_weight)
    grad_in_weight = jnp.transpose(grad_in_weight)
    return (
        block_out,
        grad_input,
        gain_sum,
        grad_in_weight,
        channel_grads[:KW],
        channel_grads[KW],
        pair_grads[:KW],
        pair_grads[KW],
        head_grads[:HG],
        head_grads[HG : 2 * HG],
        head_grads[2 * HG : 3 * HG],
        channel_grads[KW + 1],
        grad_out_weight,
    )


def solution(mesh):
    in_specs = (
        P(("seq", "fsdp"), None),
        P(),
        P("fsdp", None),
        P(None, "seq", "fsdp"),
        P("seq", "fsdp"),
        P(),
        P(),
        P("seq"),
        P("seq"),
        P("seq"),
        P("seq", "fsdp"),
        P(None, "fsdp"),
        P(("seq", "fsdp"), None),
    )
    out_specs = (
        P(("seq", "fsdp"), None),
        P(("seq", "fsdp"), None),
        P(),
        P("fsdp", None),
        P(None, "seq", "fsdp"),
        P("seq", "fsdp"),
        P(),
        P(),
        P("seq"),
        P("seq"),
        P("seq"),
        P("seq", "fsdp"),
        P(None, "fsdp"),
    )

    return jax.shard_map(body, mesh=mesh, in_specs=in_specs, out_specs=out_specs, check_vma=False)
```

```python
import functools

import jax
import jax.numpy as jnp
from jax import lax
from jax.experimental import pallas as pl
from jax.experimental.pallas import tpu as pltpu
from jax.sharding import PartitionSpec as P


H = 48
P_SIZE = 64
N = 128
KW = 4
Q = 256

norm_epsilon = 1e-05
far_below = -1e30
highest = lax.Precision.HIGHEST
f32 = jnp.float32
bf16 = jnp.bfloat16
everyone = ("seq", "fsdp")


def spread(value, axis, count):
    copies = jnp.broadcast_to(value[None], (count,) + value.shape)
    return lax.all_to_all(copies, axis, 0, 0, tiled=True)


def mm(left, right, dims, precision=None):
    return lax.dot_general(
        left, right, (dims, ((), ())), preferred_element_type=f32, precision=precision
    )


def split3(value):
    first = value.astype(bf16)
    rest = value - first.astype(f32)
    second = rest.astype(bf16)
    return first, second, (rest - second.astype(f32)).astype(bf16)


def mm_ones(ones, value, dims, flip=False):
    ones = ones.astype(bf16)
    parts = [
        mm(part, ones, dims) if flip else mm(ones, part, dims) for part in reversed(split3(value))
    ]
    return sum(parts[1:], parts[0])


def lanes_of(width):
    return [(at, min(2 * P_SIZE, width - at)) for at in range(0, width, 2 * P_SIZE)]


def widen(per_head, width):
    rows = per_head.shape[0]
    out = []
    for at, wide in lanes_of(width):
        h = at // P_SIZE
        first = jnp.broadcast_to(per_head[:, h : h + 1], (rows, wide))
        if wide > P_SIZE:
            second = jnp.broadcast_to(per_head[:, h + 1 : h + 2], (rows, wide))
            lane = lax.broadcasted_iota(jnp.int32, (rows, wide), 1)
            first = jnp.where(lane < P_SIZE, first, second)
        out.append(first)
    return out[0] if len(out) == 1 else jnp.concatenate(out, axis=1)


def pick_heads(width):
    row = lax.broadcasted_iota(jnp.int32, (width, 8), 0)
    col = lax.broadcasted_iota(jnp.int32, (width, 8), 1)
    return ((row >= col * P_SIZE) & (row < (col + 1) * P_SIZE)).astype(f32)


def lower_ones(strict=False):
    row = lax.broadcasted_iota(jnp.int32, (Q, Q), 0)
    col = lax.broadcasted_iota(jnp.int32, (Q, Q), 1)
    return (row > col) if strict else (row >= col)


def upper_ones():
    row = lax.broadcasted_iota(jnp.int32, (Q, Q), 0)
    col = lax.broadcasted_iota(jnp.int32, (Q, Q), 1)
    return row <= col


def split_heads(value):
    if value.shape[1] == P_SIZE:
        return [value]
    lane = lax.broadcasted_iota(jnp.int32, value.shape, 1)
    zero = jnp.zeros_like(value)
    return [jnp.where(lane < P_SIZE, value, zero), jnp.where(lane < P_SIZE, zero, value)]


def soft_plus(value):
    small = jnp.exp(-jnp.abs(value))
    series = small * (1.0 - small * (0.5 - small * (1.0 / 3.0 - 0.25 * small)))
    return jnp.maximum(value, 0.0) + jnp.where(small < 0.01, series, jnp.log(1.0 + small))


def choose_half(spot_ref, mine_ref, other_ref, out_ref):
    half = pl.program_id(0) // (pl.num_programs(0) // 2)
    mine = half == spot_ref[1]

    @pl.when(mine)
    def _():
        out_ref[...] = mine_ref[...]

    @pl.when(jnp.logical_not(mine))
    def _():
        out_ref[...] = other_ref[...]


def to_halves(spot_ref, block, value, away_ref, mine_ref):
    mine = (block // (pl.num_programs(0) // 2)) == spot_ref[1]

    @pl.when(mine)
    def _():
        mine_ref[...] = value

    @pl.when(jnp.logical_not(mine))
    def _():
        away_ref[...] = value


def params_kernel(
    places, width, spot_ref, small_ref, pair_ref, convx_ref, convp_ref, heads_ref, rows_ref
):
    GW = convx_ref.shape[1]
    heads = GW // P_SIZE
    lane = lax.broadcasted_iota(jnp.int32, (128, GW), 0)
    chan = lax.broadcasted_iota(jnp.int32, (128, GW), 1)
    inside = chan % P_SIZE
    total = jnp.zeros((8, GW), f32)
    for place in range(places):
        hot = (inside // width == place) & (
            lane == (chan // P_SIZE) * width + inside % width
        )
        total = total + mm_ones(hot.astype(f32), small_ref[place], ((1,), (0,)), True)
    row = lax.broadcasted_iota(jnp.int32, (8, GW), 0)
    convx_ref[...] = jnp.where(row <= KW, total, 0.0)
    convp_ref[...] = pair_ref[...]
    line = small_ref[0, KW + 2 : KW + 3]
    at = lax.broadcasted_iota(jnp.int32, (128, 128), 0)
    to = lax.broadcasted_iota(jnp.int32, (128, 128), 1)

    def shifted(start):
        hot = (at == to + start) & (to < heads)
        return mm_ones(hot.astype(f32), jnp.broadcast_to(line, (8, 128)), ((1,), (0,)), True)

    used = lax.broadcasted_iota(jnp.int32, (8, 128), 1) < heads
    rate = jnp.where(used, jnp.exp(shifted(heads)), 0.0)
    down = lax.broadcasted_iota(jnp.int32, (8, 128), 0)
    heads_ref[...] = jnp.where(down == 0, shifted(0), jnp.where(down == 1, rate, 0.0))
    skip = widen(shifted(2 * heads)[:, 0:8], GW)
    gain = jnp.broadcast_to(total[KW + 1 : KW + 2], (8, GW))
    share = jnp.full((8, GW), 1.0 / (H * P_SIZE), f32)
    rows_ref[...] = jnp.where(
        row == 0, gain, jnp.where(row == 1, skip, jnp.where(row == 2, share, 0.0))
    )


def pack_kernel(
    places, width, spot_ref, convx_ref, sums_ref, heads_ref, convp_ref, gain_ref, norm_ref, out_ref
):
    GW = convx_ref.shape[1]
    heads = GW // P_SIZE
    row = lax.broadcasted_iota(jnp.int32, (8, GW), 0)
    gate = jnp.broadcast_to(sums_ref[0:1], (8, GW))
    value = jnp.where(row <= KW, convx_ref[...], jnp.where(row == KW + 1, gate, 0.0))
    lane = lax.broadcasted_iota(jnp.int32, (GW, 128), 1)
    chan = lax.broadcasted_iota(jnp.int32, (GW, 128), 0)
    inside = chan % P_SIZE
    at = lax.broadcasted_iota(jnp.int32, (8, 128), 0)
    to = lax.broadcasted_iota(jnp.int32, (8, 128), 1)
    line = mm_ones(((to == at) & (at < heads)).astype(f32), heads_ref[...], ((1,), (0,)), True)
    both = line[0:1]
    line = mm_ones(
        ((to == at + heads) & (at < heads)).astype(f32), heads_ref[...], ((1,), (0,)), True
    )
    both = both + line[1:2]
    skip = (lane == 2 * heads + chan // P_SIZE).astype(f32)
    both = both + mm_ones(skip, sums_ref[...], ((1,), (0,)), True)[1:2]
    down = lax.broadcasted_iota(jnp.int32, (8, 128), 0)
    both = jnp.where(down == KW + 2, jnp.broadcast_to(both, (8, 128)), 0.0)
    for place in range(places):
        hot = (inside // width == place) & (
            lane == (chan // P_SIZE) * width + inside % width
        )
        out_ref[place * 8 : place * 8 + 8] = (
            mm_ones(hot.astype(f32), value, ((1,), (0,)), True) + both
        )
    at = places * 8
    out_ref[at : at + 8] = convp_ref[:, 0:128]
    out_ref[at + 8 : at + 16] = convp_ref[:, 128:256]
    out_ref[at + 16 :] = jnp.zeros((out_ref.shape[0] - at - 16, 128), f32)
    gain = gain_ref[0:1] / norm_ref[...]
    for j in range(gain_ref.shape[1] // 128):
        out_ref[at + 16 + j : at + 17 + j] = gain[:, j * 128 : (j + 1) * 128]


def pick_kernel(
    spot_ref, inner_ref, gate_ref, pair_ref, step_ref, out_ref, *refs
):
    count = len(refs) // 2
    i = pl.program_id(0)
    QW, PW = inner_ref.shape[0], pair_ref.shape[0]
    HA, PH = QW // 2, PW // 2
    heads = QW * count // P_SIZE
    group = spot_ref[1] * count + lax.rem(spot_ref[2] + i, count)
    step = step_ref[...]
    down = lax.broadcasted_iota(jnp.int32, step.shape, 0)
    step = jnp.where(down < H, step, jnp.zeros_like(step))
    row = lax.broadcasted_iota(jnp.int32, (8, step.shape[0]), 0)
    col = lax.broadcasted_iota(jnp.int32, (8, step.shape[0]), 1)
    hot = ((col == row + group * heads) & (row < heads)).astype(f32).astype(bf16)
    step = mm(hot, step, ((1,), (0,))).astype(bf16)
    for k in range(count):
        first, later = refs[k], refs[count + k]

        @pl.when(i == k)
        def _(first=first, later=later):
            first[0:HA] = inner_ref[0:HA]
            first[HA : HA + PH] = pair_ref[0:PH]
            first[HA + PH : QW + PH] = inner_ref[HA:QW]
            first[QW + PH : QW + PW] = pair_ref[PH:PW]
            first[QW + PW : QW + PW + 8] = step
            later[0:QW] = gate_ref[...]
            later[QW : 2 * QW] = out_ref[...]


def project_kernel(
    absolute, QW, spot_ref, mine_ref, other_ref, halo0_ref, halo1_ref, *refs
):
    count = (len(refs) - 23) // 2
    pieces = refs[: 2 * count]
    (
        cwx_ref, cwp_ref, heads_ref,
        x_ref, win_ref, wpair_ref, rawx_ref, rawp_ref, actx_ref, actp_ref, slopex_ref,
        slopep_ref, dt_ref, cum_ref, cumt_ref, stepin_ref, local_ref, total_ref, final_ref,
        state, whole, extx, extp,
    ) = refs[2 * count :]
    b = pl.program_id(0)
    GW = rawx_ref.shape[1]
    PH = N // count
    Dl = win_ref.shape[1] // count
    HA = pieces[0].shape[1] - PH

    @pl.when(b == 0)
    def _():
        def place(ref, at, rows, value):
            if absolute:
                ref[at : at + rows.stop - rows.start, cols] = value[far, rows]
            else:
                at = pl.multiple_of(at, 16)
                ref[pl.ds(at, rows.stop - rows.start), cols] = value[far, rows]

        for k in range(count):
            first, second = pieces[2 * k], pieces[2 * k + 1]
            here = k if absolute else spot_ref[0] ^ k
            for src in range(count):
                cols = slice(src * Dl, (src + 1) * Dl)
                far = lax.rem(spot_ref[2] - src + count, count)
                place(win_ref, here * QW, slice(0, HA), first)
                place(wpair_ref, here * 2 * PH, slice(HA, HA + PH), first)
                if HA < QW:
                    place(win_ref, here * QW + HA, slice(0, QW - HA), second)
                place(
                    wpair_ref, here * 2 * PH + PH, slice(QW - HA, QW - HA + PH), second
                )
                if k == 0:
                    win_ref[GW : GW + 8, cols] = second[far, QW - HA + PH : QW - HA + PH + 8]
        state[...] = jnp.zeros_like(state)
        whole[...] = jnp.zeros_like(whole)
        edge = halo0_ref[...] + halo1_ref[...]
        ex = mm(edge, win_ref[0:GW], ((1,), (1,))).astype(bf16).astype(f32)
        ep = mm(edge, wpair_ref[...], ((1,), (1,))).astype(bf16).astype(f32)
        extx[0:8] = ex[8:16]
        extp[0:8] = ep[8:16]

    @pl.when(b > 0)
    def _():
        extx[0:8] = extx[Q : Q + 8]
        extp[0:8] = extp[Q : Q + 8]

    choose_half(spot_ref, mine_ref, other_ref, x_ref)
    x = x_ref[...]
    rx = mm(x, win_ref[0:GW], ((1,), (1,))).astype(bf16)
    rp = mm(x, wpair_ref[...], ((1,), (1,))).astype(bf16)
    st = mm(x, win_ref[GW : GW + 8], ((1,), (1,))).astype(bf16).astype(f32)
    rawx_ref[...] = rx
    rawp_ref[...] = rp
    extx[8 : Q + 8] = rx.astype(f32)
    extp[8 : Q + 8] = rp.astype(f32)

    def conv(ext, cw, act_out, slope_out):
        pre = cw[KW : KW + 1, :]
        for k in range(KW):
            pre = pre + cw[k : k + 1, :] * ext[9 - KW + k : 9 - KW + k + Q]
        sig = jax.nn.sigmoid(pre)
        act_out[...] = (pre * sig).astype(bf16)
        slope_out[...] = (sig * (1.0 + pre * (1.0 - sig))).astype(bf16)

    conv(extx, cwx_ref, actx_ref, slopex_ref)
    conv(extp, cwp_ref, actp_ref, slopep_ref)
    step_in = st + heads_ref[0:1, 0:8]
    dt = soft_plus(step_in)
    ld = -dt * heads_ref[1:2, 0:8]
    cum = mm_ones(lower_ones().astype(f32), ld, ((1,), (0,)))
    dt_ref[...] = dt
    cum_ref[...] = cum
    stepin_ref[...] = step_in
    eye = (
        lax.broadcasted_iota(jnp.int32, (8, 8), 0) == lax.broadcasted_iota(jnp.int32, (8, 8), 1)
    ).astype(f32)
    cumt_ref[...] = mm(eye, cum, ((1,), (1,)), highest)
    total = cum[Q - 1 : Q]
    total_wide = widen(total, GW)
    total_ref[0] = jnp.broadcast_to(total_wide, (8, GW))
    u32 = actx_ref[...].astype(f32) * widen(dt, GW)
    uw = (u32 * widen(jnp.exp(total - cum), GW)).astype(bf16)
    local_ref[0] = state[...]
    state[...] = state[...] * jnp.exp(total_wide) + mm(actp_ref[:, 0:N], uw, ((0,), (0,)))
    whole[...] = whole[...] + total_wide

    @pl.when(b == pl.num_programs(0) - 1)
    def _():
        final_ref[0:N] = state[...]
        final_ref[N : N + 8] = whole[...]


def intra_kernel(spot_ref, actx_ref, actp_ref, dt_ref, cum_ref, cumt_ref, y_ref):
    GW = y_ref.shape[1]
    scores = mm(actp_ref[:, N : 2 * N], actp_ref[:, 0:N], ((1,), (1,)))
    causal = lower_ones()
    for at, wide in lanes_of(GW):
        u = (
            actx_ref[:, at : at + wide].astype(f32)
            * widen(dt_ref[...], GW)[:, at : at + wide]
        ).astype(bf16)
        mixes = []
        for h in range(at // P_SIZE, (at + wide) // P_SIZE):
            gap = cum_ref[:, h : h + 1] - cumt_ref[h : h + 1, :]
            mixes.append((scores * jnp.exp(jnp.where(causal, gap, far_below))).astype(bf16))
        y_ref[:, at : at + wide] = sum(
            mm(m, p, ((1,), (0,))) for m, p in zip(mixes, split_heads(u), strict=True)
        )


def merge_states(spot_ref, states, totals, forward):
    q = spot_ref[0]
    out = jnp.zeros(states[0].shape, f32)
    count = len(states) + 1
    for k in range(1, count):
        p = q ^ k
        between = jnp.zeros(totals[0].shape, f32)
        for j in range(1, count):
            if j != k:
                o = q ^ j
                inside = ((o > p) & (o < q)) if forward else ((o < p) & (o > q))
                between = between + totals[j - 1] * inside.astype(f32)
        reaches = (p < q) if forward else (p > q)
        out = out + states[k - 1] * (jnp.exp(between) * reaches.astype(f32))
    return out


def inter_kernel(
    spot_ref, actx_ref, actp_ref, cum_ref, total_ref, local_ref, y_ref, z_ref, bn_ref, rows_ref,
    *refs,
):
    finals = refs[:-5]
    yx_ref, states_ref, sums_ref, prefix, before_ref = refs[-5:]
    GW = y_ref.shape[1]

    @pl.when(pl.program_id(0) == 0)
    def _():
        prefix[...] = jnp.zeros_like(prefix)
        before_ref[...] = merge_states(
            spot_ref, [r[0:N] for r in finals], [r[N : N + 1] for r in finals], True
        )

    low = (local_ref[0] + jnp.exp(prefix[0:1]) * before_ref[...]).astype(bf16)
    prefix[...] = prefix[...] + total_ref[0]
    states_ref[0] = low
    yx = mm(actp_ref[:, N : 2 * N], low, ((1,), (0,))) * widen(jnp.exp(cum_ref[...]), GW)
    yx_ref[...] = yx
    mixer = y_ref[...] + yx + rows_ref[1:2] * actx_ref[...].astype(f32)
    z = z_ref[...].astype(f32)
    gated = mixer * (z * jax.nn.sigmoid(z))
    row = lax.broadcasted_iota(jnp.int32, (8, GW), 0)
    squares = mm_ones((row == 0).astype(f32), gated * gated, ((1,), (1,)))
    cross = mm_ones(
        (row == 1).astype(f32), bn_ref[...].astype(f32) * rows_ref[0:1] * gated, ((1,), (1,))
    )
    sums_ref[...] = squares + cross


def gate_kernel(
    spot_ref, actx_ref, actp_ref, cum_ref, total_ref, y_ref, yx_ref, z_ref, bn_ref, rows_ref, *refs
):
    sums = sum(r[...] for r in refs[:-10])
    out_rows_ref, gn_ref, bgate_ref, dy_ref, local_ref, first_ref, small_ref = refs[-10:-3]
    away_ref, mine_ref, state = refs[-3:]
    GW = y_ref.shape[1]
    b = pl.program_id(0)

    @pl.when(b == 0)
    def _():
        state[...] = jnp.zeros_like(state)
        small_ref[...] = jnp.zeros_like(small_ref)

    eye = (
        lax.broadcasted_iota(jnp.int32, (8, 8), 0) == lax.broadcasted_iota(jnp.int32, (8, 8), 1)
    ).astype(f32)
    cols = mm(sums, eye, ((0,), (0,)), highest)
    scale = lax.rsqrt(cols[:, 0:1] * rows_ref[2:3, 0:1] + norm_epsilon)
    cross = cols[:, 1:2] * scale * scale * scale * rows_ref[2:3, 0:1]
    x = actx_ref[...].astype(f32)
    mixer = y_ref[...] + yx_ref[...] + rows_ref[1:2] * x
    z = z_ref[...].astype(f32)
    sig = jax.nn.sigmoid(z)
    silu = z * sig
    gated = mixer * silu
    bn = bn_ref[...].astype(f32)
    gain = rows_ref[0:1]
    gn = (gated * scale * gain).astype(bf16)
    gn_ref[...] = gn
    to_halves(
        spot_ref,
        pl.num_programs(0) - 1 - b,
        mm(gn, out_rows_ref[...], ((1,), (0,))).astype(bf16),
        away_ref,
        mine_ref,
    )
    back_gated = scale * (bn * gain) - gated * cross
    dy = (back_gated * silu).astype(bf16)
    dy_ref[...] = dy
    bgate_ref[...] = (back_gated * mixer * sig * (1.0 + z * (1.0 - sig))).astype(bf16)
    dyf = dy.astype(f32)
    small_ref[0:1] += jnp.sum(bn * gated * scale, axis=0, keepdims=True)
    small_ref[1:2] += jnp.sum(dyf * x, axis=0, keepdims=True)
    dyh = (dyf * widen(jnp.exp(cum_ref[...]), GW)).astype(bf16)
    local_ref[0] = state[...]
    state[...] = state[...] * jnp.exp(total_ref[0, 0:1]) + mm(
        actp_ref[:, N : 2 * N], dyh, ((0,), (0,))
    )

    @pl.when(b == pl.num_programs(0) - 1)
    def _():
        first_ref[...] = state[...]


def back_intra_kernel(
    spot_ref, actx_ref, actp_ref, dt_ref, cum_ref, cumt_ref, dy_ref, states_ref,
    du_ref, dbc_ref,
):
    GW = dy_ref.shape[1]
    bs = actp_ref[:, 0:N]
    cs = actp_ref[:, N : 2 * N]
    scores = mm(cs, bs, ((1,), (1,)))
    causal = lower_ones()
    dscores = jnp.zeros((Q, Q), f32)
    dt_wide = widen(dt_ref[...], GW)
    for at, wide in lanes_of(GW):
        u = (actx_ref[:, at : at + wide].astype(f32) * dt_wide[:, at : at + wide]).astype(bf16)
        du = jnp.zeros((Q, wide), f32)
        for k, dyk in enumerate(split_heads(dy_ref[:, at : at + wide])):
            h = at // P_SIZE + k
            gap = cum_ref[:, h : h + 1] - cumt_ref[h : h + 1, :]
            decay = jnp.exp(jnp.where(causal, gap, far_below))
            mix = (scores * decay).astype(bf16)
            dscores = dscores + mm(dyk, u, ((1,), (1,))) * decay
            du = du + mm(mix, dyk, ((0,), (0,)))
        du_ref[:, at : at + wide] = du
    dlow = dscores.astype(bf16)
    dyh = (dy_ref[...].astype(f32) * widen(jnp.exp(cum_ref[...]), GW)).astype(bf16)
    dbc_ref[:, 0:N] = mm(dlow, cs, ((0,), (0,)))
    dbc_ref[:, N : 2 * N] = mm(dlow, bs, ((1,), (0,))) + mm(dyh, states_ref[0], ((1,), (1,)))


def back_inter_kernel(
    spot_ref, actx_ref, actp_ref, slopex_ref, slopep_ref, dt_ref, cum_ref, stepin_ref, total_ref, whole_ref,
    local_ref, states_ref, dy_ref, y_ref, yx_ref, du_ref, dbc_ref, heads_ref, rows_ref, *refs,
):
    others, refs = refs[:-7], refs[-7:]
    dprex_ref, dprep_ref, dstep_ref, hsum_ref, edge_ref, seen, after_ref = refs
    finals, firsts = others[: len(others) // 2], others[len(others) // 2 :]
    GW = dy_ref.shape[1]
    b = pl.program_id(0)

    @pl.when(b == 0)
    def _():
        seen[...] = jnp.zeros_like(seen)
        hsum_ref[...] = jnp.zeros_like(hsum_ref)
        after_ref[...] = merge_states(
            spot_ref, [r[...] for r in firsts], [r[N : N + 1] for r in finals], False
        )

    seen[...] = seen[...] + total_ref[0]
    left = jnp.exp(whole_ref[0:1] - seen[0:1])
    grown = local_ref[0] + left * after_ref[...]
    low = grown.astype(bf16)
    cum = cum_ref[...]
    total = cum[Q - 1 : Q]
    dt = dt_ref[...]
    dt_wide = widen(dt, GW)
    tail = widen(jnp.exp(total - cum), GW)
    x = actx_ref[...].astype(f32)
    u32 = x * dt_wide
    ub = u32.astype(bf16).astype(f32)
    uw = (u32 * tail).astype(bf16)
    bs = actp_ref[:, 0:N]
    du_inter = mm(bs, low, ((1,), (0,))) * tail
    dui = du_ref[...]
    du = dui + du_inter
    dy = dy_ref[...].astype(f32)
    dprex_ref[...] = (du * dt_wide + rows_ref[1:2] * dy) * slopex_ref[...].astype(f32)
    db = dbc_ref[:, 0:N] + mm(uw, low, ((1,), (1,)))
    dprep_ref[:, 0:N] = db * slopep_ref[:, 0:N].astype(f32)
    dprep_ref[:, N : 2 * N] = dbc_ref[:, N : 2 * N] * slopep_ref[:, N : 2 * N].astype(f32)

    @pl.when(b == 0)
    def _():
        edge_ref[:, 0:GW] = dprex_ref[0:8]
        edge_ref[:, GW:] = dprep_ref[0:8]

    sel = pick_heads(GW)
    ddt = mm_ones(sel, x * du, ((1,), (0,)), True)
    later = mm_ones(sel, dy * (y_ref[...] + yx_ref[...]) - ub * dui, ((1,), (0,)), True)
    earlier = mm_ones(sel, u32 * du_inter, ((1,), (0,)), True)
    over = jnp.sum(grown * states_ref[0].astype(f32), axis=0, keepdims=True)
    over = mm(jnp.broadcast_to(over, (8, GW)), sel, ((1,), (0,)), highest)[0:1] * jnp.exp(total)
    dld = (
        mm_ones(upper_ones().astype(f32), later, ((1,), (0,)))
        + mm_ones(lower_ones(True).astype(f32), earlier, ((1,), (0,)))
        + over
    )
    rate = heads_ref[1:2, 0:8]
    dstep = (ddt - rate * dld) * jax.nn.sigmoid(stepin_ref[...])
    dstep_ref[...] = dstep
    hsum_ref[0:1] += jnp.sum(dstep, axis=0, keepdims=True)
    hsum_ref[1:2] += jnp.sum(-dld * dt * rate, axis=0, keepdims=True)


def back_conv_kernel(
    spot_ref, dprex_ref, dprep_ref, nextx_ref, nextp_ref, halo_ref, rawx_ref, rawp_ref,
    cwx_ref, cwp_ref, bgate_ref, step_ref, x_ref, wgate_ref, win_ref, wpair_ref,
    backx_ref, backp_ref, gradx_ref, gradp_ref, away_ref, mine_ref, gain_ref,
    extx, extp,
):
    b = pl.program_id(0)
    last = b == pl.num_programs(0) - 1

    @pl.when(b == 0)
    def _():
        gradx_ref[...] = jnp.zeros_like(gradx_ref)
        gradp_ref[...] = jnp.zeros_like(gradp_ref)
        gain_ref[...] = jnp.zeros_like(gain_ref)

    def conv(dpre, following, halo, raw, cw, ext, grad):
        ext[0:Q] = dpre[...]
        ext[Q : Q + 8] = jnp.where(last, halo, following[...])
        value = raw[...].astype(f32)
        total = jnp.zeros(dpre.shape, f32)
        for k in range(KW):
            shifted = ext[KW - 1 - k : KW - 1 - k + Q]
            total = total + cw[k : k + 1, :] * shifted
            grad[k : k + 1] += jnp.sum(value * shifted, axis=0, keepdims=True)
        grad[KW : KW + 1] += jnp.sum(dpre[...], axis=0, keepdims=True)
        return total.astype(bf16)

    GW = dprex_ref.shape[1]
    inner = conv(dprex_ref, nextx_ref, halo_ref[:, 0:GW], rawx_ref, cwx_ref, extx, gradx_ref)
    backx_ref[...] = inner
    pair = conv(dprep_ref, nextp_ref, halo_ref[:, GW:], rawp_ref, cwp_ref, extp, gradp_ref)
    backp_ref[...] = pair
    value = mm(bgate_ref[...], wgate_ref[...], ((1,), (0,)))
    value = value + mm(step_ref[...].astype(bf16), win_ref[GW : GW + 8], ((1,), (0,)))
    value = value + mm(inner, win_ref[0:GW], ((1,), (0,)))
    value = value + mm(pair, wpair_ref[...], ((1,), (0,)))
    gain_ref[0:1] += jnp.sum(value * x_ref[...].astype(f32), axis=0, keepdims=True)
    to_halves(spot_ref, b, value.astype(bf16), away_ref, mine_ref)


def cotangent_kernel(absolute, spot_ref, mine_ref, other_ref, x_ref, *refs):
    pieces = refs[:-5]
    cot_ref, gate_rows_ref, rows_ref, z_ref, bn_ref = refs[-5:]
    count = len(pieces)
    QW = rows_ref.shape[0] // count
    Dl = rows_ref.shape[1] // count

    @pl.when(pl.program_id(0) == 0)
    def _():
        for k, piece in enumerate(pieces):
            for src in range(count):
                cols = slice(src * Dl, (src + 1) * Dl)
                far = lax.rem(spot_ref[2] - src + count, count)
                if absolute:
                    gate_rows_ref[k * QW : (k + 1) * QW, cols] = piece[far, 0:QW]
                    rows_ref[k * QW : (k + 1) * QW, cols] = piece[far, QW : 2 * QW]
                else:
                    at = pl.multiple_of((spot_ref[0] ^ k) * QW, 16)
                    gate_rows_ref[pl.ds(at, QW), cols] = piece[far, 0:QW]
                    rows_ref[pl.ds(at, QW), cols] = piece[far, QW : 2 * QW]

    choose_half(spot_ref, mine_ref, other_ref, cot_ref)
    z_ref[...] = mm(x_ref[...], gate_rows_ref[...], ((1,), (1,))).astype(bf16)
    bn_ref[...] = mm(cot_ref[...], rows_ref[...], ((1,), (1,))).astype(bf16)


def partial_blocks_kernel(count, pairs, spot_ref, *refs):
    lefts, rights = refs[:pairs], refs[pairs : 2 * pairs]
    step_ref, pair_ref = refs[2:4] if pairs == 1 else (None, None)
    held = 4 if pairs == 1 else 2
    outs, turned, total = refs[-count - held : -held], refs[-held], refs[1 - held]
    GW = total.shape[0]
    QW = GW // count

    @pl.when(pl.program_id(0) == 0)
    def _():
        for at in range(pairs):
            turned[at] = lefts[at][...].T
        if pair_ref is not None:
            refs[-2][...] = pair_ref[...].T

    for at in range(pairs):
        right = rights[at][...]
        total[...] = mm(turned[at], right, ((1,), (0,)))
        for k in range(count):
            start = pl.multiple_of((spot_ref[0] ^ k) * QW, 8)
            outs[k][0, at * QW : (at + 1) * QW] = total[pl.ds(start, QW)].astype(bf16)
    if step_ref is not None:
        value = mm(step_ref[...].astype(bf16), rights[0][...], ((0,), (0,)))
        for k in range(count):
            keep = ((spot_ref[0] ^ k) == 0).astype(f32)
            outs[k][0, QW : QW + 8] = (value * keep).astype(bf16)
        refs[-1][...] = mm(refs[-2][...], rights[0][...], ((1,), (0,)))
        PW = refs[-1].shape[0] // count
        for k in range(count):
            start = pl.multiple_of((spot_ref[0] ^ k) * PW, 8)
            outs[k][0, QW + 8 : QW + 8 + PW] = refs[-1][pl.ds(start, PW)].astype(bf16)


def partial_kernel(count, pairs, spot_ref, *refs):
    lefts, rights = refs[:pairs], refs[pairs : 2 * pairs]
    step_ref, pair_ref = refs[2:4] if pairs == 1 else (None, None)
    held = 3 if pairs == 1 else pairs
    outs, sums = refs[len(refs) - count - held : len(refs) - held], refs[len(refs) - held :]
    b = pl.program_id(0)
    lefts = [r[...] for r in lefts]
    rights = [r[...] for r in rights]
    if step_ref is not None:
        lefts.extend([step_ref[...].astype(bf16), pair_ref[...]])
        rights.extend([rights[0], rights[0]])
    for left, right, total in zip(lefts, rights, sums, strict=True):
        value = mm(left, right, ((0,), (0,)))

        @pl.when(b == 0)
        def _(value=value, total=total):
            total[...] = value

        @pl.when(b > 0)
        def _(value=value, total=total):
            total[...] += value

    @pl.when(b == pl.num_programs(0) - 1)
    def _():
        GW, D = sums[0].shape
        QW, Dl = GW // count, D // count
        for k in range(count):
            part = spot_ref[0] ^ k
            start = pl.multiple_of(part * QW, 8)
            for j in range(count):
                cols = slice(j * Dl, (j + 1) * Dl)
                for at in range(pairs):
                    outs[k][j, at * QW : (at + 1) * QW] = sums[at][pl.ds(start, QW), cols].astype(
                        bf16
                    )
                if step_ref is not None:
                    keep = (part == 0).astype(f32)
                    outs[k][j, QW : QW + 8] = (sums[1][:, cols] * keep).astype(bf16)
                    PW = sums[2].shape[0] // count
                    at = pl.multiple_of(part * PW, 8)
                    outs[k][j, QW + 8 : QW + 8 + PW] = sums[2][pl.ds(at, PW), cols].astype(bf16)


def sum_kernel(outs_count, spot_ref, *refs):
    i = pl.program_id(0)
    outs = refs[len(refs) - outs_count :]
    total = sum(r[0].astype(f32) for r in refs[: len(refs) - outs_count]).astype(bf16)
    for k, out in enumerate(outs):

        @pl.when(i == k)
        def _(out=out):
            out[...] = total


def place_rows(count, spot_ref, step, own, other, rows, out_ref):
    q, c, f = spot_ref[0], spot_ref[1], spot_ref[2]
    far = lax.rem(f - lax.rem(step, count) + count, count)
    width = rows.stop - rows.start
    for side in range(2):
        owner = c if side == 0 else 1 - c

        @pl.when((step >= owner * count) & (step < (owner + 1) * count))
        def _(side=side):
            for k in range(count):
                value = own[k][far, rows] if side == 0 else other[k, far, rows]
                out_ref[pl.ds(pl.multiple_of((q ^ k) * width, 8), width)] = value.astype(f32)


def early_grads_kernel(count, spot_ref, *refs):
    own, other, in_ref, out_ref = refs[:count], refs[count], refs[-2], refs[-1]
    QW = own[0].shape[1] // 2
    step = pl.program_id(0)
    place_rows(count, spot_ref, step, own, other, slice(0, QW), out_ref)
    place_rows(count, spot_ref, step, own, other, slice(QW, 2 * QW), in_ref)


def late_grads_kernel(count, QW, heads, spot_ref, *refs):
    own, other, in_ref = refs[:count], refs[count], refs[-1]
    step = pl.program_id(0)
    place_rows(count, spot_ref, step, own, other, slice(0, QW), in_ref)
    q, c, f = spot_ref[0], spot_ref[1], spot_ref[2]
    GW = in_ref.shape[0]
    groups = 2 * count
    for block in range(-(-(2 * N + H) // GW)):

        @pl.when(step == groups + block)
        def _(block=block):
            first = block * GW
            PW = 2 * N // count
            base = QW + 8
            for k in range(count):
                total = sum(
                    own[k][g, base : base + PW].astype(f32)
                    + other[k, g, base : base + PW].astype(f32)
                    for g in range(count)
                )
                start = (q ^ k) * PW - first

                @pl.when((start >= 0) & (start < GW))
                def _(total=total, start=start):
                    in_ref[pl.ds(pl.multiple_of(start, 8), PW)] = total


                @pl.when((q ^ k) == 0)
                def _(k=k):
                    for g in range(groups):
                        at = 2 * N + g * heads - first
                        if at < 0 or at >= GW:
                            continue
                        far = lax.rem(f - g % count + count, count)
                        mine = own[k][far, QW : QW + 8].astype(f32)
                        theirs = other[k, far, QW : QW + 8].astype(f32)
                        value = jnp.where(c == g // count, mine, theirs)
                        in_ref[at : at + heads] = value[0:heads]


def body(
    block_in,
    norm_gain,
    in_weight,
    conv_inner_weight,
    conv_inner_bias,
    conv_pair_weight,
    conv_pair_bias,
    step_bias,
    decay_log,
    skip_gain,
    gate_gain,
    out_weight,
    cotangent,
):
    S = lax.axis_size("seq")
    F = lax.axis_size("fsdp")
    devices = S * F
    R = S // F
    s = lax.axis_index("seq")
    f = lax.axis_index("fsdp")
    q = s // R
    c = s % R
    member = c * F + f
    spot = jnp.stack([q, c, f]).astype(jnp.int32)
    tokens, D = block_in.shape
    TL = tokens * S
    blocks = TL // Q
    half = blocks // 2
    HG = H // S
    GW = HG * P_SIZE
    QW = GW // F
    DI = H * P_SIZE
    Dl = in_weight.shape[0]
    PF = P_SIZE // F
    NP = 2 * N
    PH = N // F
    absolute = QW % 16 != 0 or PH % 16 != 0
    twins = [(i, i ^ 1) for i in range(S)]
    back = [(i + R, i) for i in range(S - R)]
    bits = [1 << i for i in range(F.bit_length() - 1)]
    struct = jax.ShapeDtypeStruct

    def twin(value):
        return lax.ppermute(value, "seq", twins)

    def from_part(value, k):
        return lax.ppermute(value, "seq", [(i, i ^ (k * R)) for i in range(S)])

    def from_line(value, k):
        return lax.ppermute(value, "fsdp", [(i, (i + k) % F) for i in range(F)])

    def take(value, at, axis=0):
        return lax.dynamic_index_in_dim(value, at, axis, keepdims=False)

    def line_chain(value):
        up, down, ups, downs = value, value, [], []
        for k in range(1, F):
            up = lax.ppermute(up, "fsdp", [(i, i + 1) for i in range(k - 1, F - 1)])
            down = lax.ppermute(down, "fsdp", [(i, i - 1) for i in range(1, F - k + 1)])
            ups.append(up)
            downs.append(down)
        line = []
        for j in range(F):
            here = value
            for k in range(1, F):
                if j + k < F:
                    here = jnp.where(f == j + k, ups[k - 1], here)
                if j - k >= 0:
                    here = jnp.where(f == j - k, downs[k - 1], here)
            line.append(here)
        return jnp.concatenate(line, axis=0)

    def line_ordered(rel):
        line = []
        for j in range(F):
            here = rel[0]
            for k in range(1, F):
                here = jnp.where(lax.rem(f - k + F, F) == j, rel[k], here)
            line.append(here)
        return jnp.concatenate(line, axis=0)

    def gather_parts(value, order):
        pieces = {0: value}
        for bit in order:
            pieces.update({k ^ bit: from_part(v, bit) for k, v in list(pieces.items())})
        return [pieces[k] for k in range(F)]

    def in_order(pieces):
        if not absolute:
            return pieces
        out = []
        for j in range(F):
            here = pieces[0]
            for k in range(1, F):
                here = jnp.where(q == (j ^ k), pieces[k], here)
            out.append(here)
        return out

    def rows_of(width, shift=0):
        return pl.BlockSpec((Q, width), lambda i, p: (i + shift, 0))

    def rows_back(width):
        return pl.BlockSpec((Q, width), lambda i, p: (blocks - 1 - i, 0))

    def fixed(*shape):
        return pl.BlockSpec(shape, lambda i, p: (0,) * len(shape))

    def per_block(rows, width, shift=0):
        return pl.BlockSpec((1, rows, width), lambda i, p: (i + shift, 0, 0))

    def per_block_back(rows, width):
        return pl.BlockSpec((1, rows, width), lambda i, p: (blocks - 1 - i, 0, 0))

    def half_of(width, own):
        def index(i, p):
            return (
                jnp.where(p[1] == own, jnp.maximum(i - half, 0), jnp.minimum(i, half - 1)), 0
            )

        return pl.BlockSpec((Q, width), index)

    def half_of_back(width, own):
        def index(i, p):
            at = blocks - 1 - i
            return (
                jnp.where(p[1] == own, jnp.maximum(at - half, 0), jnp.minimum(at, half - 1)), 0
            )

        return pl.BlockSpec((Q, width), index)

    across = pl.BlockSpec((8, Q), lambda i, p: (0, i))
    across_back = pl.BlockSpec((8, Q), lambda i, p: (0, blocks - 1 - i))
    anywhere = pl.BlockSpec(memory_space=pl.ANY)

    def call(kernel, steps, in_specs, out_specs, out_shape, scratch=(), aliases=None):
        return pl.pallas_call(
            kernel,
            grid_spec=pltpu.PrefetchScalarGridSpec(
                num_scalar_prefetch=1,
                grid=(steps,),
                in_specs=in_specs,
                out_specs=out_specs,
                scratch_shapes=list(scratch),
            ),
            out_shape=out_shape,
            input_output_aliases=aliases or {},
            compiler_params=pltpu.CompilerParams(dimension_semantics=("arbitrary",)),
        )

    small = jnp.concatenate(
        [
            conv_inner_weight.reshape(KW, HG * PF),
            conv_inner_bias.reshape(1, HG * PF),
            gate_gain.reshape(1, HG * PF),
        ],
        axis=0,
    )
    small = jnp.pad(small, ((0, 0), (0, 128 - HG * PF)))
    heads_row = jnp.concatenate([step_bias, decay_log, skip_gain])
    heads_row = jnp.pad(heads_row, (0, 128 - 3 * HG))[None]
    small = jnp.concatenate([small, heads_row, jnp.zeros((1, 128), f32)], axis=0)
    small_all = spread(small, everyone, devices)
    small_here = lax.dynamic_slice(small_all, (member * F, 0, 0), (F, 8, 128))
    hidden = block_in.astype(f32)
    inverse_scale = lax.rsqrt(jnp.mean(hidden * hidden, axis=1, keepdims=True) + norm_epsilon)
    normed = (hidden * inverse_scale * norm_gain[None, :]).astype(bf16)
    x_line = line_chain(normed)
    x_other = twin(x_line)
    last_rows = x_line[F * tokens - 16 :]
    edge_own = lax.ppermute(last_rows, "seq", [(i, i + R) for i in range(S - R) if i % R == R - 1])
    edge_twin = lax.ppermute(last_rows, "seq", [(i, i + 1) for i in range(S - R) if i % R == R - 1])

    columns = jnp.transpose(in_weight)
    HA = QW // 2 if QW % 32 == 0 else QW

    def rows_for(place):
        group = c * F + place
        inner = lax.dynamic_slice(columns, (DI + group * GW + q * QW, 0), (QW, Dl))
        pair = lax.dynamic_slice(columns, (2 * DI + q * 2 * PH, 0), (2 * PH, Dl))
        step = lax.dynamic_slice(columns, (2 * DI + NP + group * HG, 0), (HG, Dl))
        step = jnp.pad(step, ((0, 8 - HG), (0, 0)))
        return jnp.concatenate([inner[:HA], pair[:PH], inner[HA:], pair[PH:], step], axis=0)

    def later_rows_for(place):
        group = c * F + place
        gate_part = lax.dynamic_slice(columns, (group * GW + q * QW, 0), (QW, Dl))
        out_part = lax.dynamic_slice(out_weight, (group * GW + q * QW, 0), (QW, Dl))
        return jnp.concatenate([gate_part, out_part], axis=0)

    def line_rows(rows):
        return [rows[0]] + [from_line(rows[k], k) for k in range(1, F)]

    if QW % 32 == 0 and DI % QW == 0 and 2 * PH >= H:

        def group_rows(width, start):
            def index(i, p):
                return (start + (p[1] * F + lax.rem(p[2] + i, F)) * F + p[0], 0)

            return pl.BlockSpec((width, Dl), index)

        picked = call(
            pick_kernel,
            F,
            [
                group_rows(QW, DI // QW),
                group_rows(QW, 0),
                pl.BlockSpec((2 * PH, Dl), lambda i, p: (DI // PH + p[0], 0)),
                pl.BlockSpec((2 * PH, Dl), lambda i, p: ((2 * DI + NP) // (2 * PH), 0)),
                group_rows(QW, 0),
            ],
            [fixed(QW + 2 * PH + 8, Dl)] * F + [fixed(2 * QW, Dl)] * F,
            [struct((QW + 2 * PH + 8, Dl), bf16)] * F + [struct((2 * QW, Dl), bf16)] * F,
        )(spot, columns, columns, columns, columns, out_weight)
        rows_now, rows_later = picked[:F], picked[F:]
    else:
        rows_now = [rows_for(lax.rem(f + k, F)) for k in range(F)]
        rows_later = [later_rows_for(lax.rem(f + k, F)) for k in range(F)]
    first_rows = line_rows(rows_now)
    rows_a = jnp.stack([value[: HA + PH] for value in first_rows])
    rows_b = jnp.stack([value[HA + PH :] for value in first_rows])
    if F == 4:
        beside_a, beside_b = from_part(rows_a, 1), from_part(rows_b, 2)
        pieces_a = [rows_a, beside_a, from_part(rows_a, 2), from_part(beside_a, 2)]
        pieces_b = [rows_b, from_part(rows_b, 1), beside_b, from_part(beside_b, 1)]
    else:
        pieces_a, pieces_b = gather_parts(rows_a, bits), gather_parts(rows_b, bits)
    pieces_a, pieces_b = in_order(pieces_a), in_order(pieces_b)

    later = line_rows(rows_later)
    later = jnp.stack(later)
    cot_rel = [from_line(cotangent, k) for k in range(1, F)]

    pair_params = jnp.concatenate(
        [conv_pair_weight, conv_pair_bias[None], jnp.zeros((7 - KW, NP), f32)], axis=0
    )
    conv_x, conv_p, heads, wide_rows = call(
        functools.partial(params_kernel, F, PF),
        1,
        [fixed(F, 8, 128), fixed(8, NP)],
        [fixed(8, GW), fixed(8, NP), fixed(8, 128), fixed(8, GW)],
        [
            struct((8, GW), f32), struct((8, NP), f32), struct((8, 128), f32),
            struct((8, GW), f32),
        ],
    )(spot, small_here, pair_params)
    weight_pieces = [piece for pair in zip(pieces_a, pieces_b, strict=True) for piece in pair]
    (
        x_group, in_rows, pair_in, rawx, rawp, actx, actp, slopex, slopep, dt, cum, cumt,
        step_in, local, total, final,
    ) = call(
        functools.partial(project_kernel, absolute, QW),
        blocks,
        [half_of(D, 1), half_of(D, 0), fixed(16, D), fixed(16, D)]
        + [fixed(F, HA + PH, Dl), fixed(F, QW - HA + PH + 8, Dl)] * F
        + [fixed(8, GW), fixed(8, NP), fixed(8, 128)],
        [
            rows_of(D), fixed(GW + 8, D), fixed(NP, D),
            rows_of(GW), rows_of(NP), rows_of(GW), rows_of(NP), rows_of(GW),
            rows_of(NP), rows_of(8), rows_of(8), across, rows_of(8), per_block(N, GW),
            per_block(8, GW), fixed(N + 8, GW),
        ],
        [
            struct((TL, D), bf16), struct((GW + 8, D), bf16), struct((NP, D), bf16),
            struct((TL, GW), bf16), struct((TL, NP), bf16),
            struct((TL, GW), bf16), struct((TL, NP), bf16), struct((TL, GW), bf16),
            struct((TL, NP), bf16), struct((TL, 8), f32), struct((TL, 8), f32),
            struct((8, TL), f32), struct((TL, 8), f32), struct((blocks, N, GW), f32),
            struct((blocks, 8, GW), f32), struct((N + 8, GW), f32),
        ],
        [
            pltpu.VMEM((N, GW), f32), pltpu.VMEM((8, GW), f32),
            pltpu.VMEM((Q + 8, GW), f32), pltpu.VMEM((Q + 8, NP), f32),
        ],
    )(spot, x_line, x_other, edge_own, edge_twin, *weight_pieces, conv_x, conv_p, heads)

    finals = [from_part(final, k) for k in range(1, F)]
    later_pieces = in_order([later] + [from_part(later, k) for k in range(1, F)])
    *cot_rel, final_low = lax.optimization_barrier((*cot_rel, final[:8]))
    cot_line = line_ordered([cotangent] + cot_rel)
    cot_other = twin(cot_line)
    y_intra = call(
        intra_kernel,
        blocks,
        [rows_of(GW), rows_of(NP), rows_of(8), rows_of(8), across],
        rows_of(GW),
        struct((TL, GW), f32),
    )(spot, actx, actp, dt, cum, cumt)
    cot_group, gate_rows, out_rows, gate, back_normed = call(
        functools.partial(cotangent_kernel, absolute),
        blocks,
        [half_of(D, 1), half_of(D, 0), rows_of(D)] + [fixed(F, 2 * QW, Dl)] * F,
        [rows_of(D), fixed(GW, D), fixed(GW, D), rows_of(GW), rows_of(GW)],
        [
            struct((TL, D), bf16), struct((GW, D), bf16), struct((GW, D), bf16),
            struct((TL, GW), bf16), struct((TL, GW), bf16),
        ],
    )(spot, cot_line, cot_other, x_group, *later_pieces)
    y_inter, states, sums = call(
        inter_kernel,
        blocks,
        [
            rows_of(GW), rows_of(NP), rows_of(8), per_block(8, GW), per_block(N, GW),
            rows_of(GW), rows_of(GW), rows_of(GW), fixed(8, GW),
        ]
        + [fixed(N + 8, GW)] * (F - 1),
        [rows_of(GW), per_block(N, GW), across],
        [struct((TL, GW), f32), struct((blocks, N, GW), bf16), struct((8, TL), f32)],
        [pltpu.VMEM((8, GW), f32), pltpu.VMEM((N, GW), f32)],
    )(spot, actx, actp, cum, total, local, y_intra, gate, back_normed, wide_rows, *finals)

    sums = sums + twin(sums)
    sums = [sums] + [from_line(sums, k) for k in range(1, F)]
    gated_normed, back_gate, dy, local_back, first_back, small_sums, away, mine = call(
        gate_kernel,
        blocks,
        [
            rows_back(GW), rows_back(NP), rows_back(8), per_block_back(8, GW), rows_back(GW),
            rows_back(GW), rows_back(GW), rows_back(GW), fixed(8, GW),
        ]
        + [across_back] * F
        + [fixed(GW, D)],
        [
            rows_back(GW), rows_back(GW), rows_back(GW), per_block_back(N, GW), fixed(N, GW),
            fixed(8, GW), half_of_back(D, 0), half_of_back(D, 1),
        ],
        [
            struct((TL, GW), bf16), struct((TL, GW), bf16), struct((TL, GW), bf16),
            struct((blocks, N, GW), f32), struct((N, GW), f32), struct((8, GW), f32),
            struct((TL // 2, D), bf16), struct((TL // 2, D), bf16),
        ],
        [pltpu.VMEM((N, GW), f32)],
    )(
        spot, actx, actp, cum, total, y_intra, y_inter, gate, back_normed, wide_rows, *sums,
        out_rows,
    )
    firsts = [from_part(first_back, k) for k in range(1, F)]

    def by_line(arrays):
        rows, width = arrays[0].shape[1:]
        block = pl.BlockSpec((1, rows, width), lambda i, p: (lax.rem(p[2] + i, F), 0, 0))
        sums = call(
            functools.partial(sum_kernel, F),
            F,
            [block] * len(arrays),
            [fixed(rows, width)] * F,
            [struct((rows, width), bf16)] * F,
        )(spot, *arrays)
        return [sums[0]] + [from_line(sums[k], k) for k in range(1, F)]

    def add_group(away, mine):
        shape = (F, tokens, mine.shape[1])
        pieces = by_line([mine.reshape(shape), twin(away).reshape(shape)])
        return sum(piece.astype(f32) for piece in pieces)

    def partial_sums(lefts, rights, extra):
        pairs = len(lefts)
        rows = pairs * QW + (8 + 2 * PH if extra else 0)
        if Dl % 128 == 0:
            columns_of = pl.BlockSpec((TL, Dl), lambda i, p: (0, i))
            return call(
                functools.partial(partial_blocks_kernel, F, pairs),
                F,
                [fixed(TL, GW)] * pairs
                + [columns_of] * pairs
                + [fixed(*value.shape) for value in extra],
                [pl.BlockSpec((1, rows, Dl), lambda i, p: (i, 0, 0))] * F,
                [struct((F, rows, Dl), bf16)] * F,
                [pltpu.VMEM((pairs, GW, TL), bf16), pltpu.VMEM((GW, Dl), f32)]
                + [pltpu.VMEM((NP, TL), bf16), pltpu.VMEM((NP, Dl), f32)] * bool(extra),
            )(spot, *lefts, *rights, *extra)
        return call(
            functools.partial(partial_kernel, F, pairs),
            blocks,
            [rows_of(GW)] * pairs
            + [rows_of(D)] * pairs
            + [rows_of(value.shape[1]) for value in extra],
            [fixed(F, rows, Dl)] * F,
            [struct((F, rows, Dl), bf16)] * F,
            [pltpu.VMEM((GW, D), f32)] * pairs
            + [pltpu.VMEM((value.shape[1], D), f32) for value in extra],
        )(spot, *lefts, *rights, *extra)

    def share(pieces):
        piece = jnp.stack(pieces)
        mine = [piece] + [from_part(piece, k) for k in range(1, F)]
        return mine + [twin(jnp.stack(mine))]

    block_out = (hidden + add_group(away, mine)).astype(bf16)

    early = partial_sums([gated_normed, back_gate], [cot_group, x_group], ())
    early = [early[0]] + [from_part(early[k], k) for k in range(1, F)]
    early = share(by_line(early))

    du_intra, dbc = call(
        back_intra_kernel,
        blocks,
        [
            rows_of(GW), rows_of(NP), rows_of(8), rows_of(8), across, rows_of(GW),
            per_block(N, GW),
        ],
        [rows_of(GW), rows_of(NP)],
        [struct((TL, GW), f32), struct((TL, NP), f32)],
    )(spot, actx, actp, dt, cum, cumt, dy, states)

    dprex, dprep, back_step, head_sums, edge_back = call(
        back_inter_kernel,
        blocks,
        [
            rows_of(GW), rows_of(NP), rows_of(GW), rows_of(NP), rows_of(8), rows_of(8),
            rows_of(8), per_block(8, GW), fixed(8, GW), per_block(N, GW), per_block(N, GW),
            rows_of(GW), rows_of(GW), rows_of(GW), rows_of(GW), rows_of(NP), fixed(8, 128),
            fixed(8, GW),
        ]
        + [fixed(N + 8, GW)] * (F - 1)
        + [fixed(N, GW)] * (F - 1),
        [rows_of(GW), rows_of(NP), rows_of(8), fixed(8, 8), fixed(8, GW + NP)],
        [
            struct((TL, GW), f32), struct((TL, NP), f32), struct((TL, 8), f32),
            struct((8, 8), f32), struct((8, GW + NP), f32),
        ],
        [pltpu.VMEM((8, GW), f32), pltpu.VMEM((N, GW), f32)],
    )(
        spot, actx, actp, slopex, slopep, dt, cum, step_in, total, final[N:], local_back,
        states, dy, y_intra, y_inter, du_intra, dbc, heads, wide_rows, *finals, *firsts,
    )
    halo_back = lax.ppermute(edge_back, "seq", back)

    def following(width):
        return pl.BlockSpec(
            (8, width), lambda i, p: (jnp.minimum((i + 1) * (Q // 8), TL // 8 - 1), 0)
        )

    (
        back_inner, back_pair, conv_x_part, conv_p_part, away, mine, gain_rows,
    ) = call(
        back_conv_kernel,
        blocks,
        [
            rows_of(GW), rows_of(NP), following(GW), following(NP), fixed(8, GW + NP),
            rows_of(GW), rows_of(NP), fixed(8, GW), fixed(8, NP), rows_of(GW), rows_of(8),
            rows_of(D), fixed(GW, D), fixed(GW + 8, D), fixed(NP, D),
        ],
        [
            rows_of(GW), rows_of(NP), fixed(8, GW), fixed(8, NP),
            half_of(D, 0), half_of(D, 1), fixed(8, D),
        ],
        [
            struct((TL, GW), bf16), struct((TL, NP), bf16), struct((8, GW), f32), struct((8, NP), f32), struct((TL // 2, D), bf16),
            struct((TL // 2, D), bf16), struct((8, D), f32),
        ],
        [pltpu.VMEM((Q + 8, GW), f32), pltpu.VMEM((Q + 8, NP), f32)],
    )(
        spot, dprex, dprep, dprex, dprep, halo_back, rawx, rawp, conv_x, conv_p, back_gate,
        back_step, x_group, gate_rows, in_rows, pair_in,
    )

    late = partial_sums([back_inner], [x_group], (back_step, back_pair))
    late = [late[0]] + [from_part(late[k], k) for k in range(1, F)]
    back_in = add_group(away, mine)
    late = share(by_line(late))

    rows = F * 8 + 16 + -(-D // 1024) * 8
    small = call(
        functools.partial(pack_kernel, F, PF),
        1,
        [fixed(8, GW), fixed(8, GW), fixed(8, 8), fixed(8, NP), fixed(8, D), fixed(1, D)],
        fixed(rows, 128),
        struct((rows, 128), f32),
    )(spot, conv_x_part, small_sums, head_sums, conv_p_part, gain_rows, norm_gain[None])
    for bit in bits:
        small = small + from_part(small, bit)
    slots, shared = small[: F * 8].reshape(F, 8, 128), small[F * 8 :]
    shared = shared + twin(shared)
    for bit in bits:
        shared = shared + lax.ppermute(shared, "fsdp", [(i, i ^ bit) for i in range(F)])
    owners = [
        ((qq * R + cc) * F + ff, (cc * F + ff) * F + qq)
        for qq in range(F)
        for cc in range(R)
        for ff in range(F)
    ]
    mine_small = lax.ppermute(take(slots, q), everyone, owners)
    pair_grads = jnp.concatenate([shared[:8], shared[8:16]], axis=1)[: KW + 1]
    gain_sum = shared[16:].reshape(-1)[:D]
    channel_grads = mine_small[: KW + 2, : HG * PF].reshape(KW + 2, HG, PF)
    head_grads = mine_small[KW + 2]

    *late_rest, channel_grads, head_grads, pair_grads, gain_sum = lax.optimization_barrier(
        (*early, channel_grads, head_grads, pair_grads, gain_sum)
    )
    early = late_rest

    scaled_back = back_in * norm_gain[None, :]
    inverse_cubed = inverse_scale * inverse_scale * inverse_scale
    grad_input = (
        cotangent.astype(f32)
        + inverse_scale * scaled_back
        - hidden * inverse_cubed * jnp.mean(scaled_back * hidden, axis=1, keepdims=True)
    ).astype(bf16)

    E = in_weight.shape[1]
    grad_in_weight, grad_out_weight = call(
        functools.partial(early_grads_kernel, F),
        S,
        [fixed(F, 2 * QW, Dl)] * F + [fixed(F, F, 2 * QW, Dl)],
        [pl.BlockSpec((GW, Dl), lambda i, p: (i, 0))] * 2,
        [struct((E, Dl), f32), struct((DI, Dl), f32)],
    )(spot, *early)
    grad_in_weight = call(
        functools.partial(late_grads_kernel, F, QW, HG),
        S + -(-(E - 2 * DI) // GW),
        [fixed(F, QW + 8 + 2 * PH, Dl)] * F + [fixed(F, F, QW + 8 + 2 * PH, Dl), anywhere],
        pl.BlockSpec((GW, Dl), lambda i, p: (S + i, 0)),
        struct((E, Dl), f32),
        aliases={F + 2: 0},
    )(spot, *late, grad_in_weight)
    grad_in_weight = jnp.transpose(grad_in_weight)
    return (
        block_out,
        grad_input,
        gain_sum,
        grad_in_weight,
        channel_grads[:KW],
        channel_grads[KW],
        pair_grads[:KW],
        pair_grads[KW],
        head_grads[:HG],
        head_grads[HG : 2 * HG],
        head_grads[2 * HG : 3 * HG],
        channel_grads[KW + 1],
        grad_out_weight,
    )


def solution(mesh):
    in_specs = (
        P(("seq", "fsdp"), None),
        P(),
        P("fsdp", None),
        P(None, "seq", "fsdp"),
        P("seq", "fsdp"),
        P(),
        P(),
        P("seq"),
        P("seq"),
        P("seq"),
        P("seq", "fsdp"),
        P(None, "fsdp"),
        P(("seq", "fsdp"), None),
    )
    out_specs = (
        P(("seq", "fsdp"), None),
        P(("seq", "fsdp"), None),
        P(),
        P("fsdp", None),
        P(None, "seq", "fsdp"),
        P("seq", "fsdp"),
        P(),
        P(),
        P("seq"),
        P("seq"),
        P("seq"),
        P("seq", "fsdp"),
        P(None, "fsdp"),
    )

    return jax.shard_map(body, mesh=mesh, in_specs=in_specs, out_specs=out_specs, check_vma=False)
```

```python
import functools

import jax
import jax.numpy as jnp
from jax import lax
from jax.experimental import pallas as pl
from jax.experimental.pallas import tpu as pltpu
from jax.sharding import PartitionSpec as P


H = 48
P_SIZE = 64
N = 128
KW = 4
Q = 256

norm_epsilon = 1e-05
far_below = -1e30
highest = lax.Precision.HIGHEST
f32 = jnp.float32
bf16 = jnp.bfloat16
everyone = ("seq", "fsdp")


def spread(value, axis, count):
    copies = jnp.broadcast_to(value[None], (count,) + value.shape)
    return lax.all_to_all(copies, axis, 0, 0, tiled=True)


def mm(left, right, dims, precision=None):
    return lax.dot_general(
        left, right, (dims, ((), ())), preferred_element_type=f32, precision=precision
    )


def split3(value):
    first = value.astype(bf16)
    rest = value - first.astype(f32)
    second = rest.astype(bf16)
    return first, second, (rest - second.astype(f32)).astype(bf16)


def mm_ones(ones, value, dims, flip=False):
    ones = ones.astype(bf16)
    parts = [
        mm(part, ones, dims) if flip else mm(ones, part, dims) for part in reversed(split3(value))
    ]
    return sum(parts[1:], parts[0])


def lanes_of(width):
    return [(at, min(2 * P_SIZE, width - at)) for at in range(0, width, 2 * P_SIZE)]


def widen(per_head, width):
    rows = per_head.shape[0]
    out = []
    for at, wide in lanes_of(width):
        h = at // P_SIZE
        first = jnp.broadcast_to(per_head[:, h : h + 1], (rows, wide))
        if wide > P_SIZE:
            second = jnp.broadcast_to(per_head[:, h + 1 : h + 2], (rows, wide))
            lane = lax.broadcasted_iota(jnp.int32, (rows, wide), 1)
            first = jnp.where(lane < P_SIZE, first, second)
        out.append(first)
    return out[0] if len(out) == 1 else jnp.concatenate(out, axis=1)


def pick_heads(width):
    row = lax.broadcasted_iota(jnp.int32, (width, 8), 0)
    col = lax.broadcasted_iota(jnp.int32, (width, 8), 1)
    return ((row >= col * P_SIZE) & (row < (col + 1) * P_SIZE)).astype(f32)


def lower_ones(strict=False):
    row = lax.broadcasted_iota(jnp.int32, (Q, Q), 0)
    col = lax.broadcasted_iota(jnp.int32, (Q, Q), 1)
    return (row > col) if strict else (row >= col)


def upper_ones():
    row = lax.broadcasted_iota(jnp.int32, (Q, Q), 0)
    col = lax.broadcasted_iota(jnp.int32, (Q, Q), 1)
    return row <= col


def split_heads(value):
    if value.shape[1] == P_SIZE:
        return [value]
    lane = lax.broadcasted_iota(jnp.int32, value.shape, 1)
    zero = jnp.zeros_like(value)
    return [jnp.where(lane < P_SIZE, value, zero), jnp.where(lane < P_SIZE, zero, value)]


def soft_plus(value):
    small = jnp.exp(-jnp.abs(value))
    series = small * (1.0 - small * (0.5 - small * (1.0 / 3.0 - 0.25 * small)))
    return jnp.maximum(value, 0.0) + jnp.where(small < 0.01, series, jnp.log(1.0 + small))


def choose_half(spot_ref, mine_ref, other_ref, out_ref):
    half = pl.program_id(0) // (pl.num_programs(0) // 2)
    mine = half == spot_ref[1]

    @pl.when(mine)
    def _():
        out_ref[...] = mine_ref[...]

    @pl.when(jnp.logical_not(mine))
    def _():
        out_ref[...] = other_ref[...]


def to_halves(spot_ref, block, value, away_ref, mine_ref):
    mine = (block // (pl.num_programs(0) // 2)) == spot_ref[1]

    @pl.when(mine)
    def _():
        mine_ref[...] = value

    @pl.when(jnp.logical_not(mine))
    def _():
        away_ref[...] = value


def params_kernel(
    places, width, spot_ref, small_ref, pair_ref, convx_ref, convp_ref, heads_ref, rows_ref
):
    GW = convx_ref.shape[1]
    heads = GW // P_SIZE
    lane = lax.broadcasted_iota(jnp.int32, (128, GW), 0)
    chan = lax.broadcasted_iota(jnp.int32, (128, GW), 1)
    inside = chan % P_SIZE
    total = jnp.zeros((8, GW), f32)
    for place in range(places):
        hot = (inside // width == place) & (
            lane == (chan // P_SIZE) * width + inside % width
        )
        total = total + mm_ones(hot.astype(f32), small_ref[place], ((1,), (0,)), True)
    row = lax.broadcasted_iota(jnp.int32, (8, GW), 0)
    convx_ref[...] = jnp.where(row <= KW, total, 0.0)
    convp_ref[...] = pair_ref[...]
    line = small_ref[0, KW + 2 : KW + 3]
    at = lax.broadcasted_iota(jnp.int32, (128, 128), 0)
    to = lax.broadcasted_iota(jnp.int32, (128, 128), 1)

    def shifted(start):
        hot = (at == to + start) & (to < heads)
        return mm_ones(hot.astype(f32), jnp.broadcast_to(line, (8, 128)), ((1,), (0,)), True)

    used = lax.broadcasted_iota(jnp.int32, (8, 128), 1) < heads
    rate = jnp.where(used, jnp.exp(shifted(heads)), 0.0)
    down = lax.broadcasted_iota(jnp.int32, (8, 128), 0)
    heads_ref[...] = jnp.where(down == 0, shifted(0), jnp.where(down == 1, rate, 0.0))
    skip = widen(shifted(2 * heads)[:, 0:8], GW)
    gain = jnp.broadcast_to(total[KW + 1 : KW + 2], (8, GW))
    share = jnp.full((8, GW), 1.0 / (H * P_SIZE), f32)
    rows_ref[...] = jnp.where(
        row == 0, gain, jnp.where(row == 1, skip, jnp.where(row == 2, share, 0.0))
    )


def pack_kernel(
    places, width, spot_ref, convx_ref, sums_ref, heads_ref, convp_ref, gain_ref, norm_ref, out_ref
):
    GW = convx_ref.shape[1]
    heads = GW // P_SIZE
    row = lax.broadcasted_iota(jnp.int32, (8, GW), 0)
    gate = jnp.broadcast_to(sums_ref[0:1], (8, GW))
    value = jnp.where(row <= KW, convx_ref[...], jnp.where(row == KW + 1, gate, 0.0))
    lane = lax.broadcasted_iota(jnp.int32, (GW, 128), 1)
    chan = lax.broadcasted_iota(jnp.int32, (GW, 128), 0)
    inside = chan % P_SIZE
    at = lax.broadcasted_iota(jnp.int32, (8, 128), 0)
    to = lax.broadcasted_iota(jnp.int32, (8, 128), 1)
    line = mm_ones(((to == at) & (at < heads)).astype(f32), heads_ref[...], ((1,), (0,)), True)
    both = line[0:1]
    line = mm_ones(
        ((to == at + heads) & (at < heads)).astype(f32), heads_ref[...], ((1,), (0,)), True
    )
    both = both + line[1:2]
    skip = (lane == 2 * heads + chan // P_SIZE).astype(f32)
    both = both + mm_ones(skip, sums_ref[...], ((1,), (0,)), True)[1:2]
    down = lax.broadcasted_iota(jnp.int32, (8, 128), 0)
    both = jnp.where(down == KW + 2, jnp.broadcast_to(both, (8, 128)), 0.0)
    for place in range(places):
        hot = (inside // width == place) & (
            lane == (chan // P_SIZE) * width + inside % width
        )
        out_ref[place * 8 : place * 8 + 8] = (
            mm_ones(hot.astype(f32), value, ((1,), (0,)), True) + both
        )
    at = places * 8
    out_ref[at : at + 8] = convp_ref[:, 0:128]
    out_ref[at + 8 : at + 16] = convp_ref[:, 128:256]
    out_ref[at + 16 :] = jnp.zeros((out_ref.shape[0] - at - 16, 128), f32)
    gain = gain_ref[0:1] / norm_ref[...]
    for j in range(gain_ref.shape[1] // 128):
        out_ref[at + 16 + j : at + 17 + j] = gain[:, j * 128 : (j + 1) * 128]


def pick_kernel(
    spot_ref, inner_ref, gate_ref, pair_ref, step_ref, out_ref, *refs
):
    count = len(refs) // 2
    i = pl.program_id(0)
    QW, PW = inner_ref.shape[0], pair_ref.shape[0]
    HA, PH = QW // 2, PW // 2
    heads = QW * count // P_SIZE
    group = spot_ref[1] * count + lax.rem(spot_ref[2] + i, count)
    step = step_ref[...]
    down = lax.broadcasted_iota(jnp.int32, step.shape, 0)
    step = jnp.where(down < H, step, jnp.zeros_like(step))
    row = lax.broadcasted_iota(jnp.int32, (8, step.shape[0]), 0)
    col = lax.broadcasted_iota(jnp.int32, (8, step.shape[0]), 1)
    hot = ((col == row + group * heads) & (row < heads)).astype(f32).astype(bf16)
    step = mm(hot, step, ((1,), (0,))).astype(bf16)
    for k in range(count):
        first, later = refs[k], refs[count + k]

        @pl.when(i == k)
        def _(first=first, later=later):
            first[0:HA] = inner_ref[0:HA]
            first[HA : HA + PH] = pair_ref[0:PH]
            first[HA + PH : QW + PH] = inner_ref[HA:QW]
            first[QW + PH : QW + PW] = pair_ref[PH:PW]
            first[QW + PW : QW + PW + 8] = step
            later[0:QW] = gate_ref[...]
            later[QW : 2 * QW] = out_ref[...]


def project_kernel(
    absolute, QW, spot_ref, mine_ref, other_ref, halo0_ref, halo1_ref, *refs
):
    count = (len(refs) - 23) // 2
    pieces = refs[: 2 * count]
    (
        cwx_ref, cwp_ref, heads_ref,
        x_ref, win_ref, wpair_ref, rawx_ref, rawp_ref, actx_ref, actp_ref, slopex_ref,
        slopep_ref, dt_ref, cum_ref, cumt_ref, stepin_ref, local_ref, total_ref, final_ref,
        state, whole, extx, extp,
    ) = refs[2 * count :]
    b = pl.program_id(0)
    GW = rawx_ref.shape[1]
    PH = N // count
    Dl = win_ref.shape[1] // count
    HA = pieces[0].shape[1] - PH

    @pl.when(b == 0)
    def _():
        def place(ref, at, rows, value):
            if absolute:
                ref[at : at + rows.stop - rows.start, cols] = value[far, rows]
            else:
                at = pl.multiple_of(at, 16)
                ref[pl.ds(at, rows.stop - rows.start), cols] = value[far, rows]

        for k in range(count):
            first, second = pieces[2 * k], pieces[2 * k + 1]
            here = k if absolute else spot_ref[0] ^ k
            for src in range(count):
                cols = slice(src * Dl, (src + 1) * Dl)
                far = lax.rem(spot_ref[2] - src + count, count)
                place(win_ref, here * QW, slice(0, HA), first)
                place(wpair_ref, here * 2 * PH, slice(HA, HA + PH), first)
                if HA < QW:
                    place(win_ref, here * QW + HA, slice(0, QW - HA), second)
                place(
                    wpair_ref, here * 2 * PH + PH, slice(QW - HA, QW - HA + PH), second
                )
                if k == 0:
                    win_ref[GW : GW + 8, cols] = second[far, QW - HA + PH : QW - HA + PH + 8]
        state[...] = jnp.zeros_like(state)
        whole[...] = jnp.zeros_like(whole)
        edge = halo0_ref[...] + halo1_ref[...]
        ex = mm(edge, win_ref[0:GW], ((1,), (1,))).astype(bf16).astype(f32)
        ep = mm(edge, wpair_ref[...], ((1,), (1,))).astype(bf16).astype(f32)
        extx[0:8] = ex[8:16]
        extp[0:8] = ep[8:16]

    @pl.when(b > 0)
    def _():
        extx[0:8] = extx[Q : Q + 8]
        extp[0:8] = extp[Q : Q + 8]

    choose_half(spot_ref, mine_ref, other_ref, x_ref)
    x = x_ref[...]
    rx = mm(x, win_ref[0:GW], ((1,), (1,))).astype(bf16)
    rp = mm(x, wpair_ref[...], ((1,), (1,))).astype(bf16)
    st = mm(x, win_ref[GW : GW + 8], ((1,), (1,))).astype(bf16).astype(f32)
    rawx_ref[...] = rx
    rawp_ref[...] = rp
    extx[8 : Q + 8] = rx.astype(f32)
    extp[8 : Q + 8] = rp.astype(f32)

    def conv(ext, cw, act_out, slope_out):
        pre = cw[KW : KW + 1, :]
        for k in range(KW):
            pre = pre + cw[k : k + 1, :] * ext[9 - KW + k : 9 - KW + k + Q]
        sig = jax.nn.sigmoid(pre)
        act_out[...] = (pre * sig).astype(bf16)
        slope_out[...] = (sig * (1.0 + pre * (1.0 - sig))).astype(bf16)

    conv(extx, cwx_ref, actx_ref, slopex_ref)
    conv(extp, cwp_ref, actp_ref, slopep_ref)
    step_in = st + heads_ref[0:1, 0:8]
    dt = soft_plus(step_in)
    ld = -dt * heads_ref[1:2, 0:8]
    cum = mm_ones(lower_ones().astype(f32), ld, ((1,), (0,)))
    dt_ref[...] = dt
    cum_ref[...] = cum
    stepin_ref[...] = step_in
    eye = (
        lax.broadcasted_iota(jnp.int32, (8, 8), 0) == lax.broadcasted_iota(jnp.int32, (8, 8), 1)
    ).astype(f32)
    cumt_ref[...] = mm(eye, cum, ((1,), (1,)), highest)
    total = cum[Q - 1 : Q]
    total_wide = widen(total, GW)
    total_ref[0] = jnp.broadcast_to(total_wide, (8, GW))
    u32 = actx_ref[...].astype(f32) * widen(dt, GW)
    uw = (u32 * widen(jnp.exp(total - cum), GW)).astype(bf16)
    local_ref[0] = state[...]
    state[...] = state[...] * jnp.exp(total_wide) + mm(actp_ref[:, 0:N], uw, ((0,), (0,)))
    whole[...] = whole[...] + total_wide

    @pl.when(b == pl.num_programs(0) - 1)
    def _():
        final_ref[0:N] = state[...]
        final_ref[N : N + 8] = whole[...]


def intra_kernel(spot_ref, actx_ref, actp_ref, dt_ref, cum_ref, cumt_ref, y_ref):
    GW = y_ref.shape[1]
    scores = mm(actp_ref[:, N : 2 * N], actp_ref[:, 0:N], ((1,), (1,)))
    causal = lower_ones()
    for at, wide in lanes_of(GW):
        u = (
            actx_ref[:, at : at + wide].astype(f32)
            * widen(dt_ref[...], GW)[:, at : at + wide]
        ).astype(bf16)
        mixes = []
        for h in range(at // P_SIZE, (at + wide) // P_SIZE):
            gap = cum_ref[:, h : h + 1] - cumt_ref[h : h + 1, :]
            mixes.append((scores * jnp.exp(jnp.where(causal, gap, far_below))).astype(bf16))
        y_ref[:, at : at + wide] = sum(
            mm(m, p, ((1,), (0,))) for m, p in zip(mixes, split_heads(u), strict=True)
        )


def merge_states(spot_ref, states, totals, forward):
    q = spot_ref[0]
    out = jnp.zeros(states[0].shape, f32)
    count = len(states) + 1
    for k in range(1, count):
        p = q ^ k
        between = jnp.zeros(totals[0].shape, f32)
        for j in range(1, count):
            if j != k:
                o = q ^ j
                inside = ((o > p) & (o < q)) if forward else ((o < p) & (o > q))
                between = between + totals[j - 1] * inside.astype(f32)
        reaches = (p < q) if forward else (p > q)
        out = out + states[k - 1] * (jnp.exp(between) * reaches.astype(f32))
    return out


def inter_kernel(
    spot_ref, actx_ref, actp_ref, cum_ref, total_ref, local_ref, y_ref, z_ref, bn_ref, rows_ref,
    *refs,
):
    finals = refs[:-5]
    yx_ref, states_ref, sums_ref, prefix, before_ref = refs[-5:]
    GW = y_ref.shape[1]

    @pl.when(pl.program_id(0) == 0)
    def _():
        prefix[...] = jnp.zeros_like(prefix)
        before_ref[...] = merge_states(
            spot_ref, [r[0:N] for r in finals], [r[N : N + 1] for r in finals], True
        )

    low = (local_ref[0] + jnp.exp(prefix[0:1]) * before_ref[...]).astype(bf16)
    prefix[...] = prefix[...] + total_ref[0]
    states_ref[0] = low
    yx = mm(actp_ref[:, N : 2 * N], low, ((1,), (0,))) * widen(jnp.exp(cum_ref[...]), GW)
    yx_ref[...] = yx.astype(bf16)
    mixer = y_ref[...] + yx + rows_ref[1:2] * actx_ref[...].astype(f32)
    z = z_ref[...].astype(f32)
    gated = mixer * (z * jax.nn.sigmoid(z))
    row = lax.broadcasted_iota(jnp.int32, (8, GW), 0)
    squares = mm_ones((row == 0).astype(f32), gated * gated, ((1,), (1,)))
    cross = mm_ones(
        (row == 1).astype(f32), bn_ref[...].astype(f32) * rows_ref[0:1] * gated, ((1,), (1,))
    )
    sums_ref[...] = squares + cross


def gate_kernel(
    spot_ref, actx_ref, actp_ref, cum_ref, total_ref, y_ref, yx_ref, z_ref, bn_ref, rows_ref, *refs
):
    sums = sum(r[...] for r in refs[:-10])
    out_rows_ref, gn_ref, bgate_ref, dy_ref, local_ref, first_ref, small_ref = refs[-10:-3]
    away_ref, mine_ref, state = refs[-3:]
    GW = y_ref.shape[1]
    b = pl.program_id(0)

    @pl.when(b == 0)
    def _():
        state[...] = jnp.zeros_like(state)
        small_ref[...] = jnp.zeros_like(small_ref)

    eye = (
        lax.broadcasted_iota(jnp.int32, (8, 8), 0) == lax.broadcasted_iota(jnp.int32, (8, 8), 1)
    ).astype(f32)
    cols = mm(sums, eye, ((0,), (0,)), highest)
    scale = lax.rsqrt(cols[:, 0:1] * rows_ref[2:3, 0:1] + norm_epsilon)
    cross = cols[:, 1:2] * scale * scale * scale * rows_ref[2:3, 0:1]
    x = actx_ref[...].astype(f32)
    mixer = y_ref[...] + yx_ref[...].astype(f32) + rows_ref[1:2] * x
    z = z_ref[...].astype(f32)
    sig = jax.nn.sigmoid(z)
    silu = z * sig
    gated = mixer * silu
    bn = bn_ref[...].astype(f32)
    gain = rows_ref[0:1]
    gn = (gated * scale * gain).astype(bf16)
    gn_ref[...] = gn
    to_halves(
        spot_ref,
        pl.num_programs(0) - 1 - b,
        mm(gn, out_rows_ref[...], ((1,), (0,))).astype(bf16),
        away_ref,
        mine_ref,
    )
    back_gated = scale * (bn * gain) - gated * cross
    dy = (back_gated * silu).astype(bf16)
    dy_ref[...] = dy
    bgate_ref[...] = (back_gated * mixer * sig * (1.0 + z * (1.0 - sig))).astype(bf16)
    dyf = dy.astype(f32)
    small_ref[0:1] += jnp.sum(bn * gated * scale, axis=0, keepdims=True)
    small_ref[1:2] += jnp.sum(dyf * x, axis=0, keepdims=True)
    dyh = (dyf * widen(jnp.exp(cum_ref[...]), GW)).astype(bf16)
    local_ref[0] = state[...]
    state[...] = state[...] * jnp.exp(total_ref[0, 0:1]) + mm(
        actp_ref[:, N : 2 * N], dyh, ((0,), (0,))
    )

    @pl.when(b == pl.num_programs(0) - 1)
    def _():
        first_ref[...] = state[...]


def back_intra_kernel(
    spot_ref, actx_ref, actp_ref, dt_ref, cum_ref, cumt_ref, dy_ref, states_ref,
    du_ref, dbc_ref,
):
    GW = dy_ref.shape[1]
    bs = actp_ref[:, 0:N]
    cs = actp_ref[:, N : 2 * N]
    scores = mm(cs, bs, ((1,), (1,)))
    causal = lower_ones()
    dscores = jnp.zeros((Q, Q), f32)
    dt_wide = widen(dt_ref[...], GW)
    for at, wide in lanes_of(GW):
        u = (actx_ref[:, at : at + wide].astype(f32) * dt_wide[:, at : at + wide]).astype(bf16)
        du = jnp.zeros((Q, wide), f32)
        for k, dyk in enumerate(split_heads(dy_ref[:, at : at + wide])):
            h = at // P_SIZE + k
            gap = cum_ref[:, h : h + 1] - cumt_ref[h : h + 1, :]
            decay = jnp.exp(jnp.where(causal, gap, far_below))
            mix = (scores * decay).astype(bf16)
            dscores = dscores + mm(dyk, u, ((1,), (1,))) * decay
            du = du + mm(mix, dyk, ((0,), (0,)))
        du_ref[:, at : at + wide] = du
    dlow = dscores.astype(bf16)
    dyh = (dy_ref[...].astype(f32) * widen(jnp.exp(cum_ref[...]), GW)).astype(bf16)
    dbc_ref[:, 0:N] = mm(dlow, cs, ((0,), (0,)))
    dbc_ref[:, N : 2 * N] = mm(dlow, bs, ((1,), (0,))) + mm(dyh, states_ref[0], ((1,), (1,)))


def back_inter_kernel(
    spot_ref, actx_ref, actp_ref, slopex_ref, slopep_ref, dt_ref, cum_ref, stepin_ref, total_ref, whole_ref,
    local_ref, states_ref, dy_ref, y_ref, yx_ref, du_ref, dbc_ref, heads_ref, rows_ref, *refs,
):
    others, refs = refs[:-7], refs[-7:]
    dprex_ref, dprep_ref, dstep_ref, hsum_ref, edge_ref, seen, after_ref = refs
    finals, firsts = others[: len(others) // 2], others[len(others) // 2 :]
    GW = dy_ref.shape[1]
    b = pl.program_id(0)

    @pl.when(b == 0)
    def _():
        seen[...] = jnp.zeros_like(seen)
        hsum_ref[...] = jnp.zeros_like(hsum_ref)
        after_ref[...] = merge_states(
            spot_ref, [r[...] for r in firsts], [r[N : N + 1] for r in finals], False
        )

    seen[...] = seen[...] + total_ref[0]
    left = jnp.exp(whole_ref[0:1] - seen[0:1])
    grown = local_ref[0] + left * after_ref[...]
    low = grown.astype(bf16)
    cum = cum_ref[...]
    total = cum[Q - 1 : Q]
    dt = dt_ref[...]
    dt_wide = widen(dt, GW)
    tail = widen(jnp.exp(total - cum), GW)
    x = actx_ref[...].astype(f32)
    u32 = x * dt_wide
    ub = u32.astype(bf16).astype(f32)
    uw = (u32 * tail).astype(bf16)
    bs = actp_ref[:, 0:N]
    du_inter = mm(bs, low, ((1,), (0,))) * tail
    dui = du_ref[...]
    du = dui + du_inter
    dy = dy_ref[...].astype(f32)
    dprex_ref[...] = (
        (du * dt_wide + rows_ref[1:2] * dy) * slopex_ref[...].astype(f32)
    ).astype(bf16)
    db = dbc_ref[:, 0:N] + mm(uw, low, ((1,), (1,)))
    dprep_ref[:, 0:N] = (db * slopep_ref[:, 0:N].astype(f32)).astype(bf16)
    dprep_ref[:, N : 2 * N] = (
        dbc_ref[:, N : 2 * N] * slopep_ref[:, N : 2 * N].astype(f32)
    ).astype(bf16)

    @pl.when(b == 0)
    def _():
        edge_ref[:, 0:GW] = dprex_ref[0:16].astype(f32)[0:8]
        edge_ref[:, GW:] = dprep_ref[0:16].astype(f32)[0:8]

    sel = pick_heads(GW)
    ddt = mm_ones(sel, x * du, ((1,), (0,)), True)
    later = mm_ones(sel, dy * (y_ref[...] + yx_ref[...].astype(f32)) - ub * dui, ((1,), (0,)), True)
    earlier = mm_ones(sel, u32 * du_inter, ((1,), (0,)), True)
    over = jnp.sum(grown * states_ref[0].astype(f32), axis=0, keepdims=True)
    over = mm(jnp.broadcast_to(over, (8, GW)), sel, ((1,), (0,)), highest)[0:1] * jnp.exp(total)
    dld = (
        mm_ones(upper_ones().astype(f32), later, ((1,), (0,)))
        + mm_ones(lower_ones(True).astype(f32), earlier, ((1,), (0,)))
        + over
    )
    rate = heads_ref[1:2, 0:8]
    dstep = (ddt - rate * dld) * jax.nn.sigmoid(stepin_ref[...])
    dstep_ref[...] = dstep
    hsum_ref[0:1] += jnp.sum(dstep, axis=0, keepdims=True)
    hsum_ref[1:2] += jnp.sum(-dld * dt * rate, axis=0, keepdims=True)


def back_conv_kernel(
    spot_ref, dprex_ref, dprep_ref, nextx_ref, nextp_ref, halo_ref, rawx_ref, rawp_ref,
    cwx_ref, cwp_ref, bgate_ref, step_ref, x_ref, wgate_ref, win_ref, wpair_ref,
    backx_ref, backp_ref, gradx_ref, gradp_ref, away_ref, mine_ref, gain_ref,
    extx, extp,
):
    b = pl.program_id(0)
    last = b == pl.num_programs(0) - 1

    @pl.when(b == 0)
    def _():
        gradx_ref[...] = jnp.zeros_like(gradx_ref)
        gradp_ref[...] = jnp.zeros_like(gradp_ref)
        gain_ref[...] = jnp.zeros_like(gain_ref)

    def conv(dpre, following, halo, raw, cw, ext, grad):
        here = dpre[...].astype(f32)
        ext[0:Q] = here
        ext[Q : Q + 8] = jnp.where(last, halo, following[...].astype(f32)[0:8])
        value = raw[...].astype(f32)
        total = jnp.zeros(dpre.shape, f32)
        for k in range(KW):
            shifted = ext[KW - 1 - k : KW - 1 - k + Q]
            total = total + cw[k : k + 1, :] * shifted
            grad[k : k + 1] += jnp.sum(value * shifted, axis=0, keepdims=True)
        grad[KW : KW + 1] += jnp.sum(here, axis=0, keepdims=True)
        return total.astype(bf16)

    GW = dprex_ref.shape[1]
    inner = conv(dprex_ref, nextx_ref, halo_ref[:, 0:GW], rawx_ref, cwx_ref, extx, gradx_ref)
    backx_ref[...] = inner
    pair = conv(dprep_ref, nextp_ref, halo_ref[:, GW:], rawp_ref, cwp_ref, extp, gradp_ref)
    backp_ref[...] = pair
    value = mm(bgate_ref[...], wgate_ref[...], ((1,), (0,)))
    value = value + mm(step_ref[...].astype(bf16), win_ref[GW : GW + 8], ((1,), (0,)))
    value = value + mm(inner, win_ref[0:GW], ((1,), (0,)))
    value = value + mm(pair, wpair_ref[...], ((1,), (0,)))
    gain_ref[0:1] += jnp.sum(value * x_ref[...].astype(f32), axis=0, keepdims=True)
    to_halves(spot_ref, b, value.astype(bf16), away_ref, mine_ref)


def cotangent_kernel(absolute, spot_ref, mine_ref, other_ref, x_ref, *refs):
    pieces = refs[:-5]
    cot_ref, gate_rows_ref, rows_ref, z_ref, bn_ref = refs[-5:]
    count = len(pieces)
    QW = rows_ref.shape[0] // count
    Dl = rows_ref.shape[1] // count

    @pl.when(pl.program_id(0) == 0)
    def _():
        for k, piece in enumerate(pieces):
            for src in range(count):
                cols = slice(src * Dl, (src + 1) * Dl)
                far = lax.rem(spot_ref[2] - src + count, count)
                if absolute:
                    gate_rows_ref[k * QW : (k + 1) * QW, cols] = piece[far, 0:QW]
                    rows_ref[k * QW : (k + 1) * QW, cols] = piece[far, QW : 2 * QW]
                else:
                    at = pl.multiple_of((spot_ref[0] ^ k) * QW, 16)
                    gate_rows_ref[pl.ds(at, QW), cols] = piece[far, 0:QW]
                    rows_ref[pl.ds(at, QW), cols] = piece[far, QW : 2 * QW]

    choose_half(spot_ref, mine_ref, other_ref, cot_ref)
    z_ref[...] = mm(x_ref[...], gate_rows_ref[...], ((1,), (1,))).astype(bf16)
    bn_ref[...] = mm(cot_ref[...], rows_ref[...], ((1,), (1,))).astype(bf16)


def partial_blocks_kernel(count, pairs, spot_ref, *refs):
    lefts, rights = refs[:pairs], refs[pairs : 2 * pairs]
    step_ref, pair_ref = refs[2:4] if pairs == 1 else (None, None)
    held = 4 if pairs == 1 else 2
    outs, turned, total = refs[-count - held : -held], refs[-held], refs[1 - held]
    GW = total.shape[0]
    QW = GW // count

    @pl.when(pl.program_id(0) == 0)
    def _():
        for at in range(pairs):
            turned[at] = lefts[at][...].T
        if pair_ref is not None:
            refs[-2][...] = pair_ref[...].T

    for at in range(pairs):
        right = rights[at][...]
        total[...] = mm(turned[at], right, ((1,), (0,)))
        for k in range(count):
            start = pl.multiple_of((spot_ref[0] ^ k) * QW, 8)
            outs[k][0, at * QW : (at + 1) * QW] = total[pl.ds(start, QW)].astype(bf16)
    if step_ref is not None:
        value = mm(step_ref[...].astype(bf16), rights[0][...], ((0,), (0,)))
        for k in range(count):
            keep = ((spot_ref[0] ^ k) == 0).astype(f32)
            outs[k][0, QW : QW + 8] = (value * keep).astype(bf16)
        refs[-1][...] = mm(refs[-2][...], rights[0][...], ((1,), (0,)))
        PW = refs[-1].shape[0] // count
        for k in range(count):
            start = pl.multiple_of((spot_ref[0] ^ k) * PW, 8)
            outs[k][0, QW + 8 : QW + 8 + PW] = refs[-1][pl.ds(start, PW)].astype(bf16)


def partial_kernel(count, pairs, spot_ref, *refs):
    lefts, rights = refs[:pairs], refs[pairs : 2 * pairs]
    step_ref, pair_ref = refs[2:4] if pairs == 1 else (None, None)
    held = 3 if pairs == 1 else pairs
    outs, sums = refs[len(refs) - count - held : len(refs) - held], refs[len(refs) - held :]
    b = pl.program_id(0)
    lefts = [r[...] for r in lefts]
    rights = [r[...] for r in rights]
    if step_ref is not None:
        lefts.extend([step_ref[...].astype(bf16), pair_ref[...]])
        rights.extend([rights[0], rights[0]])
    for left, right, total in zip(lefts, rights, sums, strict=True):
        value = mm(left, right, ((0,), (0,)))

        @pl.when(b == 0)
        def _(value=value, total=total):
            total[...] = value

        @pl.when(b > 0)
        def _(value=value, total=total):
            total[...] += value

    @pl.when(b == pl.num_programs(0) - 1)
    def _():
        GW, D = sums[0].shape
        QW, Dl = GW // count, D // count
        for k in range(count):
            part = spot_ref[0] ^ k
            start = pl.multiple_of(part * QW, 8)
            for j in range(count):
                cols = slice(j * Dl, (j + 1) * Dl)
                for at in range(pairs):
                    outs[k][j, at * QW : (at + 1) * QW] = sums[at][pl.ds(start, QW), cols].astype(
                        bf16
                    )
                if step_ref is not None:
                    keep = (part == 0).astype(f32)
                    outs[k][j, QW : QW + 8] = (sums[1][:, cols] * keep).astype(bf16)
                    PW = sums[2].shape[0] // count
                    at = pl.multiple_of(part * PW, 8)
                    outs[k][j, QW + 8 : QW + 8 + PW] = sums[2][pl.ds(at, PW), cols].astype(bf16)


def sum_kernel(outs_count, spot_ref, *refs):
    i = pl.program_id(0)
    outs = refs[len(refs) - outs_count :]
    total = sum(r[0].astype(f32) for r in refs[: len(refs) - outs_count]).astype(bf16)
    for k, out in enumerate(outs):

        @pl.when(i == k)
        def _(out=out):
            out[...] = total


def place_rows(count, spot_ref, step, own, other, rows, out_ref):
    q, c, f = spot_ref[0], spot_ref[1], spot_ref[2]
    far = lax.rem(f - lax.rem(step, count) + count, count)
    width = rows.stop - rows.start
    for side in range(2):
        owner = c if side == 0 else 1 - c

        @pl.when((step >= owner * count) & (step < (owner + 1) * count))
        def _(side=side):
            for k in range(count):
                value = own[k][far, rows] if side == 0 else other[k, far, rows]
                out_ref[pl.ds(pl.multiple_of((q ^ k) * width, 8), width)] = value.astype(f32)


def early_grads_kernel(count, spot_ref, *refs):
    own, other, in_ref, out_ref = refs[:count], refs[count], refs[-2], refs[-1]
    QW = own[0].shape[1] // 2
    step = pl.program_id(0)
    place_rows(count, spot_ref, step, own, other, slice(0, QW), out_ref)
    place_rows(count, spot_ref, step, own, other, slice(QW, 2 * QW), in_ref)


def late_grads_kernel(count, QW, heads, spot_ref, *refs):
    own, other, in_ref = refs[:count], refs[count], refs[-1]
    step = pl.program_id(0)
    place_rows(count, spot_ref, step, own, other, slice(0, QW), in_ref)
    q, c, f = spot_ref[0], spot_ref[1], spot_ref[2]
    GW = in_ref.shape[0]
    groups = 2 * count
    for block in range(-(-(2 * N + H) // GW)):

        @pl.when(step == groups + block)
        def _(block=block):
            first = block * GW
            PW = 2 * N // count
            base = QW + 8
            for k in range(count):
                total = sum(
                    own[k][g, base : base + PW].astype(f32)
                    + other[k, g, base : base + PW].astype(f32)
                    for g in range(count)
                )
                start = (q ^ k) * PW - first

                @pl.when((start >= 0) & (start < GW))
                def _(total=total, start=start):
                    in_ref[pl.ds(pl.multiple_of(start, 8), PW)] = total


                @pl.when((q ^ k) == 0)
                def _(k=k):
                    for g in range(groups):
                        at = 2 * N + g * heads - first
                        if at < 0 or at >= GW:
                            continue
                        far = lax.rem(f - g % count + count, count)
                        mine = own[k][far, QW : QW + 8].astype(f32)
                        theirs = other[k, far, QW : QW + 8].astype(f32)
                        value = jnp.where(c == g // count, mine, theirs)
                        in_ref[at : at + heads] = value[0:heads]


def body(
    block_in,
    norm_gain,
    in_weight,
    conv_inner_weight,
    conv_inner_bias,
    conv_pair_weight,
    conv_pair_bias,
    step_bias,
    decay_log,
    skip_gain,
    gate_gain,
    out_weight,
    cotangent,
):
    S = lax.axis_size("seq")
    F = lax.axis_size("fsdp")
    devices = S * F
    R = S // F
    s = lax.axis_index("seq")
    f = lax.axis_index("fsdp")
    q = s // R
    c = s % R
    member = c * F + f
    spot = jnp.stack([q, c, f]).astype(jnp.int32)
    tokens, D = block_in.shape
    TL = tokens * S
    blocks = TL // Q
    half = blocks // 2
    HG = H // S
    GW = HG * P_SIZE
    QW = GW // F
    DI = H * P_SIZE
    Dl = in_weight.shape[0]
    PF = P_SIZE // F
    NP = 2 * N
    PH = N // F
    absolute = QW % 16 != 0 or PH % 16 != 0
    twins = [(i, i ^ 1) for i in range(S)]
    back = [(i + R, i) for i in range(S - R)]
    bits = [1 << i for i in range(F.bit_length() - 1)]
    struct = jax.ShapeDtypeStruct

    def twin(value):
        return lax.ppermute(value, "seq", twins)

    def from_part(value, k):
        return lax.ppermute(value, "seq", [(i, i ^ (k * R)) for i in range(S)])

    def from_line(value, k):
        return lax.ppermute(value, "fsdp", [(i, (i + k) % F) for i in range(F)])

    def take(value, at, axis=0):
        return lax.dynamic_index_in_dim(value, at, axis, keepdims=False)

    def line_chain(value):
        up, down, ups, downs = value, value, [], []
        for k in range(1, F):
            up = lax.ppermute(up, "fsdp", [(i, i + 1) for i in range(k - 1, F - 1)])
            down = lax.ppermute(down, "fsdp", [(i, i - 1) for i in range(1, F - k + 1)])
            ups.append(up)
            downs.append(down)
        line = []
        for j in range(F):
            here = value
            for k in range(1, F):
                if j + k < F:
                    here = jnp.where(f == j + k, ups[k - 1], here)
                if j - k >= 0:
                    here = jnp.where(f == j - k, downs[k - 1], here)
            line.append(here)
        return jnp.concatenate(line, axis=0)

    def line_ordered(rel):
        line = []
        for j in range(F):
            here = rel[0]
            for k in range(1, F):
                here = jnp.where(lax.rem(f - k + F, F) == j, rel[k], here)
            line.append(here)
        return jnp.concatenate(line, axis=0)

    def gather_parts(value, order):
        pieces = {0: value}
        for bit in order:
            pieces.update({k ^ bit: from_part(v, bit) for k, v in list(pieces.items())})
        return [pieces[k] for k in range(F)]

    def in_order(pieces):
        if not absolute:
            return pieces
        out = []
        for j in range(F):
            here = pieces[0]
            for k in range(1, F):
                here = jnp.where(q == (j ^ k), pieces[k], here)
            out.append(here)
        return out

    def rows_of(width, shift=0):
        return pl.BlockSpec((Q, width), lambda i, p: (i + shift, 0))

    def rows_back(width):
        return pl.BlockSpec((Q, width), lambda i, p: (blocks - 1 - i, 0))

    def fixed(*shape):
        return pl.BlockSpec(shape, lambda i, p: (0,) * len(shape))

    def per_block(rows, width, shift=0):
        return pl.BlockSpec((1, rows, width), lambda i, p: (i + shift, 0, 0))

    def per_block_back(rows, width):
        return pl.BlockSpec((1, rows, width), lambda i, p: (blocks - 1 - i, 0, 0))

    def half_of(width, own):
        def index(i, p):
            return (
                jnp.where(p[1] == own, jnp.maximum(i - half, 0), jnp.minimum(i, half - 1)), 0
            )

        return pl.BlockSpec((Q, width), index)

    def half_of_back(width, own):
        def index(i, p):
            at = blocks - 1 - i
            return (
                jnp.where(p[1] == own, jnp.maximum(at - half, 0), jnp.minimum(at, half - 1)), 0
            )

        return pl.BlockSpec((Q, width), index)

    across = pl.BlockSpec((8, Q), lambda i, p: (0, i))
    across_back = pl.BlockSpec((8, Q), lambda i, p: (0, blocks - 1 - i))
    anywhere = pl.BlockSpec(memory_space=pl.ANY)

    def call(kernel, steps, in_specs, out_specs, out_shape, scratch=(), aliases=None):
        return pl.pallas_call(
            kernel,
            grid_spec=pltpu.PrefetchScalarGridSpec(
                num_scalar_prefetch=1,
                grid=(steps,),
                in_specs=in_specs,
                out_specs=out_specs,
                scratch_shapes=list(scratch),
            ),
            out_shape=out_shape,
            input_output_aliases=aliases or {},
            compiler_params=pltpu.CompilerParams(dimension_semantics=("arbitrary",)),
        )

    small = jnp.concatenate(
        [
            conv_inner_weight.reshape(KW, HG * PF),
            conv_inner_bias.reshape(1, HG * PF),
            gate_gain.reshape(1, HG * PF),
        ],
        axis=0,
    )
    small = jnp.pad(small, ((0, 0), (0, 128 - HG * PF)))
    heads_row = jnp.concatenate([step_bias, decay_log, skip_gain])
    heads_row = jnp.pad(heads_row, (0, 128 - 3 * HG))[None]
    small = jnp.concatenate([small, heads_row, jnp.zeros((1, 128), f32)], axis=0)
    small_all = spread(small, everyone, devices)
    small_here = lax.dynamic_slice(small_all, (member * F, 0, 0), (F, 8, 128))
    hidden = block_in.astype(f32)
    inverse_scale = lax.rsqrt(jnp.mean(hidden * hidden, axis=1, keepdims=True) + norm_epsilon)
    normed = (hidden * inverse_scale * norm_gain[None, :]).astype(bf16)
    x_line = line_chain(normed)
    x_other = twin(x_line)
    last_rows = x_line[F * tokens - 16 :]
    edge_own = lax.ppermute(last_rows, "seq", [(i, i + R) for i in range(S - R) if i % R == R - 1])
    edge_twin = lax.ppermute(last_rows, "seq", [(i, i + 1) for i in range(S - R) if i % R == R - 1])

    columns = jnp.transpose(in_weight)
    HA = QW // 2 if QW % 32 == 0 else QW

    def rows_for(place):
        group = c * F + place
        inner = lax.dynamic_slice(columns, (DI + group * GW + q * QW, 0), (QW, Dl))
        pair = lax.dynamic_slice(columns, (2 * DI + q * 2 * PH, 0), (2 * PH, Dl))
        step = lax.dynamic_slice(columns, (2 * DI + NP + group * HG, 0), (HG, Dl))
        step = jnp.pad(step, ((0, 8 - HG), (0, 0)))
        return jnp.concatenate([inner[:HA], pair[:PH], inner[HA:], pair[PH:], step], axis=0)

    def later_rows_for(place):
        group = c * F + place
        gate_part = lax.dynamic_slice(columns, (group * GW + q * QW, 0), (QW, Dl))
        out_part = lax.dynamic_slice(out_weight, (group * GW + q * QW, 0), (QW, Dl))
        return jnp.concatenate([gate_part, out_part], axis=0)

    def line_rows(rows):
        return [rows[0]] + [from_line(rows[k], k) for k in range(1, F)]

    if QW % 32 == 0 and DI % QW == 0 and 2 * PH >= H:

        def group_rows(width, start):
            def index(i, p):
                return (start + (p[1] * F + lax.rem(p[2] + i, F)) * F + p[0], 0)

            return pl.BlockSpec((width, Dl), index)

        picked = call(
            pick_kernel,
            F,
            [
                group_rows(QW, DI // QW),
                group_rows(QW, 0),
                pl.BlockSpec((2 * PH, Dl), lambda i, p: (DI // PH + p[0], 0)),
                pl.BlockSpec((2 * PH, Dl), lambda i, p: ((2 * DI + NP) // (2 * PH), 0)),
                group_rows(QW, 0),
            ],
            [fixed(QW + 2 * PH + 8, Dl)] * F + [fixed(2 * QW, Dl)] * F,
            [struct((QW + 2 * PH + 8, Dl), bf16)] * F + [struct((2 * QW, Dl), bf16)] * F,
        )(spot, columns, columns, columns, columns, out_weight)
        rows_now, rows_later = picked[:F], picked[F:]
    else:
        rows_now = [rows_for(lax.rem(f + k, F)) for k in range(F)]
        rows_later = [later_rows_for(lax.rem(f + k, F)) for k in range(F)]
    first_rows = line_rows(rows_now)
    rows_a = jnp.stack([value[: HA + PH] for value in first_rows])
    rows_b = jnp.stack([value[HA + PH :] for value in first_rows])
    if F == 4:
        beside_a, beside_b = from_part(rows_a, 1), from_part(rows_b, 2)
        pieces_a = [rows_a, beside_a, from_part(rows_a, 2), from_part(beside_a, 2)]
        pieces_b = [rows_b, from_part(rows_b, 1), beside_b, from_part(beside_b, 1)]
    else:
        pieces_a, pieces_b = gather_parts(rows_a, bits), gather_parts(rows_b, bits)
    pieces_a, pieces_b = in_order(pieces_a), in_order(pieces_b)

    later = line_rows(rows_later)
    later = jnp.stack(later)
    cot_rel = [from_line(cotangent, k) for k in range(1, F)]

    pair_params = jnp.concatenate(
        [conv_pair_weight, conv_pair_bias[None], jnp.zeros((7 - KW, NP), f32)], axis=0
    )
    conv_x, conv_p, heads, wide_rows = call(
        functools.partial(params_kernel, F, PF),
        1,
        [fixed(F, 8, 128), fixed(8, NP)],
        [fixed(8, GW), fixed(8, NP), fixed(8, 128), fixed(8, GW)],
        [
            struct((8, GW), f32), struct((8, NP), f32), struct((8, 128), f32),
            struct((8, GW), f32),
        ],
    )(spot, small_here, pair_params)
    weight_pieces = [piece for pair in zip(pieces_a, pieces_b, strict=True) for piece in pair]
    (
        x_group, in_rows, pair_in, rawx, rawp, actx, actp, slopex, slopep, dt, cum, cumt,
        step_in, local, total, final,
    ) = call(
        functools.partial(project_kernel, absolute, QW),
        blocks,
        [half_of(D, 1), half_of(D, 0), fixed(16, D), fixed(16, D)]
        + [fixed(F, HA + PH, Dl), fixed(F, QW - HA + PH + 8, Dl)] * F
        + [fixed(8, GW), fixed(8, NP), fixed(8, 128)],
        [
            rows_of(D), fixed(GW + 8, D), fixed(NP, D),
            rows_of(GW), rows_of(NP), rows_of(GW), rows_of(NP), rows_of(GW),
            rows_of(NP), rows_of(8), rows_of(8), across, rows_of(8), per_block(N, GW),
            per_block(8, GW), fixed(N + 8, GW),
        ],
        [
            struct((TL, D), bf16), struct((GW + 8, D), bf16), struct((NP, D), bf16),
            struct((TL, GW), bf16), struct((TL, NP), bf16),
            struct((TL, GW), bf16), struct((TL, NP), bf16), struct((TL, GW), bf16),
            struct((TL, NP), bf16), struct((TL, 8), f32), struct((TL, 8), f32),
            struct((8, TL), f32), struct((TL, 8), f32), struct((blocks, N, GW), f32),
            struct((blocks, 8, GW), f32), struct((N + 8, GW), f32),
        ],
        [
            pltpu.VMEM((N, GW), f32), pltpu.VMEM((8, GW), f32),
            pltpu.VMEM((Q + 8, GW), f32), pltpu.VMEM((Q + 8, NP), f32),
        ],
    )(spot, x_line, x_other, edge_own, edge_twin, *weight_pieces, conv_x, conv_p, heads)

    finals = [from_part(final, k) for k in range(1, F)]
    later_pieces = in_order([later] + [from_part(later, k) for k in range(1, F)])
    *cot_rel, final_low = lax.optimization_barrier((*cot_rel, final[:8]))
    cot_line = line_ordered([cotangent] + cot_rel)
    cot_other = twin(cot_line)
    y_intra = call(
        intra_kernel,
        blocks,
        [rows_of(GW), rows_of(NP), rows_of(8), rows_of(8), across],
        rows_of(GW),
        struct((TL, GW), f32),
    )(spot, actx, actp, dt, cum, cumt)
    cot_group, gate_rows, out_rows, gate, back_normed = call(
        functools.partial(cotangent_kernel, absolute),
        blocks,
        [half_of(D, 1), half_of(D, 0), rows_of(D)] + [fixed(F, 2 * QW, Dl)] * F,
        [rows_of(D), fixed(GW, D), fixed(GW, D), rows_of(GW), rows_of(GW)],
        [
            struct((TL, D), bf16), struct((GW, D), bf16), struct((GW, D), bf16),
            struct((TL, GW), bf16), struct((TL, GW), bf16),
        ],
    )(spot, cot_line, cot_other, x_group, *later_pieces)
    y_inter, states, sums = call(
        inter_kernel,
        blocks,
        [
            rows_of(GW), rows_of(NP), rows_of(8), per_block(8, GW), per_block(N, GW),
            rows_of(GW), rows_of(GW), rows_of(GW), fixed(8, GW),
        ]
        + [fixed(N + 8, GW)] * (F - 1),
        [rows_of(GW), per_block(N, GW), across],
        [struct((TL, GW), bf16), struct((blocks, N, GW), bf16), struct((8, TL), f32)],
        [pltpu.VMEM((8, GW), f32), pltpu.VMEM((N, GW), f32)],
    )(spot, actx, actp, cum, total, local, y_intra, gate, back_normed, wide_rows, *finals)

    sums = sums + twin(sums)
    sums = [sums] + [from_line(sums, k) for k in range(1, F)]
    gated_normed, back_gate, dy, local_back, first_back, small_sums, away, mine = call(
        gate_kernel,
        blocks,
        [
            rows_back(GW), rows_back(NP), rows_back(8), per_block_back(8, GW), rows_back(GW),
            rows_back(GW), rows_back(GW), rows_back(GW), fixed(8, GW),
        ]
        + [across_back] * F
        + [fixed(GW, D)],
        [
            rows_back(GW), rows_back(GW), rows_back(GW), per_block_back(N, GW), fixed(N, GW),
            fixed(8, GW), half_of_back(D, 0), half_of_back(D, 1),
        ],
        [
            struct((TL, GW), bf16), struct((TL, GW), bf16), struct((TL, GW), bf16),
            struct((blocks, N, GW), f32), struct((N, GW), f32), struct((8, GW), f32),
            struct((TL // 2, D), bf16), struct((TL // 2, D), bf16),
        ],
        [pltpu.VMEM((N, GW), f32)],
    )(
        spot, actx, actp, cum, total, y_intra, y_inter, gate, back_normed, wide_rows, *sums,
        out_rows,
    )
    firsts = [from_part(first_back, k) for k in range(1, F)]

    def by_line(arrays):
        rows, width = arrays[0].shape[1:]
        block = pl.BlockSpec((1, rows, width), lambda i, p: (lax.rem(p[2] + i, F), 0, 0))
        sums = call(
            functools.partial(sum_kernel, F),
            F,
            [block] * len(arrays),
            [fixed(rows, width)] * F,
            [struct((rows, width), bf16)] * F,
        )(spot, *arrays)
        return [sums[0]] + [from_line(sums[k], k) for k in range(1, F)]

    def add_group(away, mine):
        shape = (F, tokens, mine.shape[1])
        pieces = by_line([mine.reshape(shape), twin(away).reshape(shape)])
        return sum(piece.astype(f32) for piece in pieces)

    def partial_sums(lefts, rights, extra):
        pairs = len(lefts)
        rows = pairs * QW + (8 + 2 * PH if extra else 0)
        if Dl % 128 == 0:
            columns_of = pl.BlockSpec((TL, Dl), lambda i, p: (0, i))
            return call(
                functools.partial(partial_blocks_kernel, F, pairs),
                F,
                [fixed(TL, GW)] * pairs
                + [columns_of] * pairs
                + [fixed(*value.shape) for value in extra],
                [pl.BlockSpec((1, rows, Dl), lambda i, p: (i, 0, 0))] * F,
                [struct((F, rows, Dl), bf16)] * F,
                [pltpu.VMEM((pairs, GW, TL), bf16), pltpu.VMEM((GW, Dl), f32)]
                + [pltpu.VMEM((NP, TL), bf16), pltpu.VMEM((NP, Dl), f32)] * bool(extra),
            )(spot, *lefts, *rights, *extra)
        return call(
            functools.partial(partial_kernel, F, pairs),
            blocks,
            [rows_of(GW)] * pairs
            + [rows_of(D)] * pairs
            + [rows_of(value.shape[1]) for value in extra],
            [fixed(F, rows, Dl)] * F,
            [struct((F, rows, Dl), bf16)] * F,
            [pltpu.VMEM((GW, D), f32)] * pairs
            + [pltpu.VMEM((value.shape[1], D), f32) for value in extra],
        )(spot, *lefts, *rights, *extra)

    def share(pieces):
        piece = jnp.stack(pieces)
        mine = [piece] + [from_part(piece, k) for k in range(1, F)]
        return mine + [twin(jnp.stack(mine))]

    block_out = (hidden + add_group(away, mine)).astype(bf16)

    early = partial_sums([gated_normed, back_gate], [cot_group, x_group], ())
    early = [early[0]] + [from_part(early[k], k) for k in range(1, F)]
    early = share(by_line(early))

    du_intra, dbc = call(
        back_intra_kernel,
        blocks,
        [
            rows_of(GW), rows_of(NP), rows_of(8), rows_of(8), across, rows_of(GW),
            per_block(N, GW),
        ],
        [rows_of(GW), rows_of(NP)],
        [struct((TL, GW), f32), struct((TL, NP), f32)],
    )(spot, actx, actp, dt, cum, cumt, dy, states)

    dprex, dprep, back_step, head_sums, edge_back = call(
        back_inter_kernel,
        blocks,
        [
            rows_of(GW), rows_of(NP), rows_of(GW), rows_of(NP), rows_of(8), rows_of(8),
            rows_of(8), per_block(8, GW), fixed(8, GW), per_block(N, GW), per_block(N, GW),
            rows_of(GW), rows_of(GW), rows_of(GW), rows_of(GW), rows_of(NP), fixed(8, 128),
            fixed(8, GW),
        ]
        + [fixed(N + 8, GW)] * (F - 1)
        + [fixed(N, GW)] * (F - 1),
        [rows_of(GW), rows_of(NP), rows_of(8), fixed(8, 8), fixed(8, GW + NP)],
        [
            struct((TL, GW), bf16), struct((TL, NP), bf16), struct((TL, 8), f32),
            struct((8, 8), f32), struct((8, GW + NP), f32),
        ],
        [pltpu.VMEM((8, GW), f32), pltpu.VMEM((N, GW), f32)],
    )(
        spot, actx, actp, slopex, slopep, dt, cum, step_in, total, final[N:], local_back,
        states, dy, y_intra, y_inter, du_intra, dbc, heads, wide_rows, *finals, *firsts,
    )
    halo_back = lax.ppermute(edge_back, "seq", back)

    def following(width):
        return pl.BlockSpec(
            (16, width), lambda i, p: (jnp.minimum((i + 1) * (Q // 16), TL // 16 - 1), 0)
        )

    (
        back_inner, back_pair, conv_x_part, conv_p_part, away, mine, gain_rows,
    ) = call(
        back_conv_kernel,
        blocks,
        [
            rows_of(GW), rows_of(NP), following(GW), following(NP), fixed(8, GW + NP),
            rows_of(GW), rows_of(NP), fixed(8, GW), fixed(8, NP), rows_of(GW), rows_of(8),
            rows_of(D), fixed(GW, D), fixed(GW + 8, D), fixed(NP, D),
        ],
        [
            rows_of(GW), rows_of(NP), fixed(8, GW), fixed(8, NP),
            half_of(D, 0), half_of(D, 1), fixed(8, D),
        ],
        [
            struct((TL, GW), bf16), struct((TL, NP), bf16), struct((8, GW), f32), struct((8, NP), f32), struct((TL // 2, D), bf16),
            struct((TL // 2, D), bf16), struct((8, D), f32),
        ],
        [pltpu.VMEM((Q + 8, GW), f32), pltpu.VMEM((Q + 8, NP), f32)],
    )(
        spot, dprex, dprep, dprex, dprep, halo_back, rawx, rawp, conv_x, conv_p, back_gate,
        back_step, x_group, gate_rows, in_rows, pair_in,
    )

    late = partial_sums([back_inner], [x_group], (back_step, back_pair))
    late = [late[0]] + [from_part(late[k], k) for k in range(1, F)]
    back_in = add_group(away, mine)
    late = share(by_line(late))

    rows = F * 8 + 16 + -(-D // 1024) * 8
    small = call(
        functools.partial(pack_kernel, F, PF),
        1,
        [fixed(8, GW), fixed(8, GW), fixed(8, 8), fixed(8, NP), fixed(8, D), fixed(1, D)],
        fixed(rows, 128),
        struct((rows, 128), f32),
    )(spot, conv_x_part, small_sums, head_sums, conv_p_part, gain_rows, norm_gain[None])
    for bit in bits:
        small = small + from_part(small, bit)
    slots, shared = small[: F * 8].reshape(F, 8, 128), small[F * 8 :]
    shared = shared + twin(shared)
    for bit in bits:
        shared = shared + lax.ppermute(shared, "fsdp", [(i, i ^ bit) for i in range(F)])
    owners = [
        ((qq * R + cc) * F + ff, (cc * F + ff) * F + qq)
        for qq in range(F)
        for cc in range(R)
        for ff in range(F)
    ]
    mine_small = lax.ppermute(take(slots, q), everyone, owners)
    pair_grads = jnp.concatenate([shared[:8], shared[8:16]], axis=1)[: KW + 1]
    gain_sum = shared[16:].reshape(-1)[:D]
    channel_grads = mine_small[: KW + 2, : HG * PF].reshape(KW + 2, HG, PF)
    head_grads = mine_small[KW + 2]

    *late_rest, channel_grads, head_grads, pair_grads, gain_sum = lax.optimization_barrier(
        (*early, channel_grads, head_grads, pair_grads, gain_sum)
    )
    early = late_rest

    scaled_back = back_in * norm_gain[None, :]
    inverse_cubed = inverse_scale * inverse_scale * inverse_scale
    grad_input = (
        cotangent.astype(f32)
        + inverse_scale * scaled_back
        - hidden * inverse_cubed * jnp.mean(scaled_back * hidden, axis=1, keepdims=True)
    ).astype(bf16)

    E = in_weight.shape[1]
    grad_in_weight, grad_out_weight = call(
        functools.partial(early_grads_kernel, F),
        S,
        [fixed(F, 2 * QW, Dl)] * F + [fixed(F, F, 2 * QW, Dl)],
        [pl.BlockSpec((GW, Dl), lambda i, p: (i, 0))] * 2,
        [struct((E, Dl), f32), struct((DI, Dl), f32)],
    )(spot, *early)
    grad_in_weight = call(
        functools.partial(late_grads_kernel, F, QW, HG),
        S + -(-(E - 2 * DI) // GW),
        [fixed(F, QW + 8 + 2 * PH, Dl)] * F + [fixed(F, F, QW + 8 + 2 * PH, Dl), anywhere],
        pl.BlockSpec((GW, Dl), lambda i, p: (S + i, 0)),
        struct((E, Dl), f32),
        aliases={F + 2: 0},
    )(spot, *late, grad_in_weight)
    grad_in_weight = jnp.transpose(grad_in_weight)
    return (
        block_out,
        grad_input,
        gain_sum,
        grad_in_weight,
        channel_grads[:KW],
        channel_grads[KW],
        pair_grads[:KW],
        pair_grads[KW],
        head_grads[:HG],
        head_grads[HG : 2 * HG],
        head_grads[2 * HG : 3 * HG],
        channel_grads[KW + 1],
        grad_out_weight,
    )


def solution(mesh):
    in_specs = (
        P(("seq", "fsdp"), None),
        P(),
        P("fsdp", None),
        P(None, "seq", "fsdp"),
        P("seq", "fsdp"),
        P(),
        P(),
        P("seq"),
        P("seq"),
        P("seq"),
        P("seq", "fsdp"),
        P(None, "fsdp"),
        P(("seq", "fsdp"), None),
    )
    out_specs = (
        P(("seq", "fsdp"), None),
        P(("seq", "fsdp"), None),
        P(),
        P("fsdp", None),
        P(None, "seq", "fsdp"),
        P("seq", "fsdp"),
        P(),
        P(),
        P("seq"),
        P("seq"),
        P("seq"),
        P("seq", "fsdp"),
        P(None, "fsdp"),
    )

    return jax.shard_map(body, mesh=mesh, in_specs=in_specs, out_specs=out_specs, check_vma=False)
```
